32 devices in a mesh: row: 4 (over y, x), col: 8 (over z, core).
Axes of the slice: x: 2, y: 2, z: 4, core: 2. Of those that a mesh axis runs over, the one named last changes fastest.
Arguments:
- owned_blocks: bfloat16 [1024, 8, 128, 128], P(('row', 'col')), may hold values from -0.8984375 to 0.8984375
- owned_rows: int32 [1024], P(('row', 'col')), may hold values from 0 to 64, as said below
- owned_cols: int32 [1024, 8], P(('row', 'col')), may hold values from 0 to 31
- keep: int32 [8, 256], P('row', 'col'), may hold values 0 or 1
Outputs:
- purified: bfloat16 [1024, 32768], P('row', 'col')
The draws below stay inside these ranges and needn't reach their ends.
Inputs may be any that keep to these rules, and one draw needn't show every extreme that they name: `owned_rows`: every block row of P stands in exactly one slot, in a slot of its own band; in every band some owner fills all 8 of its slots for that band.
All inputs are finite; a program needn't handle non-finite values. No bound on the sum of `keep` on one device may be relied on, other than what follows from the above.
Results may differ from the reference program's by a relative error of at most 0.005.
Values may be sent and summed in bfloat16 or wider, within the bound.
A program may use at most 256 MiB of HBM per device.

```python
import jax
import jax.numpy as jnp
from jax import lax

BLK = 128
GCOL = 32
RLOC = 2
NB = 256
HB = 64
W = 8
BANDCAP = 8
OWNSLOTS = 32
N_ROW = 4
N_COL = 8
DEVICES = 32


def draw_owned_rows(key, part):
    band_rows = 2 * GCOL
    full_count = band_rows // (2 * BANDCAP)
    remaining = band_rows - full_count * BANDCAP
    others = DEVICES - full_count
    base_share = remaining // others
    extra_share = remaining % others
    position = jnp.arange(DEVICES, dtype=jnp.int32)
    later = position - full_count
    counts = jnp.where(position < full_count, BANDCAP, base_share + (later < extra_share).astype(jnp.int32))
    starts = jnp.cumsum(counts) - counts
    slot_ids = jnp.arange(BANDCAP, dtype=jnp.int32)

    def one_band(band_id):
        band_key = jax.random.fold_in(key, 17 + band_id)
        owner_order = jax.random.permutation(jax.random.fold_in(band_key, 1), DEVICES)
        row_order = jax.random.permutation(jax.random.fold_in(band_key, 2), band_rows).astype(jnp.int32)
        spots = starts[:, None] + slot_ids[None, :]
        values = jnp.where(slot_ids[None, :] < counts[:, None], row_order[jnp.minimum(spots, band_rows - 1)], band_rows)
        return jnp.zeros((DEVICES, BANDCAP), jnp.int32).at[owner_order].set(values.astype(jnp.int32))
    tables = jax.vmap(one_band)(jnp.arange(N_ROW, dtype=jnp.int32))
    return tables.transpose(1, 0, 2).reshape(DEVICES * N_ROW * BANDCAP).astype(jnp.int32)


def with_ends(entries, key, least, top_value):
    place = [jax.random.randint(jax.random.fold_in(key, axis), (), 0, length) for axis, length in enumerate(entries.shape)]
    main_axis = entries.shape.index(max(entries.shape))
    next_to = place[:main_axis] + [(place[main_axis] + 1) % entries.shape[main_axis]] + place[main_axis + 1:]
    return entries.at[tuple(place)].set(least).at[tuple(next_to)].set(top_value)


def block_levels(stream_key, dims, split, least, largest):
    factor_of, own = 1.0, jax.random.fold_in(stream_key, 6)
    for dim, shards_of in split:
        draws = jnp.exp(jax.random.uniform(jax.random.fold_in(own, dim), (shards_of,), jnp.float32, least / len(split), largest / len(split)))
        factor_of = factor_of * jnp.repeat(draws, dims[dim] // shards_of).reshape([-1 if axis == dim else 1 for axis in range(len(dims))])
    return factor_of


def bell_draw(stream_key, dims, deviation, most, cuts=(), kind=jnp.bfloat16):
    array = jax.random.normal(stream_key, dims, jnp.float32) * deviation
    if len(cuts) > 0:
        array = block_levels(stream_key, dims, cuts, -0.22, 0.18) * array
    return jnp.clip(array, min=-most, max=most).astype(kind)


def setup_inputs(seed: int = 0) -> dict:
    seeds = jax.random.split(jax.random.key(seed), 5)
    owned_blocks = bell_draw(seeds[0], (DEVICES * OWNSLOTS, N_COL, BLK, BLK), 0.15, 0.8984375, ((0, 32),))
    owned_rows = draw_owned_rows(jax.random.fold_in(seeds[4], 71), 0)
    owned_cols = with_ends(jax.random.randint(seeds[2], (DEVICES * OWNSLOTS, N_COL), 0, GCOL), jax.random.fold_in(seeds[2], 1), 0, GCOL - 1).astype(jnp.int32)
    keep = with_ends((jax.random.randint(seeds[3], (W, NB), 0, 8) < 7).astype(jnp.int32), jax.random.fold_in(seeds[3], 1), 0, 1)
    return dict(owned_blocks=owned_blocks, owned_rows=owned_rows, owned_cols=owned_cols, keep=keep)


def build_matrix(owned_blocks, owned_rows, owned_cols):
    slot_count = owned_rows.shape[0]
    band_ids = (jnp.arange(slot_count).astype(jnp.int32) // BANDCAP) % N_ROW
    row_ids = GCOL * (band_ids + N_ROW * (owned_rows // GCOL)) + owned_rows % GCOL
    row_ids = jnp.where(owned_rows < HB, row_ids, NB).astype(jnp.int32)
    blocks = jnp.zeros((NB, N_COL, BLK, BLK), jnp.bfloat16).at[row_ids].set(owned_blocks, mode="drop")
    columns = jnp.zeros((NB, N_COL), jnp.int32).at[row_ids].set(owned_cols, mode="drop")
    return blocks, columns


def reference(owned_blocks, owned_rows, owned_cols, keep):
    blocks, columns = build_matrix(owned_blocks, owned_rows, owned_cols)
    group_base = (GCOL * jnp.arange(N_COL)).astype(jnp.int32)
    window_ids = jnp.arange(W).astype(jnp.int32)
    window = (GCOL * (window_ids // RLOC) + window_ids % RLOC).astype(jnp.int32)
    left_blocks = blocks[window].astype(jnp.float32)
    inner_rows = (group_base[None, :] + columns[window]).astype(jnp.int32)
    right_blocks = blocks[inner_rows].astype(jnp.float32)
    targets = (group_base[None, None, :] + columns[inner_rows]).astype(jnp.int32)
    products = jnp.einsum("wgab,wghbc->wghac", left_blocks, right_blocks, precision=lax.Precision.HIGHEST)
    row_index = jnp.broadcast_to(window_ids[:, None, None], targets.shape)
    square = jnp.zeros((W, NB, BLK, BLK), jnp.float32).at[row_index, targets].add(products)
    keep_mask = keep.astype(jnp.float32)[:, :, None, None]
    filtered = (square * keep_mask).astype(jnp.bfloat16)

    def add_row(running, inner_id):
        left_piece = lax.dynamic_index_in_dim(filtered, inner_id, 1, keepdims=False).astype(jnp.float32)
        right_piece = blocks[inner_id].astype(jnp.float32)
        partial_terms = jnp.einsum("wab,gbc->wgac", left_piece, right_piece, precision=lax.Precision.HIGHEST)
        spots = (group_base + columns[inner_id]).astype(jnp.int32)
        return running.at[:, spots].add(partial_terms), None

    cubed, _ = lax.scan(add_row, jnp.zeros((W, NB, BLK, BLK), jnp.float32), jnp.arange(NB).astype(jnp.int32))
    purified = (3.0 * filtered.astype(jnp.float32) - 2.0 * cubed).astype(jnp.bfloat16)
    return purified.transpose(0, 2, 1, 3).reshape(W * BLK, NB * BLK)
```

```python
import functools

import jax
import jax.numpy as jnp
from jax import lax
from jax.experimental import pallas as pl
from jax.experimental.pallas import tpu as pltpu
from jax.sharding import PartitionSpec as P

MESH = pl.DeviceIdType.MESH
ANY = pl.BlockSpec(memory_space=pl.ANY)
SMEM = pl.BlockSpec(memory_space=pltpu.SMEM)
VMEM = pl.BlockSpec(memory_space=pltpu.VMEM)
DMA = pltpu.SemaphoreType.DMA
BIG = 60 * 1024 * 1024


def remote_params(number):
    return pltpu.CompilerParams(collective_id=number, has_side_effects=True)


def spread_kernel(n_row, n_col, meta, owned, meta_all, sibling, send, recv, pair_send, pair_recv):
    r, c = lax.axis_index("row"), lax.axis_index("col")
    me = r * n_col + c
    devices = n_row * n_col
    barrier = pltpu.get_barrier_semaphore()

    def greet(i, carry):
        d = lax.rem(me + i, devices)
        pl.semaphore_signal(barrier, inc=1, device_id=(d // n_col, lax.rem(d, n_col)), device_id_type=MESH)
        return carry

    lax.fori_loop(1, devices, greet, 0)
    pl.semaphore_wait(barrier, devices - 1)
    z, k = c // 2, lax.rem(c, 2)
    other = 1 - k
    pair = pltpu.make_async_remote_copy(
        src_ref=owned.at[:, :, other], dst_ref=sibling, send_sem=pair_send, recv_sem=pair_recv,
        device_id=(r, 2 * z + other), device_id_type=MESH)
    pair.start()

    def copy_to(i):
        d = lax.rem(me + i, devices)
        return pltpu.make_async_remote_copy(
            src_ref=meta, dst_ref=meta_all.at[me], send_sem=send.at[i], recv_sem=recv.at[i],
            device_id=(d // n_col, lax.rem(d, n_col)), device_id_type=MESH)

    def begin(i, carry):
        copy_to(i).start()
        return carry

    def finish(i, carry):
        copy_to(i).wait()
        return carry

    lax.fori_loop(1, devices, begin, 0)
    lax.fori_loop(1, devices, finish, 0)
    pair.wait()


def greet(partners):
    barrier = pltpu.get_barrier_semaphore()
    for partner in partners:
        pl.semaphore_signal(barrier, inc=1, device_id=partner, device_id_type=MESH)
    pl.semaphore_wait(barrier, len(partners))


def send_to(source, dest, sems, step, partner):
    return pltpu.make_async_remote_copy(
        src_ref=source, dst_ref=dest, send_sem=sems[0].at[step], recv_sem=sems[1].at[step],
        device_id=partner, device_id_type=MESH)


def place_of(nz):
    r, c = lax.axis_index("row"), lax.axis_index("col")
    z, k = c // 2, lax.rem(c, 2)
    return r, c, z, k, [(r, 2 * lax.rem(z + step, nz) + k) for step in range(1, nz)]


def first_kernel(nz, count, source, got, send, recv):
    r, c, z, k, others = place_of(nz)
    greet(others)
    copies = [send_to(source.at[to[1] // 2, pl.ds(0, count)], got.at[z], (send, recv), step, to)
              for step, to in enumerate(others)]
    for copy in copies:
        copy.start()
    for copy in copies:
        copy.wait()


def second_kernel(n_row, nz, source, wanted, got, plane_got, send, recv, psend, precv):
    r, c, z, k, others = place_of(nz)
    lines = [(lax.rem(r + step, n_row), c) for step in range(1, n_row)]
    greet(others + lines)
    count = got.shape[1]
    copies = [send_to(wanted.at[to[0]], plane_got.at[r], (psend, precv), step, to) for step, to in enumerate(lines)]
    copies += [send_to(source.at[to[1] // 2, pl.ds(0, count)], got.at[z], (send, recv), step, to)
               for step, to in enumerate(others)]
    for copy in copies:
        copy.start()
    for copy in copies:
        copy.wait()


def left_kernel(nz, piece, got, send, recv, psend, precv):
    r, c, z, k, others = place_of(nz)
    mate = (r, 2 * z + 1 - k)
    greet(others + [mate])
    copies = [send_to(piece, got.at[c], (send, recv), step, to) for step, to in enumerate(others)]
    for copy in copies:
        copy.start()
    pairs = [send_to(piece, got.at[c], (psend, precv), 0, mate)]
    pairs[0].start()
    for step in range(1, nz):
        copies[step - 1].wait_recv()
        origin = 2 * lax.rem(z - step + nz, nz) + k
        pairs.append(send_to(got.at[origin], got.at[origin], (psend, precv), step, mate))
        pairs[-1].start()
    for copy in copies:
        copy.wait_send()
    for pair in pairs:
        pair.wait()


def last_kernel(n_row, nz, wanted, filtered, plane_got, every, send, recv, up_send, up_recv, down_send, down_recv,
                psend, precv):
    r, c, z, k, others = place_of(nz)
    mate = (r, 2 * z + 1 - k)
    lines = [(lax.rem(r + step, n_row), c) for step in range(1, n_row)]
    above, below = (r, 2 * lax.rem(z + 1, nz) + k), (r, 2 * lax.rem(z + nz - 1, nz) + k)
    greet(lines + [above, below, mate])
    plane = [send_to(wanted.at[to[0]], plane_got.at[r], (send, recv), step, to) for step, to in enumerate(lines)]

    def up(step, own):
        block = every.at[2 * lax.rem(z - step + nz, nz) + k]
        return send_to(filtered if own else block, block, (up_send, up_recv), step, above)

    def down(step, own):
        block = every.at[2 * lax.rem(z + step, nz) + k]
        return send_to(filtered if own else block, block, (down_send, down_recv), step, below)

    def across(step, own):
        block = every.at[2 * lax.rem(z + step, nz) + k]
        return send_to(filtered if own else block, block, (psend, precv), step, mate)

    @pl.when(z < nz - 1)
    def _():
        up(0, True).start()

    @pl.when(z > 0)
    def _():
        down(0, True).start()

    across(0, True).start()
    for copy in plane:
        copy.start()
    for step in range(1, nz):
        @pl.when(z - step >= 0)
        def _():
            up(step - 1, False).wait_recv()
            across(nz - step, False).start()

        @pl.when((z - step >= 0) & (z < nz - 1))
        def _():
            up(step, False).start()

        @pl.when(z + step <= nz - 1)
        def _():
            down(step - 1, False).wait_recv()
            across(step, False).start()

        @pl.when((z + step <= nz - 1) & (z > 0))
        def _():
            down(step, False).start()
    for step in range(nz):
        @pl.when((z - step >= 0) & (z < nz - 1))
        def _():
            up(step, False).wait_send()

        @pl.when((z + step <= nz - 1) & (z > 0))
        def _():
            down(step, False).wait_send()
    for step in range(nz):
        across(step, False).wait()
    for copy in plane:
        copy.wait()


def pick(sources, index, dest, sem):
    start = 0
    for source in sources:
        stop = start + source.shape[0]

        @pl.when((index >= start) & (index < stop))
        def _(source=source, start=start):
            pltpu.make_async_copy(source.at[index - start], dest, sem).start()

        start = stop


def gather_kernel(index, *refs):
    sources, (out, sem) = refs[:-2], refs[-2:]
    start = pl.program_id(0) * out.shape[0]

    def begin(i, carry):
        pick(sources, index[start + i], out.at[i], sem)
        return carry

    lax.fori_loop(0, out.shape[0], begin, 0)
    pltpu.make_async_copy(out, out, sem).wait()


def flat(array):
    return array.reshape((-1,) + array.shape[-2:])


def gather(index, *sources):
    block = sources[0].shape[-2:]
    count = index.shape[0]
    chunk = max(n for n in range(1, min(count, 512) + 1) if count % n == 0)
    return pl.pallas_call(
        gather_kernel,
        grid=(count // chunk,),
        out_shape=jax.ShapeDtypeStruct((count,) + block, sources[0].dtype),
        in_specs=[SMEM] + [ANY] * len(sources), out_specs=pl.BlockSpec((chunk,) + block, lambda i: (i, 0, 0)),
        scratch_shapes=[DMA],
        compiler_params=pltpu.CompilerParams(vmem_limit_bytes=BIG),
    )(index, *[flat(source) for source in sources])


def square_kernel(left_at, right_at, slot, keep, lefts, own_left, rights, own_rights, out, a, b, acc, sems):
    count = out.shape[0]

    def begin(i, carry):
        pick((lefts, own_left), left_at[i], a.at[i], sems.at[0])
        pick((rights, own_rights), right_at[i], b.at[i], sems.at[1])
        return carry

    lax.fori_loop(0, count, begin, 0)
    acc[...] = jnp.zeros_like(acc)
    pltpu.make_async_copy(a, a, sems.at[0]).wait()
    pltpu.make_async_copy(b, b, sems.at[1]).wait()

    def multiply(q, carry):
        ids = [q * 4 + i for i in range(4)]
        terms = [jnp.dot(a[i], b[i], preferred_element_type=jnp.float32) for i in ids]
        for i, term in zip(ids, terms):
            acc[slot[i]] += term
        return carry

    lax.fori_loop(0, count // 4, multiply, 0)

    def write(i, carry):
        out[i] = (acc[i] * keep[i].astype(jnp.float32)).astype(out.dtype)
        return carry

    lax.fori_loop(0, count, write, 0)


def cubed_kernel(left_at, right_at, target, own_target, every, own, got1, send1, got2, send2, out, a, b, f, acc, sems):
    count = a.shape[0]
    windows = acc.shape[0]
    block = a.shape[-1]
    per_window = count // windows
    own_per_window = f.shape[0] // windows
    mine = pltpu.make_async_copy(own, f, sems.at[2])
    mine.start()

    def begin(i, carry):
        pick((every, own), left_at[i], a.at[i], sems.at[0])
        pick((got1, send1, got2, send2), right_at[i], b.at[i], sems.at[1])
        return carry

    lax.fori_loop(0, count, begin, 0)
    acc[...] = jnp.zeros_like(acc)
    mine.wait()
    for w in range(windows):
        def add(i, carry):
            e = w * own_per_window + i
            acc[w, own_target[e]] -= 1.5 * f[e].astype(jnp.float32)
            return carry

        lax.fori_loop(0, own_per_window, add, 0)
    pltpu.make_async_copy(a, a, sems.at[0]).wait()
    pltpu.make_async_copy(b, b, sems.at[1]).wait()
    for w in range(windows):
        def multiply(q, carry):
            ids = [w * per_window + q * 4 + i for i in range(4)]
            terms = [jnp.dot(a[i], b[i], preferred_element_type=jnp.float32) for i in ids]
            for i, term in zip(ids, terms):
                acc[w, target[i]] += term
            return carry

        lax.fori_loop(0, per_window // 4, multiply, 0)
    for w in range(windows):
        for j in range(acc.shape[1]):
            out[w * block:(w + 1) * block, j * block:(j + 1) * block] = (-2.0 * acc[w, j]).astype(out.dtype)


def running(mask):
    n = mask.shape[-1]
    before = (jnp.arange(n)[:, None] < jnp.arange(n)[None, :]).astype(jnp.bfloat16)
    lines = mask.reshape(-1, n).astype(jnp.bfloat16)
    return jnp.dot(lines, before, preferred_element_type=jnp.float32).astype(jnp.int32).reshape(mask.shape)


def general(owned_blocks, owned_rows, owned_cols, keep):
    n_row, n_col = lax.axis_size("row"), lax.axis_size("col")
    devices = n_row * n_col
    nz = n_col // 2
    r, c = lax.axis_index("row"), lax.axis_index("col")
    z, k = c // 2, lax.rem(c, 2)
    block = owned_blocks.shape[-1]
    dtype = owned_blocks.dtype
    slots = owned_rows.shape[0]
    per_band = slots // n_row
    windows, gcols = keep.shape
    nb = gcols * n_col
    size = slots * (1 + n_col)
    tall = -(-size // 1024) * 8
    one = (block, block)
    chips = devices // 2
    pool = 2 * slots
    i32 = jnp.int32

    packed = jnp.concatenate([owned_rows[:, None], owned_cols], axis=1).reshape(-1)
    meta = jnp.pad(packed, (0, tall * 128 - size)).reshape(tall, 128)
    meta_all, sibling = pl.pallas_call(
        functools.partial(spread_kernel, n_row, n_col),
        out_shape=(jax.ShapeDtypeStruct((devices, tall, 128), i32),
                   jax.ShapeDtypeStruct((slots, nz) + one, dtype)),
        in_specs=[ANY, ANY], out_specs=(ANY, ANY),
        scratch_shapes=[DMA((devices,)), DMA((devices,)), DMA, DMA],
        compiler_params=remote_params(0),
    )(meta, owned_blocks.reshape((slots, nz, 2) + one))
    me = r * n_col + c
    is_me = jnp.arange(devices)[:, None] == me
    labels = jnp.where(is_me, packed[None, :], meta_all.reshape(devices, -1)[:, :size])
    labels = labels.reshape(devices * slots, 1 + n_col)
    rows, cols = labels[:, 0], labels[:, 1:]
    slot_ids = jnp.arange(devices * slots, dtype=i32)
    every_row = jnp.arange(nb, dtype=i32)
    filled = rows < gcols * 2
    row_id = jnp.where(filled, gcols * (slot_ids // per_band % n_row + n_row * (rows // gcols)) + rows % gcols, nb)
    holder = jnp.sum(jnp.where(row_id[None, :] == every_row[:, None], slot_ids[None, :], 0), axis=1)
    row_cols = cols[holder]
    chip = holder // pool
    line, plane = chip // nz, chip % nz

    base = gcols * jnp.arange(n_col, dtype=i32)
    window = gcols * jnp.arange(n_row, dtype=i32)[:, None] + jnp.arange(windows, dtype=i32)[None, :]
    inner = base + row_cols[window]
    targets = base + row_cols[inner]
    is_window = jnp.any(window[:, :, None] == every_row, axis=1)
    is_inner = jnp.any(inner.reshape(n_row, -1, 1) == every_row, axis=1) & ~is_window
    is_target = jnp.any(targets.reshape(n_row, -1, 1) == every_row, axis=1) & ~is_inner & ~is_window
    urgent = jnp.any(is_window | is_inner, axis=0)
    wanted_row = urgent.astype(i32) + jnp.any(is_window | is_inner | is_target, axis=0).astype(i32)
    wanted = jnp.sum(jnp.where(row_id[:, None] == every_row[None, :], wanted_row[None, :], 0), axis=1).reshape(chips, pool)
    urgent_count = (wanted == 2).sum(axis=1)
    place = jnp.where(wanted == 2, running(wanted == 2), urgent_count[:, None] + running(wanted == 1))
    place = jnp.where(wanted > 0, place, pool)
    spot = place.reshape(-1)[holder]
    on_line = line[None, :] == jnp.arange(n_row, dtype=i32)[:, None]

    def ranks(need):
        both = need[:, None, :] & on_line[None, :, :]
        rank = jnp.sum(jnp.where(both, running(both), 0), axis=1)
        return rank, both.sum(axis=2).max()

    rank_window, _ = ranks(is_window)
    rank_inner, most_inner = ranks(is_inner)

    def shares(early, limit):
        now = is_target & (spot < early)[None, :]
        rank_now, _ = ranks(now)
        now = now & (rank_now < limit)
        later = is_target & ~now
        rank_later, most_later = ranks(later)
        return now, rank_now, later, rank_later, most_later

    inner_mine = inner[r].reshape(-1)
    targets_mine = targets[r].reshape(-1)
    cols_mine = lax.dynamic_index_in_dim(row_cols, c, 1, keepdims=False)
    square_target = cols_mine[inner_mine].reshape(windows, n_col)
    same = square_target[:, :, None] == square_target[:, None, :]
    first = jnp.argmax(same, axis=2).astype(i32)
    square_slot = (first + n_col * jnp.arange(windows, dtype=i32)[:, None]).reshape(-1)
    kept = jnp.take_along_axis(keep, square_target, axis=1).reshape(-1)
    cubed_target = cols_mine[targets_mine]
    entries = windows * n_col

    step = (z - plane + nz) % nz
    zs = jnp.arange(nz, dtype=i32)[:, None]
    place_mine = lax.dynamic_index_in_dim(place, r * nz + z, 0, keepdims=False)

    def pooled(start, count):
        position = start + jnp.arange(count, dtype=i32)
        pick_slot = jnp.sum(
            jnp.where(place_mine[None, :] == position[:, None], jnp.arange(pool, dtype=i32)[None, :], 0), axis=1)
        at = pick_slot[None, :] % slots
        index = jnp.where(
            pick_slot[None, :] // slots == k, at * n_col + 2 * zs + k, slots * n_col + at * nz + zs)
        return gather(index.reshape(-1), owned_blocks, sibling).reshape((nz, count) + one)

    def demand(need, rank, count, source_at):
        sending = need & (line == r)[None, :]
        chosen = sending[:, None, :] & (rank[:, None, :] == jnp.arange(count, dtype=i32)[None, :, None])
        return jnp.sum(jnp.where(chosen, source_at[None, None, :], 0), axis=2)

    def opening(early, most, limit, share, parts):
        now, rank_now = share[:2]
        cap1 = windows + most + limit
        now_all = is_window | is_inner | now
        now_rank = jnp.where(is_window, rank_window, jnp.where(is_inner, windows + rank_inner, windows + most + rank_now))
        send1 = gather(demand(now_all, now_rank, cap1, step * early + spot).reshape(-1), *parts)
        found1 = line * cap1 + now_rank[r] + jnp.where(line == r, n_row * cap1, 0)
        return now_all, found1, send1.reshape((n_row, cap1) + one)

    def run(early, late, rest, share, parts, opened, outgoing, number):
        later, rank_later = share[2:4]
        now_all, found1, send1 = opened
        cap1 = send1.shape[1]
        late_at = jnp.where(plane == z, nz * late + plane * outgoing.shape[1], plane * late)
        held_at = jnp.where(spot < early, step * early + spot, nz * early + late_at + spot - early)
        got_late, got1 = pl.pallas_call(
            functools.partial(second_kernel, n_row, nz),
            out_shape=(jax.ShapeDtypeStruct((nz, late) + one, dtype),
                       jax.ShapeDtypeStruct((n_row, cap1) + one, dtype)),
            in_specs=[ANY, ANY], out_specs=(ANY, ANY),
            scratch_shapes=[DMA((nz,)), DMA((nz,)), DMA((n_row,)), DMA((n_row,))],
            compiler_params=remote_params(number + 1),
        )(outgoing, send1)
        window_mine = gcols * r + jnp.arange(windows, dtype=i32)
        left_mine = gather(found1[window_mine], got1, send1)
        lefts = pl.pallas_call(
            functools.partial(left_kernel, nz),
            out_shape=jax.ShapeDtypeStruct((n_col, windows) + one, dtype),
            in_specs=[ANY], out_specs=ANY,
            scratch_shapes=[DMA((nz,))] * 4,
            compiler_params=remote_params(number + 2),
        )(left_mine)
        ws = jnp.arange(windows, dtype=i32)[:, None]
        gs = jnp.arange(n_col, dtype=i32)[None, :]
        left_at = jnp.where(gs == c, n_col * windows + ws, gs * windows + ws).reshape(-1)
        filtered = pl.pallas_call(
            square_kernel,
            out_shape=jax.ShapeDtypeStruct((entries,) + one, dtype),
            in_specs=[SMEM] * 4 + [ANY] * 4, out_specs=VMEM,
            scratch_shapes=[pltpu.VMEM((entries,) + one, dtype), pltpu.VMEM((entries,) + one, dtype),
                            pltpu.VMEM((entries,) + one, jnp.float32), DMA((2,))],
            compiler_params=pltpu.CompilerParams(vmem_limit_bytes=BIG),
        )(left_at, found1[inner_mine], square_slot, kept, flat(lefts), left_mine, flat(got1), flat(send1))
        later_at = demand(later, rank_later, rest, held_at)
        send2 = gather(later_at.reshape(-1), *parts, got_late, outgoing).reshape((n_row, rest) + one)
        got2, every = pl.pallas_call(
            functools.partial(last_kernel, n_row, nz),
            out_shape=(jax.ShapeDtypeStruct((n_row, rest) + one, dtype),
                       jax.ShapeDtypeStruct((n_col, entries) + one, dtype)),
            in_specs=[ANY, ANY], out_specs=(ANY, ANY),
            scratch_shapes=[DMA((n_row,)), DMA((n_row,))] + [DMA((nz,))] * 6,
            compiler_params=remote_params(number + 3),
        )(send2, filtered)
        found2 = jnp.where(
            now_all[r], found1,
            2 * n_row * cap1 + line * rest + rank_later[r] + jnp.where(line == r, n_row * rest, 0))
        place3 = ws[:, :, None] * n_col + gs[:, :, None]
        groups = jnp.arange(n_col, dtype=i32)[None, None, :]
        left_at = jnp.where(groups == c, n_col * entries + place3, groups * entries + place3).reshape(-1)
        count = windows * n_col * n_col
        return pl.pallas_call(
            cubed_kernel,
            out_shape=jax.ShapeDtypeStruct((windows * block, gcols * block), dtype),
            in_specs=[SMEM] * 4 + [ANY] * 6, out_specs=VMEM,
            scratch_shapes=[pltpu.VMEM((count,) + one, dtype), pltpu.VMEM((count,) + one, dtype),
                            pltpu.VMEM((entries,) + one, dtype),
                            pltpu.VMEM((windows, gcols) + one, jnp.float32), DMA((3,))],
            compiler_params=pltpu.CompilerParams(vmem_limit_bytes=BIG),
        )(left_at, found2[targets_mine], cubed_target, square_target.reshape(-1), flat(every), filtered,
          flat(got1), flat(send1), flat(got2), flat(send2))

    most_demand = windows * n_col * n_col
    early, most, limit = 7 * pool // 32, 10 * entries // 16, most_demand // 8
    small = (early, 22 * most_demand // 128)
    middle = (26 * pool // 64, most_demand // 4)
    share = shares(early, limit)
    most_pool, most_urgent = (wanted > 0).sum(axis=1).max(), urgent_count.max()
    first_out = pooled(0, early)
    parts = [lax.dynamic_index_in_dim(first_out, z, 0, keepdims=False)]
    for by in range(1, nz):
        moved = lax.dynamic_index_in_dim(first_out, (z + by) % nz, 0, keepdims=False)
        parts.append(lax.ppermute(moved, "col", [(i, (i + 2 * by) % n_col) for i in range(n_col)]))
    late_out = pooled(early, middle[0])
    opened = opening(early, most, limit, share, parts)

    def usual(caps, number):
        return run(early, caps[0], caps[1], share, parts, opened, late_out, number)

    def widest(number):
        every_share = shares(pool, limit)
        outgoing = pooled(0, pool)
        got = pl.pallas_call(
            functools.partial(first_kernel, nz, pool),
            out_shape=jax.ShapeDtypeStruct((nz, pool) + one, dtype),
            in_specs=[ANY], out_specs=ANY,
            scratch_shapes=[DMA((nz,)), DMA((nz,))],
            compiler_params=remote_params(number),
        )(outgoing)
        held = [lax.dynamic_index_in_dim(outgoing, z, 0, keepdims=False)]
        held += [lax.dynamic_index_in_dim(got, (z - by + nz) % nz, 0, keepdims=False) for by in range(1, nz)]
        return run(pool, 1, min(most_demand, nb, n_col * slots), every_share, held,
                   opening(pool, entries, limit, every_share, held), outgoing, number)

    def fits(caps):
        return ((most_pool <= early + caps[0]) & (most_urgent <= early)
                & (most_inner <= most) & (share[-1] <= caps[1]))

    choice = jnp.where(fits(small), 0, jnp.where(fits(middle), 1, 2))
    return lax.switch(choice, [lambda: usual(small, 1), lambda: usual(middle, 5), lambda: widest(9)])


F32, BF16, I32 = jnp.float32, jnp.bfloat16, jnp.int32
LANES = 128
META = 16
ROWS = 40
STAGE = (0, 32, 64, 128)


def log2(n):
    return n.bit_length() - 1


def iota(shape, dim):
    return lax.broadcasted_iota(I32, shape, dim)


def ones(mask):
    return jnp.where(mask, 1.0, 0.0).astype(F32)


def times(a, b):
    return lax.dot_general(a.astype(BF16), b.astype(BF16), (((1,), (0,)), ((), ())), preferred_element_type=F32)


def against(a, b):
    return lax.dot_general(a.astype(BF16), b.astype(BF16), (((1,), (1,)), ((), ())), preferred_element_type=F32)


def most(column):
    return jnp.max(column, axis=0, keepdims=True)


def plan(spread, keep, r, c, sizes, tiers):
    n_row, n_col, slots, windows, gcols, nb = sizes
    nz = n_col // 2
    z, k = c // 2, lax.rem(c, 2)
    devices = n_row * n_col
    total = devices * slots
    per_band = slots // n_row
    out = {}
    lane = iota((1, total), 1)
    label = spread[n_col:n_col + 1, :].astype(I32)
    band = (lane >> log2(per_band)) & (n_row - 1)
    row_id = gcols * (band + n_row * (label >> log2(gcols))) + (label & (gcols - 1))
    row_id = jnp.where(label < 2 * gcols, row_id, nb)
    holds = ones(iota((nb, total), 0) == row_id)
    sub = iota((META, total), 0)
    device = lane >> log2(slots)
    fields = jnp.where(sub == n_col, device >> log2(n_col), 0)
    fields = jnp.where(sub == n_col + 1, (device & (n_col - 1)) >> 1, fields)
    fields = jnp.where(sub == n_col + 2, device & 1, fields)
    fields = jnp.where(sub == n_col + 3, lane & (slots - 1), fields)
    info = against(jnp.where(sub < n_col, spread, fields.astype(F32)), holds)
    line, plane, core, slot = [info[n_col + i:n_col + i + 1, :] for i in range(4)]
    column = jnp.zeros((1, nb), F32)
    for g in range(n_col):
        column = jnp.where(c == g, info[g:g + 1, :], column)
    within = iota((gcols, nb), 0).astype(F32)
    graph = jnp.concatenate([ones(info[g:g + 1, :] == within) for g in range(n_col)], axis=0).astype(BF16)
    upper = ones(iota((nb, nb), 0) < iota((nb, nb), 1)).astype(BF16)

    sub, row = iota((META, nb), 0), iota((META, nb), 1)
    wsel = ones((sub < n_row * windows) & (row == gcols * (sub >> log2(windows)) + (sub & (windows - 1))))
    once = against(wsel, graph)
    twice = against(once, graph)
    each = iota((1, nb), 1)
    soon, late = [], []
    for q in range(n_row):
        inner = sum(once[windows * q + i:windows * q + i + 1, :] for i in range(windows))
        target = sum(twice[windows * q + i:windows * q + i + 1, :] for i in range(windows))
        is_window = ((each >> log2(gcols)) == q) & ((each & (gcols - 1)) < windows)
        s = jnp.where(is_window, 1.0, ones(inner > 0.5))
        soon.append(s)
        late.append(ones(target > 0.5) * (1.0 - s))
    urgent = ones(sum(soon) > 0.5)
    need = ones(sum(soon) + sum(late) > 0.5)

    chip = (line * nz + plane).astype(I32)
    on_chip = ones(sub == chip)
    soon_mask, late_mask = on_chip * urgent, on_chip * (need - urgent)
    soon_count = jnp.sum(soon_mask, axis=1, keepdims=True)
    late_count = jnp.sum(late_mask, axis=1, keepdims=True)
    rank = jnp.where(urgent > 0.5, times(soon_mask, upper), soon_count + times(late_mask, upper))
    spot = jnp.sum(on_chip * rank, axis=0, keepdims=True)
    spot = jnp.where(need > 0.5, spot, 999.0)
    most_soon, most_pool = most(soon_count), most(soon_count + late_count)
    tight = (most_soon <= tiers[0]["n"][0]) & (most_pool <= sum(tiers[1]["n"]))
    first = jnp.where(tight, float(tiers[0]["n"][0]), float(tiers[2]["n"][0]))
    second = first + float(tiers[0]["n"][1])
    m0, m1 = tiers[0]["m"][:2]

    sender, getter = sub >> log2(n_row), sub & (n_row - 1)
    soon_pair, late_pair = jnp.zeros((META, nb), F32), jnp.zeros((META, nb), F32)
    for q in range(n_row):
        soon_pair = jnp.where(getter == q, soon[q], soon_pair)
        late_pair = jnp.where(getter == q, late[q], late_pair)
    from_line = ones((sender == line.astype(I32)) & (sender != getter))
    soon_pair, late_pair = soon_pair * from_line, late_pair * from_line
    soon_sum = jnp.sum(soon_pair, axis=1, keepdims=True)
    can = late_pair * ones(spot < first)
    at0 = jnp.where(soon_pair > 0.5, times(soon_pair, upper), soon_sum + times(can, upper))
    in0 = can * ones(at0 < float(m0))
    can = late_pair * ones(spot < second) * (1.0 - in0)
    at1 = times(can, upper)
    in1 = can * ones(at1 < float(m1))
    rest = late_pair * (1.0 - in0) * (1.0 - in1)
    at2 = times(rest, upper)
    most_line, most_rest = most(soon_sum), most(jnp.sum(rest, axis=1, keepdims=True))
    key = jnp.where(rest > 0.5, STAGE[2] + at2, -1.0)
    key = jnp.where(in1 > 0.5, STAGE[1] + at1, key)
    key = jnp.where(soon_pair + in0 > 0.5, at0, key)

    choice = jnp.full((1, 1), len(tiers), I32)
    for t in reversed(range(len(tiers))):
        n, m = tiers[t]["n"], tiers[t]["m"]
        fits = ((first == float(n[0])) & (most_soon <= float(n[0])) & (most_pool <= float(sum(n)))
                & (most_line <= float(m0)) & (most_rest <= float(m[2])))
        choice = jnp.where(fits, t, choice)
    out[33] = jnp.broadcast_to(choice, (1, LANES))

    wide = iota((LANES, nb), 0)
    col = iota((LANES, nb), 1)
    step = z.astype(F32) - plane
    step = jnp.where(step < 0, step + nz, step)
    mine = ones(chip == (r * nz + z))
    pack = ones(wide.astype(F32) == jnp.where(mine > 0.5, spot, 999.0))
    from_slot = slot + slots * ones(core != k.astype(F32))
    rows = jnp.where(sub == 0, from_slot, jnp.where(sub == 1, step, jnp.where(sub == 2, spot, 0.0)))
    rows = jnp.minimum(rows, 127.0)
    out[0] = against(rows, pack)[0:1, :].astype(I32)
    for d in range(1, n_row):
        pair = r * n_row + lax.rem(r + d, n_row)
        key_of = jnp.sum(jnp.where(sub == pair, key, 0.0), axis=0, keepdims=True)
        got = against(rows, ones(wide.astype(F32) == key_of))
        out[d] = (64.0 * got[1:2, :] + got[2:3, :]).astype(I32)

    key_in = jnp.sum(jnp.where((sender == line.astype(I32)) & (getter == r), key, 0.0), axis=0, keepdims=True)
    away = r.astype(F32) - line
    away = jnp.where(away < 0, away + n_row, away)
    where_a = jnp.where(away == 0, step, nz - 1 + away)
    where_b = jnp.clip(jnp.where(away == 0, spot, key_in), 0.0, 127.0)
    fields = jnp.where(sub == 0, where_a, jnp.where(sub == 1, where_b, jnp.where(sub == 2, column, 0.0)))

    def location(found):
        return (128.0 * found[0:1, :] + found[1:2, :]).astype(I32)

    start = gcols * r
    group = col >> log2(gcols)
    out[32] = location(against(fields, ones((wide < windows) & (col == start + wide))))
    entries, count = windows * n_col, windows * n_col * n_col
    inner = against(ones(col == start + (wide >> log2(n_col))), graph)
    inner = inner * ones((group == (wide & (n_col - 1))) & (wide < entries))
    found = against(fields, inner)
    out[15] = location(found)
    lane_at = found[2:3, :]
    sub_at = jnp.sum(inner * column, axis=1, keepdims=True)
    here, there = iota((LANES, LANES), 0), iota((LANES, LANES), 1)
    same = ones((sub_at == lane_at) & ((here >> log2(n_col)) == (there >> log2(n_col)))
                & (here < entries) & (there < entries))
    leads = ones(jnp.sum(same * ones(there < here), axis=1, keepdims=True) < 0.5) * ones(here[:, 0:1] < entries)
    keeps = jnp.zeros((LANES, gcols), F32)
    tag = iota((LANES, gcols), 0) >> log2(n_col)
    for i in range(windows):
        keeps = jnp.where(tag == i, keep[i:i + 1, :].astype(F32), keeps)
    kept = jnp.sum(keeps * ones(iota((LANES, gcols), 1).astype(F32) == sub_at), axis=1, keepdims=True)
    out[16] = (same * leads * kept)[0:entries, :].astype(I32)
    place = gcols * (here[:, 0:1] >> log2(n_col)).astype(F32) + sub_at
    at = ones(place == there.astype(F32)) * leads
    out[13] = jnp.sum(at * here.astype(F32), axis=0, keepdims=True).astype(I32)
    out[14] = jnp.sum(at, axis=0, keepdims=True).astype(I32)

    inner = against(ones(col == start + (wide >> log2(n_col * n_col))), graph)
    inner = inner * ones(group == ((wide >> log2(n_col)) & (n_col - 1)))
    target = against(inner, graph) * ones(group == (wide & (n_col - 1)))
    found = against(fields, target)
    sub_at = gcols * (here[:, 0:1] >> log2(n_col * n_col)).astype(F32) + jnp.sum(target * column, axis=1, keepdims=True)
    lane_at = gcols * (there[0:1, :] >> log2(n_col * n_col)).astype(F32) + found[2:3, :]
    ahead = ones(sub_at == lane_at) * ones(there < here)
    order = jnp.sum(ones(lane_at < sub_at) + ahead, axis=1, keepdims=True)
    put = ones(order == there.astype(F32))
    narrow = iota((META, LANES), 0)
    got = times(jnp.where(narrow == 3, iota((META, LANES), 1).astype(F32), found), put)
    out[8] = location(got)
    out[9] = got[3:4, :].astype(I32)
    follows = ones(jnp.sum(ahead, axis=1, keepdims=True) > 0.5)
    out[10] = jnp.sum(put * follows, axis=0, keepdims=True).astype(I32)
    out[11] = (jnp.sum(ones(sub_at <= there.astype(F32)), axis=0, keepdims=True) - 1.0).astype(I32)
    out[12] = jnp.minimum(jnp.sum(ones(sub_at == there.astype(F32)), axis=0, keepdims=True), 1.0).astype(I32)
    return out


def plan_kernel(sizes, tiers, labels, cols, keep, owned, index, sibling, tile, tiles, send, recv, pair_send,
                pair_recv):
    n_row, n_col, slots = sizes[:3]
    r, c = lax.axis_index("row"), lax.axis_index("col")
    me = r * n_col + c
    devices = n_row * n_col
    barrier = pltpu.get_barrier_semaphore()

    def hello(i, carry):
        d = lax.rem(me + i, devices)
        pl.semaphore_signal(barrier, inc=1, device_id=(d // n_col, lax.rem(d, n_col)), device_id_type=MESH)
        return carry

    lax.fori_loop(1, devices, hello, 0)
    share = LANES // slots
    turned = against(ones(iota((META, n_col), 0) == iota((META, n_col), 1)), cols[...].astype(F32))
    turned = jnp.where(iota((META, slots), 0) == n_col, labels[...].astype(F32), turned)
    shift = slots * lax.rem(me, share)
    tile[...] = times(turned, ones(iota((slots, LANES), 0) + shift == iota((slots, LANES), 1))).astype(BF16)
    tiles[me] = tile[...]
    pl.semaphore_wait(barrier, devices - 1)
    z, k = c // 2, lax.rem(c, 2)
    other = 1 - k
    pair = pltpu.make_async_remote_copy(
        src_ref=owned.at[:, :, other], dst_ref=sibling, send_sem=pair_send, recv_sem=pair_recv,
        device_id=(r, 2 * z + other), device_id_type=MESH)

    def copy_to(i):
        d = lax.rem(me + i, devices)
        return pltpu.make_async_remote_copy(
            src_ref=tile, dst_ref=tiles.at[me], send_sem=send.at[i], recv_sem=recv.at[i],
            device_id=(d // n_col, lax.rem(d, n_col)), device_id_type=MESH)

    def begin(i, carry):
        copy_to(i).start()
        return carry

    def finish(i, carry):
        copy_to(i).wait()
        return carry

    lax.fori_loop(1, devices, begin, 0)
    pair.start()
    lax.fori_loop(1, devices, finish, 0)
    spread = jnp.concatenate(
        [sum(tiles[share * q + i].astype(F32) for i in range(share)) for q in range(devices // share)], axis=1)
    index[...] = jnp.zeros_like(index)
    for row, value in plan(spread, keep[...], r, c, sizes, tiers).items():
        index[row:row + value.shape[0], :] = value
    pair.wait()


def main_kernel(sizes, tier, index, owned, sibling, out, pool, zsend0, zsend1, zsend2, zall0, zall1, zall2,
                xsend0, xsend1, xsend2, xrecv0, xrecv1, xrecv2, lefts, parts, every, rights, sums, sems, zs, zr, xs, xr,
                ls, lr, us, ur, ds, dr, ps, pr):
    n_row, n_col, slots, windows, gcols, nb = sizes
    nz = n_col // 2
    entries, count = windows * n_col, windows * n_col * n_col
    block = out.shape[0] // windows
    r, c = lax.axis_index("row"), lax.axis_index("col")
    z, k = c // 2, lax.rem(c, 2)
    zsend, zall = (zsend0, zsend1, zsend2), (zall0, zall1, zall2)
    xsend, xrecv = (xsend0, xsend1, xsend2), (xrecv0, xrecv1, xrecv2)
    n, m = tier["n"], tier["m"]
    bounds = [0, n[0], n[0] + n[1], n[0] + n[1] + n[2]]
    others = [(r, 2 * lax.rem(z + step, nz) + k) for step in range(1, nz)]
    lines = [(lax.rem(r + step, n_row), c) for step in range(1, n_row)]
    mate = (r, 2 * z + 1 - k)
    above, below = others[0], others[-1]
    loads = [pltpu.make_async_copy(owned.at[:, :, k], pool.at[pl.ds(0, slots)], sems.at[0]),
             pltpu.make_async_copy(sibling, pool.at[pl.ds(slots, slots)], sems.at[1])]
    for load in loads:
        load.start()
    greet(others + lines + [mate])
    for load in loads:
        load.wait()

    def zpack(s):
        def body(p, carry):
            slot = index[0, bounds[s] + p]
            zall[s][p] = pool[slot, z]
            for step in range(1, nz):
                zsend[s][(step - 1) * n[s] + p] = pool[slot, lax.rem(z + step, nz)]
            return carry

        lax.fori_loop(0, n[s], body, 0)

    def zcopies(s):
        return [pltpu.make_async_remote_copy(
            src_ref=zsend[s].at[pl.ds((step - 1) * n[s], n[s])], dst_ref=zall[s].at[pl.ds(step * n[s], n[s])],
            send_sem=zs.at[s * nz + step], recv_sem=zr.at[s * nz + step], device_id=others[step - 1],
            device_id_type=MESH) for step in range(1, nz)]

    def from_z(step, spot, upto, value):
        for s in upto:
            inside = (step >= 0) & (spot >= bounds[s]) & (spot < bounds[s + 1])
            got = zall[s][jnp.where(inside, step * n[s] + spot - bounds[s], 0)]
            value = got if value is None else lax.select(inside, got, value)
        return value

    def from_x(away, key, upto, value):
        for s in upto:
            inside = (away >= 0) & (key >= STAGE[s]) & (key < STAGE[s] + m[s])
            got = xrecv[s][jnp.where(inside, away * m[s] + key - STAGE[s], 0)]
            value = lax.select(inside, got, value)
        return value

    def fetch(code, zupto, xupto, value=None):
        a, b = code // 128, lax.rem(code, 128)
        value = from_z(jnp.where(a < nz, a, -1), b, zupto, value)
        return from_x(jnp.where(a < nz, -1, a - nz), b, xupto, value)

    def xpack(s):
        for d in range(1, n_row):
            def body(q, carry):
                code = index[d, STAGE[s] + q]
                xsend[s][(d - 1) * m[s] + q] = from_z(code // 64, lax.rem(code, 64), range(s + 1), None)
                return carry

            lax.fori_loop(0, m[s], body, 0)

    def xcopies(s):
        return [pltpu.make_async_remote_copy(
            src_ref=xsend[s].at[pl.ds((d - 1) * m[s], m[s])], dst_ref=xrecv[s].at[pl.ds((d - 1) * m[s], m[s])],
            send_sem=xs.at[s * n_row + d], recv_sem=xr.at[s * n_row + d], device_id=lines[d - 1],
            device_id_type=MESH) for d in range(1, n_row)]

    def start(copies):
        for copy in copies:
            copy.start()

    def arrive(copies):
        for copy in copies:
            copy.wait_recv()

    def left_send(sem, source, to):
        slab = lefts.at[source]
        return pltpu.make_async_remote_copy(
            src_ref=slab, dst_ref=slab, send_sem=ls.at[sem], recv_sem=lr.at[sem], device_id=to, device_id_type=MESH)

    zpack(0)
    start(zcopies(0))
    zpack(1)
    start(zcopies(1))
    zpack(2)
    arrive(zcopies(0))
    xpack(0)
    start(xcopies(0))
    arrive(xcopies(0))
    for i in range(windows):
        lefts[c, i] = fetch(index[32, i], [0], [0])
    left_out = [left_send(step, c, to) for step, to in enumerate(others)]
    left_pair = [left_send(nz, c, mate)]
    start(left_out)
    start(left_pair)
    start(zcopies(2))
    arrive(zcopies(1))
    xpack(1)
    start(xcopies(1))
    for step in range(1, nz):
        left_out[step - 1].wait_recv()
        left_pair.append(left_send(nz + step, 2 * lax.rem(z - step + nz, nz) + k, mate))
        left_pair[-1].start()
    arrive(left_pair)

    def square(e, carry):
        right = fetch(index[15, e], [0], [0])
        left = lefts[lax.rem(e, n_col), e // n_col]
        parts[e] = jnp.dot(left, right, preferred_element_type=F32)
        return carry

    lax.fori_loop(0, entries, square, 0)

    def merge(e, carry):
        start_at = e // n_col * n_col
        total = parts[start_at] * index[16 + e, start_at].astype(F32)
        for i in range(1, n_col):
            total += parts[start_at + i] * index[16 + e, start_at + i].astype(F32)
        every[c, e] = total.astype(BF16)
        return carry

    lax.fori_loop(0, entries, merge, 0)

    def pass_on(sem, step, place, to):
        slab = every.at[place]
        return pltpu.make_async_remote_copy(
            src_ref=slab, dst_ref=slab, send_sem=sem[0].at[step], recv_sem=sem[1].at[step], device_id=to,
            device_id_type=MESH)

    def up(step):
        return pass_on((us, ur), step, 2 * lax.rem(z - step + nz, nz) + k, above)

    def down(step):
        return pass_on((ds, dr), step, 2 * lax.rem(z + step, nz) + k, below)

    def across(step):
        return pass_on((ps, pr), step, 2 * lax.rem(z + step, nz) + k, mate)

    def relay(step):
        @pl.when(z - step >= 0)
        def _():
            up(step - 1).wait_recv()
            across(nz - step).start()

        @pl.when((z - step >= 0) & (z < nz - 1))
        def _():
            up(step).start()

        @pl.when(z + step <= nz - 1)
        def _():
            down(step - 1).wait_recv()
            across(step).start()

        @pl.when((z + step <= nz - 1) & (z > 0))
        def _():
            down(step).start()

    @pl.when(z < nz - 1)
    def _():
        up(0).start()

    @pl.when(z > 0)
    def _():
        down(0).start()

    across(0).start()
    arrive(xcopies(1))

    def gather_early(t, carry):
        rights[t] = fetch(index[8, t], [0, 1], [0, 1])
        return carry

    lax.fori_loop(0, count, gather_early, 0)
    relay(1)
    arrive(zcopies(2))
    xpack(2)
    start(xcopies(2))
    for step in range(2, nz):
        relay(step)
    for step in range(nz):
        across(step).wait_recv()
    arrive(xcopies(2))

    def multiply(q, acc):
        for i in range(4):
            t = q * 4 + i
            p = index[9, t]
            right = fetch(index[8, t], [2], [2], rights[t])
            term = jnp.dot(every[lax.rem(p, n_col), p // n_col], right, preferred_element_type=F32)
            acc = acc * index[10, t].astype(F32) + term
            sums[t] = acc
        return acc

    lax.fori_loop(0, count // 4, multiply, jnp.zeros((block, block), F32))
    for w in range(windows):
        def write(j, carry):
            at = w * gcols + j
            cube = sums[jnp.maximum(index[11, at], 0)] * (-2.0 * index[12, at].astype(F32))
            own = every[c, index[13, at]].astype(F32) * (3.0 * index[14, at].astype(F32))
            out[w * block:(w + 1) * block, pl.ds(pl.multiple_of(j * block, block), block)] = (own + cube).astype(BF16)
            return carry

        lax.fori_loop(0, gcols, write, 0)

    for s in range(3):
        for copy in zcopies(s) + xcopies(s):
            copy.wait_send()
    for copy in left_out + left_pair:
        copy.wait_send()
    for step in range(nz):
        @pl.when((z - step >= 0) & (z < nz - 1))
        def _():
            up(step).wait_send()

        @pl.when((z + step <= nz - 1) & (z > 0))
        def _():
            down(step).wait_send()

        across(step).wait_send()


TIERS = (dict(n=(11, 6, 9), m=(14, 12, 16)), dict(n=(11, 6, 14), m=(14, 12, 22)), dict(n=(14, 6, 20), m=(14, 12, 22)))


def local(owned_blocks, owned_rows, owned_cols, keep):
    n_row, n_col = lax.axis_size("row"), lax.axis_size("col")
    nz = n_col // 2
    slots = owned_rows.shape[0]
    windows, gcols = keep.shape
    nb = gcols * n_col
    block = owned_blocks.shape[-1]
    one = (block, block)
    dtype = owned_blocks.dtype
    entries, count = windows * n_col, windows * n_col * n_col
    if (count > LANES or n_col > 8 or n_row > 4 or entries > 16 or nz > 4 or LANES % slots or 2 * slots > 64
            or windows * gcols > LANES or n_row < 2 or nz < 2):
        return general(owned_blocks, owned_rows, owned_cols, keep)
    sizes = (n_row, n_col, slots, windows, gcols, nb)
    devices = n_row * n_col
    halves = owned_blocks.reshape((slots, nz, 2) + one)
    index, sibling = pl.pallas_call(
        functools.partial(plan_kernel, sizes, TIERS),
        out_shape=(jax.ShapeDtypeStruct((ROWS, LANES), I32), jax.ShapeDtypeStruct((slots, nz) + one, dtype)),
        in_specs=[VMEM, VMEM, VMEM, ANY], out_specs=(VMEM, ANY),
        scratch_shapes=[pltpu.VMEM((META, LANES), BF16), pltpu.VMEM((devices, META, LANES), BF16),
                        DMA((devices,)), DMA((devices,)), DMA, DMA],
        compiler_params=pltpu.CompilerParams(collective_id=20, has_side_effects=True, vmem_limit_bytes=BIG),
    )(owned_rows[None, :], owned_cols, keep, halves)

    def quick(t):
        n, m = TIERS[t]["n"], TIERS[t]["m"]
        scratch = [pltpu.VMEM((2 * slots, nz) + one, dtype)]
        scratch += [pltpu.VMEM(((nz - 1) * q,) + one, dtype) for q in n]
        scratch += [pltpu.VMEM((nz * q,) + one, dtype) for q in n]
        scratch += [pltpu.VMEM(((n_row - 1) * q,) + one, dtype) for q in m] * 2
        scratch += [pltpu.VMEM((n_col, windows) + one, dtype), pltpu.VMEM((entries,) + one, F32),
                    pltpu.VMEM((n_col, entries) + one, dtype), pltpu.VMEM((count,) + one, dtype),
                    pltpu.VMEM((count,) + one, F32), DMA((2,))]
        scratch += [DMA((3 * nz,))] * 2 + [DMA((3 * n_row,))] * 2 + [DMA((2 * nz,))] * 2 + [DMA((nz,))] * 6
        return pl.pallas_call(
            functools.partial(main_kernel, sizes, TIERS[t]),
            out_shape=jax.ShapeDtypeStruct((windows * block, gcols * block), dtype),
            in_specs=[SMEM, ANY, ANY], out_specs=VMEM, scratch_shapes=scratch,
            compiler_params=pltpu.CompilerParams(
                collective_id=21 + t, has_side_effects=True, vmem_limit_bytes=BIG),
        )(index, halves, sibling)

    branches = [functools.partial(quick, t) for t in range(len(TIERS))]
    branches.append(lambda: general(owned_blocks, owned_rows, owned_cols, keep))
    return lax.switch(index[33, 0], branches)


def solution(mesh):
    placed = (
        P(("row", "col"), None, None, None),
        P(("row", "col")),
        P(("row", "col"), None),
        P("row", "col"),
    )
    return jax.shard_map(
        local, mesh=mesh, in_specs=placed, out_specs=P("row", "col"), check_vma=False
    )
```

```python
import functools

import jax
import jax.numpy as jnp
from jax import lax
from jax.experimental import pallas as pl
from jax.experimental.pallas import tpu as pltpu
from jax.sharding import PartitionSpec as P

MESH = pl.DeviceIdType.MESH
ANY = pl.BlockSpec(memory_space=pl.ANY)
SMEM = pl.BlockSpec(memory_space=pltpu.SMEM)
VMEM = pl.BlockSpec(memory_space=pltpu.VMEM)
DMA = pltpu.SemaphoreType.DMA
BIG = 60 * 1024 * 1024


def remote_params(number):
    return pltpu.CompilerParams(collective_id=number, has_side_effects=True)


def spread_kernel(n_row, n_col, meta, owned, meta_all, sibling, send, recv, pair_send, pair_recv):
    r, c = lax.axis_index("row"), lax.axis_index("col")
    me = r * n_col + c
    devices = n_row * n_col
    barrier = pltpu.get_barrier_semaphore()

    def greet(i, carry):
        d = lax.rem(me + i, devices)
        pl.semaphore_signal(barrier, inc=1, device_id=(d // n_col, lax.rem(d, n_col)), device_id_type=MESH)
        return carry

    lax.fori_loop(1, devices, greet, 0)
    pl.semaphore_wait(barrier, devices - 1)
    z, k = c // 2, lax.rem(c, 2)
    other = 1 - k
    pair = pltpu.make_async_remote_copy(
        src_ref=owned.at[:, :, other], dst_ref=sibling, send_sem=pair_send, recv_sem=pair_recv,
        device_id=(r, 2 * z + other), device_id_type=MESH)
    pair.start()

    def copy_to(i):
        d = lax.rem(me + i, devices)
        return pltpu.make_async_remote_copy(
            src_ref=meta, dst_ref=meta_all.at[me], send_sem=send.at[i], recv_sem=recv.at[i],
            device_id=(d // n_col, lax.rem(d, n_col)), device_id_type=MESH)

    def begin(i, carry):
        copy_to(i).start()
        return carry

    def finish(i, carry):
        copy_to(i).wait()
        return carry

    lax.fori_loop(1, devices, begin, 0)
    lax.fori_loop(1, devices, finish, 0)
    pair.wait()


def greet(partners):
    barrier = pltpu.get_barrier_semaphore()
    for partner in partners:
        pl.semaphore_signal(barrier, inc=1, device_id=partner, device_id_type=MESH)
    pl.semaphore_wait(barrier, len(partners))


def send_to(source, dest, sems, step, partner):
    return pltpu.make_async_remote_copy(
        src_ref=source, dst_ref=dest, send_sem=sems[0].at[step], recv_sem=sems[1].at[step],
        device_id=partner, device_id_type=MESH)


def place_of(nz):
    r, c = lax.axis_index("row"), lax.axis_index("col")
    z, k = c // 2, lax.rem(c, 2)
    return r, c, z, k, [(r, 2 * lax.rem(z + step, nz) + k) for step in range(1, nz)]


def first_kernel(nz, count, source, got, send, recv):
    r, c, z, k, others = place_of(nz)
    greet(others)
    copies = [send_to(source.at[to[1] // 2, pl.ds(0, count)], got.at[z], (send, recv), step, to)
              for step, to in enumerate(others)]
    for copy in copies:
        copy.start()
    for copy in copies:
        copy.wait()


def second_kernel(n_row, nz, source, wanted, got, plane_got, send, recv, psend, precv):
    r, c, z, k, others = place_of(nz)
    lines = [(lax.rem(r + step, n_row), c) for step in range(1, n_row)]
    greet(others + lines)
    count = got.shape[1]
    copies = [send_to(wanted.at[to[0]], plane_got.at[r], (psend, precv), step, to) for step, to in enumerate(lines)]
    copies += [send_to(source.at[to[1] // 2, pl.ds(0, count)], got.at[z], (send, recv), step, to)
               for step, to in enumerate(others)]
    for copy in copies:
        copy.start()
    for copy in copies:
        copy.wait()


def left_kernel(nz, piece, got, send, recv, psend, precv):
    r, c, z, k, others = place_of(nz)
    mate = (r, 2 * z + 1 - k)
    greet(others + [mate])
    copies = [send_to(piece, got.at[c], (send, recv), step, to) for step, to in enumerate(others)]
    for copy in copies:
        copy.start()
    pairs = [send_to(piece, got.at[c], (psend, precv), 0, mate)]
    pairs[0].start()
    for step in range(1, nz):
        copies[step - 1].wait_recv()
        origin = 2 * lax.rem(z - step + nz, nz) + k
        pairs.append(send_to(got.at[origin], got.at[origin], (psend, precv), step, mate))
        pairs[-1].start()
    for copy in copies:
        copy.wait_send()
    for pair in pairs:
        pair.wait()


def last_kernel(n_row, nz, wanted, filtered, plane_got, every, send, recv, up_send, up_recv, down_send, down_recv,
                psend, precv):
    r, c, z, k, others = place_of(nz)
    mate = (r, 2 * z + 1 - k)
    lines = [(lax.rem(r + step, n_row), c) for step in range(1, n_row)]
    above, below = (r, 2 * lax.rem(z + 1, nz) + k), (r, 2 * lax.rem(z + nz - 1, nz) + k)
    greet(lines + [above, below, mate])
    plane = [send_to(wanted.at[to[0]], plane_got.at[r], (send, recv), step, to) for step, to in enumerate(lines)]

    def up(step, own):
        block = every.at[2 * lax.rem(z - step + nz, nz) + k]
        return send_to(filtered if own else block, block, (up_send, up_recv), step, above)

    def down(step, own):
        block = every.at[2 * lax.rem(z + step, nz) + k]
        return send_to(filtered if own else block, block, (down_send, down_recv), step, below)

    def across(step, own):
        block = every.at[2 * lax.rem(z + step, nz) + k]
        return send_to(filtered if own else block, block, (psend, precv), step, mate)

    @pl.when(z < nz - 1)
    def _():
        up(0, True).start()

    @pl.when(z > 0)
    def _():
        down(0, True).start()

    across(0, True).start()
    for copy in plane:
        copy.start()
    for step in range(1, nz):
        @pl.when(z - step >= 0)
        def _():
            up(step - 1, False).wait_recv()
            across(nz - step, False).start()

        @pl.when((z - step >= 0) & (z < nz - 1))
        def _():
            up(step, False).start()

        @pl.when(z + step <= nz - 1)
        def _():
            down(step - 1, False).wait_recv()
            across(step, False).start()

        @pl.when((z + step <= nz - 1) & (z > 0))
        def _():
            down(step, False).start()
    for step in range(nz):
        @pl.when((z - step >= 0) & (z < nz - 1))
        def _():
            up(step, False).wait_send()

        @pl.when((z + step <= nz - 1) & (z > 0))
        def _():
            down(step, False).wait_send()
    for step in range(nz):
        across(step, False).wait()
    for copy in plane:
        copy.wait()


def pick(sources, index, dest, sem):
    start = 0
    for source in sources:
        stop = start + source.shape[0]

        @pl.when((index >= start) & (index < stop))
        def _(source=source, start=start):
            pltpu.make_async_copy(source.at[index - start], dest, sem).start()

        start = stop


def gather_kernel(index, *refs):
    sources, (out, sem) = refs[:-2], refs[-2:]
    start = pl.program_id(0) * out.shape[0]

    def begin(i, carry):
        pick(sources, index[start + i], out.at[i], sem)
        return carry

    lax.fori_loop(0, out.shape[0], begin, 0)
    pltpu.make_async_copy(out, out, sem).wait()


def flat(array):
    return array.reshape((-1,) + array.shape[-2:])


def gather(index, *sources):
    block = sources[0].shape[-2:]
    count = index.shape[0]
    chunk = max(n for n in range(1, min(count, 512) + 1) if count % n == 0)
    return pl.pallas_call(
        gather_kernel,
        grid=(count // chunk,),
        out_shape=jax.ShapeDtypeStruct((count,) + block, sources[0].dtype),
        in_specs=[SMEM] + [ANY] * len(sources), out_specs=pl.BlockSpec((chunk,) + block, lambda i: (i, 0, 0)),
        scratch_shapes=[DMA],
        compiler_params=pltpu.CompilerParams(vmem_limit_bytes=BIG),
    )(index, *[flat(source) for source in sources])


def square_kernel(left_at, right_at, slot, keep, lefts, own_left, rights, own_rights, out, a, b, acc, sems):
    count = out.shape[0]

    def begin(i, carry):
        pick((lefts, own_left), left_at[i], a.at[i], sems.at[0])
        pick((rights, own_rights), right_at[i], b.at[i], sems.at[1])
        return carry

    lax.fori_loop(0, count, begin, 0)
    acc[...] = jnp.zeros_like(acc)
    pltpu.make_async_copy(a, a, sems.at[0]).wait()
    pltpu.make_async_copy(b, b, sems.at[1]).wait()

    def multiply(q, carry):
        ids = [q * 4 + i for i in range(4)]
        terms = [jnp.dot(a[i], b[i], preferred_element_type=jnp.float32) for i in ids]
        for i, term in zip(ids, terms):
            acc[slot[i]] += term
        return carry

    lax.fori_loop(0, count // 4, multiply, 0)

    def write(i, carry):
        out[i] = (acc[i] * keep[i].astype(jnp.float32)).astype(out.dtype)
        return carry

    lax.fori_loop(0, count, write, 0)


def cubed_kernel(left_at, right_at, target, own_target, every, own, got1, send1, got2, send2, out, a, b, f, acc, sems):
    count = a.shape[0]
    windows = acc.shape[0]
    block = a.shape[-1]
    per_window = count // windows
    own_per_window = f.shape[0] // windows
    mine = pltpu.make_async_copy(own, f, sems.at[2])
    mine.start()

    def begin(i, carry):
        pick((every, own), left_at[i], a.at[i], sems.at[0])
        pick((got1, send1, got2, send2), right_at[i], b.at[i], sems.at[1])
        return carry

    lax.fori_loop(0, count, begin, 0)
    acc[...] = jnp.zeros_like(acc)
    mine.wait()
    for w in range(windows):
        def add(i, carry):
            e = w * own_per_window + i
            acc[w, own_target[e]] -= 1.5 * f[e].astype(jnp.float32)
            return carry

        lax.fori_loop(0, own_per_window, add, 0)
    pltpu.make_async_copy(a, a, sems.at[0]).wait()
    pltpu.make_async_copy(b, b, sems.at[1]).wait()
    for w in range(windows):
        def multiply(q, carry):
            ids = [w * per_window + q * 4 + i for i in range(4)]
            terms = [jnp.dot(a[i], b[i], preferred_element_type=jnp.float32) for i in ids]
            for i, term in zip(ids, terms):
                acc[w, target[i]] += term
            return carry

        lax.fori_loop(0, per_window // 4, multiply, 0)
    for w in range(windows):
        for j in range(acc.shape[1]):
            out[w * block:(w + 1) * block, j * block:(j + 1) * block] = (-2.0 * acc[w, j]).astype(out.dtype)


def running(mask):
    n = mask.shape[-1]
    before = (jnp.arange(n)[:, None] < jnp.arange(n)[None, :]).astype(jnp.bfloat16)
    lines = mask.reshape(-1, n).astype(jnp.bfloat16)
    return jnp.dot(lines, before, preferred_element_type=jnp.float32).astype(jnp.int32).reshape(mask.shape)


def general(owned_blocks, owned_rows, owned_cols, keep):
    n_row, n_col = lax.axis_size("row"), lax.axis_size("col")
    devices = n_row * n_col
    nz = n_col // 2
    r, c = lax.axis_index("row"), lax.axis_index("col")
    z, k = c // 2, lax.rem(c, 2)
    block = owned_blocks.shape[-1]
    dtype = owned_blocks.dtype
    slots = owned_rows.shape[0]
    per_band = slots // n_row
    windows, gcols = keep.shape
    nb = gcols * n_col
    size = slots * (1 + n_col)
    tall = -(-size // 1024) * 8
    one = (block, block)
    chips = devices // 2
    pool = 2 * slots
    i32 = jnp.int32

    packed = jnp.concatenate([owned_rows[:, None], owned_cols], axis=1).reshape(-1)
    meta = jnp.pad(packed, (0, tall * 128 - size)).reshape(tall, 128)
    meta_all, sibling = pl.pallas_call(
        functools.partial(spread_kernel, n_row, n_col),
        out_shape=(jax.ShapeDtypeStruct((devices, tall, 128), i32),
                   jax.ShapeDtypeStruct((slots, nz) + one, dtype)),
        in_specs=[ANY, ANY], out_specs=(ANY, ANY),
        scratch_shapes=[DMA((devices,)), DMA((devices,)), DMA, DMA],
        compiler_params=remote_params(0),
    )(meta, owned_blocks.reshape((slots, nz, 2) + one))
    me = r * n_col + c
    is_me = jnp.arange(devices)[:, None] == me
    labels = jnp.where(is_me, packed[None, :], meta_all.reshape(devices, -1)[:, :size])
    labels = labels.reshape(devices * slots, 1 + n_col)
    rows, cols = labels[:, 0], labels[:, 1:]
    slot_ids = jnp.arange(devices * slots, dtype=i32)
    every_row = jnp.arange(nb, dtype=i32)
    filled = rows < gcols * 2
    row_id = jnp.where(filled, gcols * (slot_ids // per_band % n_row + n_row * (rows // gcols)) + rows % gcols, nb)
    holder = jnp.sum(jnp.where(row_id[None, :] == every_row[:, None], slot_ids[None, :], 0), axis=1)
    row_cols = cols[holder]
    chip = holder // pool
    line, plane = chip // nz, chip % nz

    base = gcols * jnp.arange(n_col, dtype=i32)
    window = gcols * jnp.arange(n_row, dtype=i32)[:, None] + jnp.arange(windows, dtype=i32)[None, :]
    inner = base + row_cols[window]
    targets = base + row_cols[inner]
    is_window = jnp.any(window[:, :, None] == every_row, axis=1)
    is_inner = jnp.any(inner.reshape(n_row, -1, 1) == every_row, axis=1) & ~is_window
    is_target = jnp.any(targets.reshape(n_row, -1, 1) == every_row, axis=1) & ~is_inner & ~is_window
    urgent = jnp.any(is_window | is_inner, axis=0)
    wanted_row = urgent.astype(i32) + jnp.any(is_window | is_inner | is_target, axis=0).astype(i32)
    wanted = jnp.sum(jnp.where(row_id[:, None] == every_row[None, :], wanted_row[None, :], 0), axis=1).reshape(chips, pool)
    urgent_count = (wanted == 2).sum(axis=1)
    place = jnp.where(wanted == 2, running(wanted == 2), urgent_count[:, None] + running(wanted == 1))
    place = jnp.where(wanted > 0, place, pool)
    spot = place.reshape(-1)[holder]
    on_line = line[None, :] == jnp.arange(n_row, dtype=i32)[:, None]

    def ranks(need):
        both = need[:, None, :] & on_line[None, :, :]
        rank = jnp.sum(jnp.where(both, running(both), 0), axis=1)
        return rank, both.sum(axis=2).max()

    rank_window, _ = ranks(is_window)
    rank_inner, most_inner = ranks(is_inner)

    def shares(early, limit):
        now = is_target & (spot < early)[None, :]
        rank_now, _ = ranks(now)
        now = now & (rank_now < limit)
        later = is_target & ~now
        rank_later, most_later = ranks(later)
        return now, rank_now, later, rank_later, most_later

    inner_mine = inner[r].reshape(-1)
    targets_mine = targets[r].reshape(-1)
    cols_mine = lax.dynamic_index_in_dim(row_cols, c, 1, keepdims=False)
    square_target = cols_mine[inner_mine].reshape(windows, n_col)
    same = square_target[:, :, None] == square_target[:, None, :]
    first = jnp.argmax(same, axis=2).astype(i32)
    square_slot = (first + n_col * jnp.arange(windows, dtype=i32)[:, None]).reshape(-1)
    kept = jnp.take_along_axis(keep, square_target, axis=1).reshape(-1)
    cubed_target = cols_mine[targets_mine]
    entries = windows * n_col

    step = (z - plane + nz) % nz
    zs = jnp.arange(nz, dtype=i32)[:, None]
    place_mine = lax.dynamic_index_in_dim(place, r * nz + z, 0, keepdims=False)

    def pooled(start, count):
        position = start + jnp.arange(count, dtype=i32)
        pick_slot = jnp.sum(
            jnp.where(place_mine[None, :] == position[:, None], jnp.arange(pool, dtype=i32)[None, :], 0), axis=1)
        at = pick_slot[None, :] % slots
        index = jnp.where(
            pick_slot[None, :] // slots == k, at * n_col + 2 * zs + k, slots * n_col + at * nz + zs)
        return gather(index.reshape(-1), owned_blocks, sibling).reshape((nz, count) + one)

    def demand(need, rank, count, source_at):
        sending = need & (line == r)[None, :]
        chosen = sending[:, None, :] & (rank[:, None, :] == jnp.arange(count, dtype=i32)[None, :, None])
        return jnp.sum(jnp.where(chosen, source_at[None, None, :], 0), axis=2)

    def opening(early, most, limit, share, parts):
        now, rank_now = share[:2]
        cap1 = windows + most + limit
        now_all = is_window | is_inner | now
        now_rank = jnp.where(is_window, rank_window, jnp.where(is_inner, windows + rank_inner, windows + most + rank_now))
        send1 = gather(demand(now_all, now_rank, cap1, step * early + spot).reshape(-1), *parts)
        found1 = line * cap1 + now_rank[r] + jnp.where(line == r, n_row * cap1, 0)
        return now_all, found1, send1.reshape((n_row, cap1) + one)

    def run(early, late, rest, share, parts, opened, outgoing, number):
        later, rank_later = share[2:4]
        now_all, found1, send1 = opened
        cap1 = send1.shape[1]
        late_at = jnp.where(plane == z, nz * late + plane * outgoing.shape[1], plane * late)
        held_at = jnp.where(spot < early, step * early + spot, nz * early + late_at + spot - early)
        got_late, got1 = pl.pallas_call(
            functools.partial(second_kernel, n_row, nz),
            out_shape=(jax.ShapeDtypeStruct((nz, late) + one, dtype),
                       jax.ShapeDtypeStruct((n_row, cap1) + one, dtype)),
            in_specs=[ANY, ANY], out_specs=(ANY, ANY),
            scratch_shapes=[DMA((nz,)), DMA((nz,)), DMA((n_row,)), DMA((n_row,))],
            compiler_params=remote_params(number + 1),
        )(outgoing, send1)
        window_mine = gcols * r + jnp.arange(windows, dtype=i32)
        left_mine = gather(found1[window_mine], got1, send1)
        lefts = pl.pallas_call(
            functools.partial(left_kernel, nz),
            out_shape=jax.ShapeDtypeStruct((n_col, windows) + one, dtype),
            in_specs=[ANY], out_specs=ANY,
            scratch_shapes=[DMA((nz,))] * 4,
            compiler_params=remote_params(number + 2),
        )(left_mine)
        ws = jnp.arange(windows, dtype=i32)[:, None]
        gs = jnp.arange(n_col, dtype=i32)[None, :]
        left_at = jnp.where(gs == c, n_col * windows + ws, gs * windows + ws).reshape(-1)
        filtered = pl.pallas_call(
            square_kernel,
            out_shape=jax.ShapeDtypeStruct((entries,) + one, dtype),
            in_specs=[SMEM] * 4 + [ANY] * 4, out_specs=VMEM,
            scratch_shapes=[pltpu.VMEM((entries,) + one, dtype), pltpu.VMEM((entries,) + one, dtype),
                            pltpu.VMEM((entries,) + one, jnp.float32), DMA((2,))],
            compiler_params=pltpu.CompilerParams(vmem_limit_bytes=BIG),
        )(left_at, found1[inner_mine], square_slot, kept, flat(lefts), left_mine, flat(got1), flat(send1))
        later_at = demand(later, rank_later, rest, held_at)
        send2 = gather(later_at.reshape(-1), *parts, got_late, outgoing).reshape((n_row, rest) + one)
        got2, every = pl.pallas_call(
            functools.partial(last_kernel, n_row, nz),
            out_shape=(jax.ShapeDtypeStruct((n_row, rest) + one, dtype),
                       jax.ShapeDtypeStruct((n_col, entries) + one, dtype)),
            in_specs=[ANY, ANY], out_specs=(ANY, ANY),
            scratch_shapes=[DMA((n_row,)), DMA((n_row,))] + [DMA((nz,))] * 6,
            compiler_params=remote_params(number + 3),
        )(send2, filtered)
        found2 = jnp.where(
            now_all[r], found1,
            2 * n_row * cap1 + line * rest + rank_later[r] + jnp.where(line == r, n_row * rest, 0))
        place3 = ws[:, :, None] * n_col + gs[:, :, None]
        groups = jnp.arange(n_col, dtype=i32)[None, None, :]
        left_at = jnp.where(groups == c, n_col * entries + place3, groups * entries + place3).reshape(-1)
        count = windows * n_col * n_col
        return pl.pallas_call(
            cubed_kernel,
            out_shape=jax.ShapeDtypeStruct((windows * block, gcols * block), dtype),
            in_specs=[SMEM] * 4 + [ANY] * 6, out_specs=VMEM,
            scratch_shapes=[pltpu.VMEM((count,) + one, dtype), pltpu.VMEM((count,) + one, dtype),
                            pltpu.VMEM((entries,) + one, dtype),
                            pltpu.VMEM((windows, gcols) + one, jnp.float32), DMA((3,))],
            compiler_params=pltpu.CompilerParams(vmem_limit_bytes=BIG),
        )(left_at, found2[targets_mine], cubed_target, square_target.reshape(-1), flat(every), filtered,
          flat(got1), flat(send1), flat(got2), flat(send2))

    most_demand = windows * n_col * n_col
    early, most, limit = 7 * pool // 32, 10 * entries // 16, most_demand // 8
    small = (early, 22 * most_demand // 128)
    middle = (26 * pool // 64, most_demand // 4)
    share = shares(early, limit)
    most_pool, most_urgent = (wanted > 0).sum(axis=1).max(), urgent_count.max()
    first_out = pooled(0, early)
    parts = [lax.dynamic_index_in_dim(first_out, z, 0, keepdims=False)]
    for by in range(1, nz):
        moved = lax.dynamic_index_in_dim(first_out, (z + by) % nz, 0, keepdims=False)
        parts.append(lax.ppermute(moved, "col", [(i, (i + 2 * by) % n_col) for i in range(n_col)]))
    late_out = pooled(early, middle[0])
    opened = opening(early, most, limit, share, parts)

    def usual(caps, number):
        return run(early, caps[0], caps[1], share, parts, opened, late_out, number)

    def widest(number):
        every_share = shares(pool, limit)
        outgoing = pooled(0, pool)
        got = pl.pallas_call(
            functools.partial(first_kernel, nz, pool),
            out_shape=jax.ShapeDtypeStruct((nz, pool) + one, dtype),
            in_specs=[ANY], out_specs=ANY,
            scratch_shapes=[DMA((nz,)), DMA((nz,))],
            compiler_params=remote_params(number),
        )(outgoing)
        held = [lax.dynamic_index_in_dim(outgoing, z, 0, keepdims=False)]
        held += [lax.dynamic_index_in_dim(got, (z - by + nz) % nz, 0, keepdims=False) for by in range(1, nz)]
        return run(pool, 1, min(most_demand, nb, n_col * slots), every_share, held,
                   opening(pool, entries, limit, every_share, held), outgoing, number)

    def fits(caps):
        return ((most_pool <= early + caps[0]) & (most_urgent <= early)
                & (most_inner <= most) & (share[-1] <= caps[1]))

    choice = jnp.where(fits(small), 0, jnp.where(fits(middle), 1, 2))
    return lax.switch(choice, [lambda: usual(small, 1), lambda: usual(middle, 5), lambda: widest(9)])


F32, BF16, I32 = jnp.float32, jnp.bfloat16, jnp.int32
LANES = 128
SHIFTED = 5
META = 16
ROWS = 40
STAGE = (0, 32, 64, 128)


def log2(n):
    return n.bit_length() - 1


def iota(shape, dim):
    return lax.broadcasted_iota(I32, shape, dim)


def ones(mask):
    return jnp.where(mask, 1.0, 0.0).astype(F32)


def times(a, b):
    return lax.dot_general(a.astype(BF16), b.astype(BF16), (((1,), (0,)), ((), ())), preferred_element_type=F32)


def against(a, b):
    return lax.dot_general(a.astype(BF16), b.astype(BF16), (((1,), (1,)), ((), ())), preferred_element_type=F32)


def most(column):
    return jnp.max(column, axis=0, keepdims=True)


def plan(spread, keep, r, c, sizes, tiers):
    n_row, n_col, slots, windows, gcols, nb = sizes
    nz = n_col // 2
    z, k = c // 2, lax.rem(c, 2)
    devices = n_row * n_col
    total = devices * slots
    per_band = slots // n_row
    out = {}
    lane = iota((1, total), 1)
    label = spread[n_col:n_col + 1, :].astype(I32)
    band = (lane >> log2(per_band)) & (n_row - 1)
    row_id = gcols * (band + n_row * (label >> log2(gcols))) + (label & (gcols - 1))
    row_id = jnp.where(label < 2 * gcols, row_id, nb)
    holds = ones(iota((nb, total), 0) == row_id)
    sub = iota((META, total), 0)
    device = ((lane >> log2(slots)) & (n_row - 1)) * n_col + (lane >> log2(slots * n_row))
    fields = jnp.where(sub == n_col, device >> log2(n_col), 0)
    fields = jnp.where(sub == n_col + 1, (device & (n_col - 1)) >> 1, fields)
    fields = jnp.where(sub == n_col + 2, device & 1, fields)
    fields = jnp.where(sub == n_col + 3, lane & (slots - 1), fields)
    info = against(jnp.where(sub < n_col, spread, fields.astype(F32)), holds)
    line, plane, core, slot = [info[n_col + i:n_col + i + 1, :] for i in range(4)]
    column = jnp.zeros((1, nb), F32)
    for g in range(n_col):
        column = jnp.where(c == g, info[g:g + 1, :], column)
    within = iota((gcols, nb), 0).astype(F32)
    graph = jnp.concatenate([ones(info[g:g + 1, :] == within) for g in range(n_col)], axis=0).astype(BF16)
    upper = ones(iota((nb, nb), 0) < iota((nb, nb), 1)).astype(BF16)

    sub, row = iota((META, nb), 0), iota((META, nb), 1)
    wsel = ones((sub < n_row * windows) & (row == gcols * (sub >> log2(windows)) + (sub & (windows - 1))))
    once = against(wsel, graph)
    twice = against(once, graph)
    each = iota((1, nb), 1)
    soon, late = [], []
    for q in range(n_row):
        inner = sum(once[windows * q + i:windows * q + i + 1, :] for i in range(windows))
        target = sum(twice[windows * q + i:windows * q + i + 1, :] for i in range(windows))
        is_window = ((each >> log2(gcols)) == q) & ((each & (gcols - 1)) < windows)
        s = jnp.where(is_window, 1.0, ones(inner > 0.5))
        soon.append(s)
        late.append(ones(target > 0.5) * (1.0 - s))
    urgent = ones(sum(soon) > 0.5)
    need = ones(sum(soon) + sum(late) > 0.5)

    chip = (line * nz + plane).astype(I32)
    on_chip = ones(sub == chip)
    soon_mask, late_mask = on_chip * urgent, on_chip * (need - urgent)
    soon_count = jnp.sum(soon_mask, axis=1, keepdims=True)
    late_count = jnp.sum(late_mask, axis=1, keepdims=True)
    most_soon = most(soon_count)
    first = jnp.full((1, 1), float(tiers[-1]["n"][0]), F32)
    for tier in reversed(tiers):
        first = jnp.where(most_soon <= float(tier["n"][0]), float(tier["n"][0]), first)

    chips = (META, META)
    left, right = iota(chips, 0), iota(chips, 1)
    load = jnp.broadcast_to(soon_count + late_count, (META, LANES))
    level = times(ones((left & (nz - 1)) == (right & (nz - 1))), load)
    level = most(jnp.floor((level + (n_row - 1.0)) * (1.0 / n_row)))
    taken = jnp.zeros_like(load)
    moves = []
    for d in range(1, n_row):
        spare = jnp.maximum(jnp.minimum(level - load, level - first - taken), 0.0)
        reach = ones(right == ((((left >> log2(nz)) + d) & (n_row - 1)) << log2(nz)) + (left & (nz - 1)))
        back = ones(right == ((((left >> log2(nz)) + n_row - d) & (n_row - 1)) << log2(nz)) + (left & (nz - 1)))
        move = jnp.minimum(jnp.minimum(jnp.maximum(load - level, 0.0), float(SHIFTED)), times(reach, spare))
        arrived = times(back, move)
        load, taken = load - move + arrived, taken + arrived
        moves.append(move[:, 0:1])
    taken = taken[:, 0:1]
    stay = late_count - sum(moves)
    kept = soon_count + stay
    most_pool = most(jnp.where(taken > 0.5, jnp.maximum(kept, first) + taken, kept))
    late_rank = jnp.sum(on_chip * times(late_mask, upper), axis=0, keepdims=True)
    below = jnp.sum(on_chip * stay, axis=0, keepdims=True)
    is_late = need - urgent
    moved, entry, carrier = jnp.zeros((1, nb), F32), jnp.zeros((1, nb), F32), line
    for d in range(1, n_row):
        above = below + jnp.sum(on_chip * moves[d - 1], axis=0, keepdims=True)
        hit = is_late * ones((late_rank >= below) & (late_rank < above))
        moved = moved + hit
        entry = entry + hit * ((d - 1) * SHIFTED + late_rank - below)
        carrier = carrier + hit * d
        below = above
    carrier = jnp.where(carrier >= n_row, carrier - n_row, carrier)
    home = chip
    chip = (carrier * nz + plane).astype(I32)
    on_chip_now = ones(sub == chip)
    rank = jnp.where(urgent > 0.5, times(soon_mask, upper), soon_count + times(late_mask, upper))
    came = jnp.maximum(kept, first) + times(on_chip_now * moved, upper)
    spot = jnp.where(moved > 0.5, jnp.sum(on_chip_now * came, axis=0, keepdims=True),
                     jnp.sum(on_chip * rank, axis=0, keepdims=True))
    spot = jnp.where(need > 0.5, spot, 999.0)
    line = carrier
    m1 = tiers[0]["m"][1]

    sender, getter = sub >> log2(n_row), sub & (n_row - 1)
    soon_pair, late_pair = jnp.zeros((META, nb), F32), jnp.zeros((META, nb), F32)
    for q in range(n_row):
        soon_pair = jnp.where(getter == q, soon[q], soon_pair)
        late_pair = jnp.where(getter == q, late[q], late_pair)
    from_line = ones((sender == line.astype(I32)) & (sender != getter))
    soon_pair, late_pair = soon_pair * from_line, late_pair * from_line
    soon_sum = jnp.sum(soon_pair, axis=1, keepdims=True)
    at0 = times(soon_pair, upper)
    can = late_pair * ones(spot < first)
    at1 = times(can, upper)
    in1 = can * ones(at1 < float(m1))
    rest = late_pair * (1.0 - in1)
    at2 = times(rest, upper)
    most_line, most_rest = most(soon_sum), most(jnp.sum(rest, axis=1, keepdims=True))
    key = jnp.where(rest > 0.5, STAGE[2] + at2, -1.0)
    key = jnp.where(in1 > 0.5, STAGE[1] + at1, key)
    key = jnp.where(soon_pair > 0.5, at0, key)

    choice = jnp.full((1, 1), len(tiers), I32)
    for t in reversed(range(len(tiers))):
        n, m = tiers[t]["n"], tiers[t]["m"]
        fits = ((first == float(n[0])) & (most_soon <= float(n[0])) & (most_pool <= float(sum(n)))
                & (most_line <= float(m[0])) & (most_rest <= float(m[2])))
        choice = jnp.where(fits, t, choice)
    out[33] = jnp.broadcast_to(choice, (1, LANES))

    wide = iota((LANES, nb), 0)
    col = iota((LANES, nb), 1)
    step = z.astype(F32) - plane
    step = jnp.where(step < 0, step + nz, step)
    mine = ones(chip == (r * nz + z))
    pack = ones(wide.astype(F32) == jnp.where(mine > 0.5, spot, 999.0))
    from_slot = slot + slots * ones(core != k.astype(F32))
    given = jnp.where((moved > 0.5) & (home == (r * nz + z)), entry, -1.0)
    slot_rows = jnp.where(sub == 0, from_slot, 0.0)
    out[34] = against(slot_rows, ones(wide.astype(F32) == given))[0:1, :].astype(I32)
    from_slot = jnp.where(moved > 0.5, 2.0 * slots + entry, from_slot)
    rows = jnp.where(sub == 0, from_slot, jnp.where(sub == 1, step, jnp.where(sub == 2, spot, 0.0)))
    rows = jnp.minimum(rows, 127.0)
    out[0] = against(rows, pack)[0:1, :].astype(I32)
    for d in range(1, n_row):
        pair = r * n_row + lax.rem(r + d, n_row)
        key_of = jnp.sum(jnp.where(sub == pair, key, 0.0), axis=0, keepdims=True)
        got = against(rows, ones(wide.astype(F32) == key_of))
        out[d] = (64.0 * got[1:2, :] + got[2:3, :]).astype(I32)

    key_in = jnp.sum(jnp.where((sender == line.astype(I32)) & (getter == r), key, 0.0), axis=0, keepdims=True)
    away = r.astype(F32) - line
    away = jnp.where(away < 0, away + n_row, away)
    where_a = jnp.where(away == 0, step, nz - 1 + away)
    where_b = jnp.clip(jnp.where(away == 0, spot, key_in), 0.0, 127.0)
    fields = jnp.where(sub == 0, where_a, jnp.where(sub == 1, where_b, jnp.where(sub == 2, column, 0.0)))

    def location(found):
        return (128.0 * found[0:1, :] + found[1:2, :]).astype(I32)

    start = gcols * r
    group = col >> log2(gcols)
    out[32] = location(against(fields, ones((wide < windows) & (col == start + wide))))
    entries, count = windows * n_col, windows * n_col * n_col
    inner = against(ones(col == start + (wide >> log2(n_col))), graph)
    inner = inner * ones((group == (wide & (n_col - 1))) & (wide < entries))
    found = against(fields, inner)
    out[15] = location(found)
    lane_at = found[2:3, :]
    sub_at = jnp.sum(inner * column, axis=1, keepdims=True)
    here, there = iota((LANES, LANES), 0), iota((LANES, LANES), 1)
    same = ones((sub_at == lane_at) & ((here >> log2(n_col)) == (there >> log2(n_col)))
                & (here < entries) & (there < entries))
    leads = ones(jnp.sum(same * ones(there < here), axis=1, keepdims=True) < 0.5) * ones(here[:, 0:1] < entries)
    keeps = jnp.zeros((LANES, gcols), F32)
    tag = iota((LANES, gcols), 0) >> log2(n_col)
    for i in range(windows):
        keeps = jnp.where(tag == i, keep[i:i + 1, :].astype(F32), keeps)
    kept = jnp.sum(keeps * ones(iota((LANES, gcols), 1).astype(F32) == sub_at), axis=1, keepdims=True)
    out[16] = (same * leads * kept)[0:entries, :].astype(I32)
    place = gcols * (here[:, 0:1] >> log2(n_col)).astype(F32) + sub_at
    at = ones(place == there.astype(F32)) * leads
    out[13] = jnp.sum(at * here.astype(F32), axis=0, keepdims=True).astype(I32)
    out[14] = jnp.sum(at, axis=0, keepdims=True).astype(I32)

    inner = against(ones(col == start + (wide >> log2(n_col * n_col))), graph)
    inner = inner * ones(group == ((wide >> log2(n_col)) & (n_col - 1)))
    target = against(inner, graph) * ones(group == (wide & (n_col - 1)))
    found = against(fields, target)
    sub_at = gcols * (here[:, 0:1] >> log2(n_col * n_col)).astype(F32) + jnp.sum(target * column, axis=1, keepdims=True)
    lane_at = gcols * (there[0:1, :] >> log2(n_col * n_col)).astype(F32) + found[2:3, :]
    ahead = ones(sub_at == lane_at) * ones(there < here)
    order = jnp.sum(ones(lane_at < sub_at) + ahead, axis=1, keepdims=True)
    put = ones(order == there.astype(F32))
    narrow = iota((META, LANES), 0)
    got = times(jnp.where(narrow == 3, iota((META, LANES), 1).astype(F32), found), put)
    out[8] = location(got)
    out[9] = got[3:4, :].astype(I32)
    follows = ones(jnp.sum(ahead, axis=1, keepdims=True) > 0.5)
    out[10] = jnp.sum(put * follows, axis=0, keepdims=True).astype(I32)
    out[11] = (jnp.sum(ones(sub_at <= there.astype(F32)), axis=0, keepdims=True) - 1.0).astype(I32)
    out[12] = jnp.minimum(jnp.sum(ones(sub_at == there.astype(F32)), axis=0, keepdims=True), 1.0).astype(I32)
    return out


def plan_kernel(sizes, tiers, labels, cols, keep, owned, index, sibling, tile, line_tiles, group, tiles, send, recv,
                col_send, col_recv, pair_send, pair_recv):
    n_row, n_col, slots = sizes[:3]
    r, c = lax.axis_index("row"), lax.axis_index("col")
    z, k = c // 2, lax.rem(c, 2)
    mate = (r, 2 * z + 1 - k)
    lines = [(lax.rem(r + step, n_row), c) for step in range(1, n_row)]
    others = [(r, lax.rem(c + step, n_col)) for step in range(1, n_col)]
    barrier = pltpu.get_barrier_semaphore()
    for to in lines + others:
        pl.semaphore_signal(barrier, inc=1, device_id=to, device_id_type=MESH)
    rows = jnp.concatenate([cols[...].astype(F32), jnp.zeros((META - n_col, slots), F32)], axis=0)
    rows = jnp.where(iota((META, slots), 0) == n_col, labels[...].astype(F32), rows)
    tile[...] = times(rows, ones(iota((slots, LANES), 0) + slots * r == iota((slots, LANES), 1))).astype(BF16)
    pl.semaphore_wait(barrier, n_row + n_col - 2)
    copies = [send_to(tile, line_tiles.at[r], (send, recv), step, to) for step, to in enumerate(lines)]
    for copy in copies:
        copy.start()
    line_tiles[r] = tile[...]
    for copy in copies:
        copy.wait()
    group[...] = sum(line_tiles[q].astype(F32) for q in range(n_row)).astype(BF16)
    copies = [send_to(group, tiles.at[c], (col_send, col_recv), step, to) for step, to in enumerate(others)]
    for copy in copies:
        copy.start()
    pair = pltpu.make_async_remote_copy(
        src_ref=owned.at[:, :, 1 - k], dst_ref=sibling, send_sem=pair_send, recv_sem=pair_recv, device_id=mate,
        device_id_type=MESH)
    pair.start()
    tiles[c] = group[...]
    for copy in copies:
        copy.wait()
    spread = jnp.concatenate([tiles[q].astype(F32) for q in range(n_col)], axis=1)
    index[...] = jnp.zeros_like(index)
    for row, value in plan(spread, keep[...], r, c, sizes, tiers).items():
        index[row:row + value.shape[0], :] = value
    pair.wait()


def copy_kernel(source, out, sem):
    copy = pltpu.make_async_copy(source, out, sem)
    copy.start()
    copy.wait()


def main_kernel(sizes, tier, index, owned, sibling, out, pool, bsend, brecv, zsend0, zsend1, zall0, zall1,
                xsend0, xsend1, xsend2, xrecv0, xrecv1, xrecv2, lefts, parts, every, rights, sums, sems, zs, zr, xs, xr,
                ls, lr, us, ur, ds, dr, ps, pr, bs, br):
    n_row, n_col, slots, windows, gcols, nb = sizes
    nz = n_col // 2
    entries, count = windows * n_col, windows * n_col * n_col
    block = out.shape[0] // windows
    r, c = lax.axis_index("row"), lax.axis_index("col")
    z, k = c // 2, lax.rem(c, 2)
    zsend, zall = (zsend0, zsend1), (zall0, zall1)
    xsend, xrecv = (xsend0, xsend1, xsend2), (xrecv0, xrecv1, xrecv2)
    n, m = tier["n"], tier["m"]
    bounds = [0, n[0], n[0] + n[1]]
    others = [(r, 2 * lax.rem(z + step, nz) + k) for step in range(1, nz)]
    lines = [(lax.rem(r + step, n_row), c) for step in range(1, n_row)]
    mate = (r, 2 * z + 1 - k)
    above, below = others[0], others[-1]
    loads = [pltpu.make_async_copy(owned.at[:, :, k], pool.at[pl.ds(0, slots)], sems.at[0]),
             pltpu.make_async_copy(sibling, pool.at[pl.ds(slots, slots)], sems.at[1])]
    for load in loads:
        load.start()
    greet(others + lines + [mate])
    for load in loads:
        load.wait()

    def bpack():
        for i in range((n_row - 1) * SHIFTED):
            slot = index[34, i]
            for other in range(nz):
                bsend[i * nz + other] = pool[slot, other]

    def bcopies():
        size = SHIFTED * nz
        return [pltpu.make_async_remote_copy(
            src_ref=bsend.at[pl.ds((d - 1) * size, size)], dst_ref=brecv.at[pl.ds((d - 1) * size, size)],
            send_sem=bs.at[d], recv_sem=br.at[d], device_id=lines[d - 1], device_id_type=MESH)
            for d in range(1, n_row)]

    def zpack(s):
        def body(p, carry):
            slot = index[0, bounds[s] + p]
            own = slot < 2 * slots
            for step in range(nz):
                to = lax.rem(z + step, nz)
                if s == 0:
                    value = pool[slot, to]
                else:
                    value = lax.select(own, pool[jnp.where(own, slot, 0), to],
                                       brecv[jnp.where(own, 0, slot - 2 * slots) * nz + to])
                if step == 0:
                    zall[s][p] = value
                else:
                    zsend[s][(step - 1) * n[s] + p] = value
            return carry

        lax.fori_loop(0, n[s], body, 0)

    def zcopies(s):
        return [pltpu.make_async_remote_copy(
            src_ref=zsend[s].at[pl.ds((step - 1) * n[s], n[s])], dst_ref=zall[s].at[pl.ds(step * n[s], n[s])],
            send_sem=zs.at[s * nz + step], recv_sem=zr.at[s * nz + step], device_id=others[step - 1],
            device_id_type=MESH) for step in range(1, nz)]

    def from_z(step, spot, upto, value):
        for s in upto:
            inside = (step >= 0) & (spot >= bounds[s]) & (spot < bounds[s + 1])
            got = zall[s][jnp.where(inside, step * n[s] + spot - bounds[s], 0)]
            value = got if value is None else lax.select(inside, got, value)
        return value

    def from_x(away, key, upto, value):
        for s in upto:
            inside = (away >= 0) & (key >= STAGE[s]) & (key < STAGE[s] + m[s])
            got = xrecv[s][jnp.where(inside, away * m[s] + key - STAGE[s], 0)]
            value = lax.select(inside, got, value)
        return value

    def fetch(code, zupto, xupto, value=None):
        a, b = code // 128, lax.rem(code, 128)
        value = from_z(jnp.where(a < nz, a, -1), b, zupto, value)
        return from_x(jnp.where(a < nz, -1, a - nz), b, xupto, value)

    def xpack(s):
        ready = [0, 1] if s == 2 else [0]

        for d in range(1, n_row):
            def body(q, carry):
                code = index[d, STAGE[s] + q]
                xsend[s][(d - 1) * m[s] + q] = from_z(code // 64, lax.rem(code, 64), ready, None)
                return carry

            lax.fori_loop(0, m[s], body, 0)

    def xcopies(s):
        return [pltpu.make_async_remote_copy(
            src_ref=xsend[s].at[pl.ds((d - 1) * m[s], m[s])], dst_ref=xrecv[s].at[pl.ds((d - 1) * m[s], m[s])],
            send_sem=xs.at[s * n_row + d], recv_sem=xr.at[s * n_row + d], device_id=lines[d - 1],
            device_id_type=MESH) for d in range(1, n_row)]

    def start(copies):
        for copy in copies:
            copy.start()

    def arrive(copies):
        for copy in copies:
            copy.wait_recv()

    def left_send(sem, source, to):
        slab = lefts.at[source]
        return pltpu.make_async_remote_copy(
            src_ref=slab, dst_ref=slab, send_sem=ls.at[sem], recv_sem=lr.at[sem], device_id=to, device_id_type=MESH)

    zpack(0)
    start(zcopies(0))
    bpack()
    start(bcopies())
    arrive(bcopies())
    zpack(1)
    arrive(zcopies(0))
    start(zcopies(1))
    xpack(0)
    start(xcopies(0))
    xpack(1)
    arrive(xcopies(0))
    for i in range(windows):
        lefts[c, i] = fetch(index[32, i], [0], [0])
    left_out = [left_send(step, c, to) for step, to in enumerate(others)]
    left_pair = [left_send(nz, c, mate)]
    start(left_out)
    start(left_pair)
    start(xcopies(1))
    for step in range(1, nz):
        left_out[step - 1].wait_recv()
        left_pair.append(left_send(nz + step, 2 * lax.rem(z - step + nz, nz) + k, mate))
        left_pair[-1].start()
    arrive(left_pair)

    def square(e, carry):
        right = fetch(index[15, e], [0], [0])
        left = lefts[lax.rem(e, n_col), e // n_col]
        parts[e] = jnp.dot(left, right, preferred_element_type=F32)
        return carry

    def merge(e, carry):
        start_at = e // n_col * n_col
        total = parts[start_at] * index[16 + e, start_at].astype(F32)
        for i in range(1, n_col):
            total += parts[start_at + i] * index[16 + e, start_at + i].astype(F32)
        every[c, e] = total.astype(BF16)
        return carry

    def pass_on(sem, half, step, place, to):
        slab = every.at[place, pl.ds(half * n_col, n_col)]
        return pltpu.make_async_remote_copy(
            src_ref=slab, dst_ref=slab, send_sem=sem[0].at[half * nz + step], recv_sem=sem[1].at[half * nz + step],
            device_id=to, device_id_type=MESH)

    def up(half, step):
        return pass_on((us, ur), half, step, 2 * lax.rem(z - step + nz, nz) + k, above)

    def down(half, step):
        return pass_on((ds, dr), half, step, 2 * lax.rem(z + step, nz) + k, below)

    def across(half, step):
        return pass_on((ps, pr), half, step, 2 * lax.rem(z + step, nz) + k, mate)

    def relay(half, step):
        @pl.when(z - step >= 0)
        def _():
            up(half, step - 1).wait_recv()

        @pl.when((z - step >= 0) & (z < nz - 1))
        def _():
            up(half, step).start()

        @pl.when(z - step >= 0)
        def _():
            across(half, nz - step).start()

        @pl.when(z + step <= nz - 1)
        def _():
            down(half, step - 1).wait_recv()

        @pl.when((z + step <= nz - 1) & (z > 0))
        def _():
            down(half, step).start()

        @pl.when(z + step <= nz - 1)
        def _():
            across(half, step).start()

    def first_pass(half):
        @pl.when(z < nz - 1)
        def _():
            up(half, 0).start()

        @pl.when(z > 0)
        def _():
            down(half, 0).start()

        across(half, 0).start()

    for w in range(windows):
        lax.fori_loop(w * n_col, (w + 1) * n_col, square, 0)
        lax.fori_loop(w * n_col, (w + 1) * n_col, merge, 0)
        first_pass(w)
    arrive(zcopies(1))
    xpack(2)
    start(xcopies(2))
    arrive(xcopies(1))

    def gather_early(t, carry):
        rights[t] = fetch(index[8, t], [0, 1], [0, 1])
        return carry

    lax.fori_loop(0, count, gather_early, 0)
    for step in range(1, nz):
        for w in range(windows):
            relay(w, step)
    for step in range(nz):
        for w in range(windows):
            across(w, step).wait_recv()
    arrive(xcopies(2))

    def multiply(q, acc):
        for i in range(4):
            t = q * 4 + i
            p = index[9, t]
            right = fetch(index[8, t], [], [2], rights[t])
            term = jnp.dot(every[lax.rem(p, n_col), p // n_col], right, preferred_element_type=F32)
            acc = acc * index[10, t].astype(F32) + term
            sums[t] = acc
        return acc

    lax.fori_loop(0, count // 4, multiply, jnp.zeros((block, block), F32))
    for w in range(windows):
        def write(j, carry):
            at = w * gcols + j
            cube = sums[jnp.maximum(index[11, at], 0)] * (-2.0 * index[12, at].astype(F32))
            own = every[c, index[13, at]].astype(F32) * (3.0 * index[14, at].astype(F32))
            out[w * block:(w + 1) * block, pl.ds(pl.multiple_of(j * block, block), block)] = (own + cube).astype(BF16)
            return carry

        lax.fori_loop(0, gcols, write, 0)

    for copies in (bcopies(), zcopies(0), zcopies(1), xcopies(0), xcopies(1), xcopies(2), left_out, left_pair):
        for copy in copies:
            copy.wait_send()
    for w in range(windows):
        for step in range(nz):
            @pl.when((z - step >= 0) & (z < nz - 1))
            def _(w=w, step=step):
                up(w, step).wait_send()

            @pl.when((z + step <= nz - 1) & (z > 0))
            def _(w=w, step=step):
                down(w, step).wait_send()

            across(w, step).wait_send()


TIERS = (dict(n=(9, 10), m=(9, 14, 18)), dict(n=(9, 18), m=(11, 14, 26)), dict(n=(11, 8), m=(11, 14, 18)),
         dict(n=(11, 16), m=(11, 14, 26)), dict(n=(14, 22), m=(14, 14, 30)))


def local(owned_blocks, owned_rows, owned_cols, keep):
    n_row, n_col = lax.axis_size("row"), lax.axis_size("col")
    nz = n_col // 2
    slots = owned_rows.shape[0]
    windows, gcols = keep.shape
    nb = gcols * n_col
    block = owned_blocks.shape[-1]
    one = (block, block)
    dtype = owned_blocks.dtype
    entries, count = windows * n_col, windows * n_col * n_col
    if (count > LANES or n_col > 8 or n_row > 4 or entries > 16 or nz > 4 or n_row * slots != LANES or 2 * slots > 64
            or windows * gcols > LANES or n_row < 2 or nz < 2):
        return general(owned_blocks, owned_rows, owned_cols, keep)
    sizes = (n_row, n_col, slots, windows, gcols, nb)
    halves = owned_blocks.reshape((slots, nz, 2) + one)
    index, sibling = pl.pallas_call(
        functools.partial(plan_kernel, sizes, TIERS),
        out_shape=(jax.ShapeDtypeStruct((ROWS, LANES), I32), jax.ShapeDtypeStruct((slots, nz) + one, dtype)),
        in_specs=[VMEM, VMEM, VMEM, ANY], out_specs=(VMEM, ANY),
        scratch_shapes=[pltpu.VMEM((META, LANES), BF16), pltpu.VMEM((n_row, META, LANES), BF16),
                        pltpu.VMEM((META, LANES), BF16), pltpu.VMEM((n_col, META, LANES), BF16),
                        DMA((n_row,)), DMA((n_row,)), DMA((n_col,)), DMA((n_col,)), DMA, DMA],
        compiler_params=pltpu.CompilerParams(collective_id=20, has_side_effects=True, vmem_limit_bytes=BIG),
    )(owned_rows[None, :], owned_cols.T, keep, halves)

    def quick(t):
        n, m = TIERS[t]["n"], TIERS[t]["m"]
        scratch = [pltpu.VMEM((2 * slots, nz) + one, dtype)]
        scratch += [pltpu.VMEM(((n_row - 1) * SHIFTED * nz,) + one, dtype)] * 2
        scratch += [pltpu.VMEM(((nz - 1) * q,) + one, dtype) for q in n]
        scratch += [pltpu.VMEM((nz * q,) + one, dtype) for q in n]
        scratch += [pltpu.VMEM(((n_row - 1) * q,) + one, dtype) for q in m] * 2
        scratch += [pltpu.VMEM((n_col, windows) + one, dtype), pltpu.VMEM((entries,) + one, F32),
                    pltpu.VMEM((n_col, entries) + one, dtype), pltpu.VMEM((count,) + one, dtype),
                    pltpu.VMEM((count,) + one, F32), DMA((2,))]
        scratch += [DMA((2 * nz,))] * 2 + [DMA((3 * n_row,))] * 2 + [DMA((2 * nz,))] * 2
        scratch += [DMA((windows * nz,))] * 6 + [DMA((n_row,))] * 2
        made = pl.pallas_call(
            functools.partial(main_kernel, sizes, TIERS[t]),
            out_shape=jax.ShapeDtypeStruct((windows * block, gcols * block), dtype),
            in_specs=[SMEM, ANY, ANY], out_specs=VMEM, scratch_shapes=scratch,
            compiler_params=pltpu.CompilerParams(
                collective_id=21 + t, has_side_effects=True, vmem_limit_bytes=BIG),
        )(index, halves, sibling)
        return pl.pallas_call(
            copy_kernel, out_shape=jax.ShapeDtypeStruct(made.shape, dtype), in_specs=[ANY], out_specs=ANY,
            scratch_shapes=[DMA])(made)

    branches = [functools.partial(quick, t) for t in range(len(TIERS))]
    branches.append(lambda: general(owned_blocks, owned_rows, owned_cols, keep))
    return lax.switch(index[33, 0], branches)


def solution(mesh):
    placed = (
        P(("row", "col"), None, None, None),
        P(("row", "col")),
        P(("row", "col"), None),
        P("row", "col"),
    )
    return jax.shard_map(
        local, mesh=mesh, in_specs=placed, out_specs=P("row", "col"), check_vma=False
    )
```

```python
import functools

import jax
import jax.numpy as jnp
from jax import lax
from jax.experimental import pallas as pl
from jax.experimental.pallas import tpu as pltpu
from jax.sharding import PartitionSpec as P

MESH = pl.DeviceIdType.MESH
ANY = pl.BlockSpec(memory_space=pl.ANY)
SMEM = pl.BlockSpec(memory_space=pltpu.SMEM)
VMEM = pl.BlockSpec(memory_space=pltpu.VMEM)
DMA = pltpu.SemaphoreType.DMA
BIG = 60 * 1024 * 1024


def remote_params(number):
    return pltpu.CompilerParams(collective_id=number, has_side_effects=True)


def spread_kernel(n_row, n_col, meta, owned, meta_all, sibling, send, recv, pair_send, pair_recv):
    r, c = lax.axis_index("row"), lax.axis_index("col")
    me = r * n_col + c
    devices = n_row * n_col
    barrier = pltpu.get_barrier_semaphore()

    def greet(i, carry):
        d = lax.rem(me + i, devices)
        pl.semaphore_signal(barrier, inc=1, device_id=(d // n_col, lax.rem(d, n_col)), device_id_type=MESH)
        return carry

    lax.fori_loop(1, devices, greet, 0)
    pl.semaphore_wait(barrier, devices - 1)
    z, k = c // 2, lax.rem(c, 2)
    other = 1 - k
    pair = pltpu.make_async_remote_copy(
        src_ref=owned.at[:, :, other], dst_ref=sibling, send_sem=pair_send, recv_sem=pair_recv,
        device_id=(r, 2 * z + other), device_id_type=MESH)
    pair.start()

    def copy_to(i):
        d = lax.rem(me + i, devices)
        return pltpu.make_async_remote_copy(
            src_ref=meta, dst_ref=meta_all.at[me], send_sem=send.at[i], recv_sem=recv.at[i],
            device_id=(d // n_col, lax.rem(d, n_col)), device_id_type=MESH)

    def begin(i, carry):
        copy_to(i).start()
        return carry

    def finish(i, carry):
        copy_to(i).wait()
        return carry

    lax.fori_loop(1, devices, begin, 0)
    lax.fori_loop(1, devices, finish, 0)
    pair.wait()


def greet(partners):
    barrier = pltpu.get_barrier_semaphore()
    for partner in partners:
        pl.semaphore_signal(barrier, inc=1, device_id=partner, device_id_type=MESH)
    pl.semaphore_wait(barrier, len(partners))


def send_to(source, dest, sems, step, partner):
    return pltpu.make_async_remote_copy(
        src_ref=source, dst_ref=dest, send_sem=sems[0].at[step], recv_sem=sems[1].at[step],
        device_id=partner, device_id_type=MESH)


def place_of(nz):
    r, c = lax.axis_index("row"), lax.axis_index("col")
    z, k = c // 2, lax.rem(c, 2)
    return r, c, z, k, [(r, 2 * lax.rem(z + step, nz) + k) for step in range(1, nz)]


def first_kernel(nz, count, source, got, send, recv):
    r, c, z, k, others = place_of(nz)
    greet(others)
    copies = [send_to(source.at[to[1] // 2, pl.ds(0, count)], got.at[z], (send, recv), step, to)
              for step, to in enumerate(others)]
    for copy in copies:
        copy.start()
    for copy in copies:
        copy.wait()


def second_kernel(n_row, nz, source, wanted, got, plane_got, send, recv, psend, precv):
    r, c, z, k, others = place_of(nz)
    lines = [(lax.rem(r + step, n_row), c) for step in range(1, n_row)]
    greet(others + lines)
    count = got.shape[1]
    copies = [send_to(wanted.at[to[0]], plane_got.at[r], (psend, precv), step, to) for step, to in enumerate(lines)]
    copies += [send_to(source.at[to[1] // 2, pl.ds(0, count)], got.at[z], (send, recv), step, to)
               for step, to in enumerate(others)]
    for copy in copies:
        copy.start()
    for copy in copies:
        copy.wait()


def left_kernel(nz, piece, got, send, recv, psend, precv):
    r, c, z, k, others = place_of(nz)
    mate = (r, 2 * z + 1 - k)
    greet(others + [mate])
    copies = [send_to(piece, got.at[c], (send, recv), step, to) for step, to in enumerate(others)]
    for copy in copies:
        copy.start()
    pairs = [send_to(piece, got.at[c], (psend, precv), 0, mate)]
    pairs[0].start()
    for step in range(1, nz):
        copies[step - 1].wait_recv()
        origin = 2 * lax.rem(z - step + nz, nz) + k
        pairs.append(send_to(got.at[origin], got.at[origin], (psend, precv), step, mate))
        pairs[-1].start()
    for copy in copies:
        copy.wait_send()
    for pair in pairs:
        pair.wait()


def last_kernel(n_row, nz, wanted, filtered, plane_got, every, send, recv, up_send, up_recv, down_send, down_recv,
                psend, precv):
    r, c, z, k, others = place_of(nz)
    mate = (r, 2 * z + 1 - k)
    lines = [(lax.rem(r + step, n_row), c) for step in range(1, n_row)]
    above, below = (r, 2 * lax.rem(z + 1, nz) + k), (r, 2 * lax.rem(z + nz - 1, nz) + k)
    greet(lines + [above, below, mate])
    plane = [send_to(wanted.at[to[0]], plane_got.at[r], (send, recv), step, to) for step, to in enumerate(lines)]

    def up(step, own):
        block = every.at[2 * lax.rem(z - step + nz, nz) + k]
        return send_to(filtered if own else block, block, (up_send, up_recv), step, above)

    def down(step, own):
        block = every.at[2 * lax.rem(z + step, nz) + k]
        return send_to(filtered if own else block, block, (down_send, down_recv), step, below)

    def across(step, own):
        block = every.at[2 * lax.rem(z + step, nz) + k]
        return send_to(filtered if own else block, block, (psend, precv), step, mate)

    @pl.when(z < nz - 1)
    def _():
        up(0, True).start()

    @pl.when(z > 0)
    def _():
        down(0, True).start()

    across(0, True).start()
    for copy in plane:
        copy.start()
    for step in range(1, nz):
        @pl.when(z - step >= 0)
        def _():
            up(step - 1, False).wait_recv()
            across(nz - step, False).start()

        @pl.when((z - step >= 0) & (z < nz - 1))
        def _():
            up(step, False).start()

        @pl.when(z + step <= nz - 1)
        def _():
            down(step - 1, False).wait_recv()
            across(step, False).start()

        @pl.when((z + step <= nz - 1) & (z > 0))
        def _():
            down(step, False).start()
    for step in range(nz):
        @pl.when((z - step >= 0) & (z < nz - 1))
        def _():
            up(step, False).wait_send()

        @pl.when((z + step <= nz - 1) & (z > 0))
        def _():
            down(step, False).wait_send()
    for step in range(nz):
        across(step, False).wait()
    for copy in plane:
        copy.wait()


def pick(sources, index, dest, sem):
    start = 0
    for source in sources:
        stop = start + source.shape[0]

        @pl.when((index >= start) & (index < stop))
        def _(source=source, start=start):
            pltpu.make_async_copy(source.at[index - start], dest, sem).start()

        start = stop


def gather_kernel(index, *refs):
    sources, (out, sem) = refs[:-2], refs[-2:]
    start = pl.program_id(0) * out.shape[0]

    def begin(i, carry):
        pick(sources, index[start + i], out.at[i], sem)
        return carry

    lax.fori_loop(0, out.shape[0], begin, 0)
    pltpu.make_async_copy(out, out, sem).wait()


def flat(array):
    return array.reshape((-1,) + array.shape[-2:])


def gather(index, *sources):
    block = sources[0].shape[-2:]
    count = index.shape[0]
    chunk = max(n for n in range(1, min(count, 512) + 1) if count % n == 0)
    return pl.pallas_call(
        gather_kernel,
        grid=(count // chunk,),
        out_shape=jax.ShapeDtypeStruct((count,) + block, sources[0].dtype),
        in_specs=[SMEM] + [ANY] * len(sources), out_specs=pl.BlockSpec((chunk,) + block, lambda i: (i, 0, 0)),
        scratch_shapes=[DMA],
        compiler_params=pltpu.CompilerParams(vmem_limit_bytes=BIG),
    )(index, *[flat(source) for source in sources])


def square_kernel(left_at, right_at, slot, keep, lefts, own_left, rights, own_rights, out, a, b, acc, sems):
    count = out.shape[0]

    def begin(i, carry):
        pick((lefts, own_left), left_at[i], a.at[i], sems.at[0])
        pick((rights, own_rights), right_at[i], b.at[i], sems.at[1])
        return carry

    lax.fori_loop(0, count, begin, 0)
    acc[...] = jnp.zeros_like(acc)
    pltpu.make_async_copy(a, a, sems.at[0]).wait()
    pltpu.make_async_copy(b, b, sems.at[1]).wait()

    def multiply(q, carry):
        ids = [q * 4 + i for i in range(4)]
        terms = [jnp.dot(a[i], b[i], preferred_element_type=jnp.float32) for i in ids]
        for i, term in zip(ids, terms):
            acc[slot[i]] += term
        return carry

    lax.fori_loop(0, count // 4, multiply, 0)

    def write(i, carry):
        out[i] = (acc[i] * keep[i].astype(jnp.float32)).astype(out.dtype)
        return carry

    lax.fori_loop(0, count, write, 0)


def cubed_kernel(left_at, right_at, target, own_target, every, own, got1, send1, got2, send2, out, a, b, f, acc, sems):
    count = a.shape[0]
    windows = acc.shape[0]
    block = a.shape[-1]
    per_window = count // windows
    own_per_window = f.shape[0] // windows
    mine = pltpu.make_async_copy(own, f, sems.at[2])
    mine.start()

    def begin(i, carry):
        pick((every, own), left_at[i], a.at[i], sems.at[0])
        pick((got1, send1, got2, send2), right_at[i], b.at[i], sems.at[1])
        return carry

    lax.fori_loop(0, count, begin, 0)
    acc[...] = jnp.zeros_like(acc)
    mine.wait()
    for w in range(windows):
        def add(i, carry):
            e = w * own_per_window + i
            acc[w, own_target[e]] -= 1.5 * f[e].astype(jnp.float32)
            return carry

        lax.fori_loop(0, own_per_window, add, 0)
    pltpu.make_async_copy(a, a, sems.at[0]).wait()
    pltpu.make_async_copy(b, b, sems.at[1]).wait()
    for w in range(windows):
        def multiply(q, carry):
            ids = [w * per_window + q * 4 + i for i in range(4)]
            terms = [jnp.dot(a[i], b[i], preferred_element_type=jnp.float32) for i in ids]
            for i, term in zip(ids, terms):
                acc[w, target[i]] += term
            return carry

        lax.fori_loop(0, per_window // 4, multiply, 0)
    for w in range(windows):
        for j in range(acc.shape[1]):
            out[w * block:(w + 1) * block, j * block:(j + 1) * block] = (-2.0 * acc[w, j]).astype(out.dtype)


def running(mask):
    n = mask.shape[-1]
    before = (jnp.arange(n)[:, None] < jnp.arange(n)[None, :]).astype(jnp.bfloat16)
    lines = mask.reshape(-1, n).astype(jnp.bfloat16)
    return jnp.dot(lines, before, preferred_element_type=jnp.float32).astype(jnp.int32).reshape(mask.shape)


def general(owned_blocks, owned_rows, owned_cols, keep):
    n_row, n_col = lax.axis_size("row"), lax.axis_size("col")
    devices = n_row * n_col
    nz = n_col // 2
    r, c = lax.axis_index("row"), lax.axis_index("col")
    z, k = c // 2, lax.rem(c, 2)
    block = owned_blocks.shape[-1]
    dtype = owned_blocks.dtype
    slots = owned_rows.shape[0]
    per_band = slots // n_row
    windows, gcols = keep.shape
    nb = gcols * n_col
    size = slots * (1 + n_col)
    tall = -(-size // 1024) * 8
    one = (block, block)
    chips = devices // 2
    pool = 2 * slots
    i32 = jnp.int32

    packed = jnp.concatenate([owned_rows[:, None], owned_cols], axis=1).reshape(-1)
    meta = jnp.pad(packed, (0, tall * 128 - size)).reshape(tall, 128)
    meta_all, sibling = pl.pallas_call(
        functools.partial(spread_kernel, n_row, n_col),
        out_shape=(jax.ShapeDtypeStruct((devices, tall, 128), i32),
                   jax.ShapeDtypeStruct((slots, nz) + one, dtype)),
        in_specs=[ANY, ANY], out_specs=(ANY, ANY),
        scratch_shapes=[DMA((devices,)), DMA((devices,)), DMA, DMA],
        compiler_params=remote_params(0),
    )(meta, owned_blocks.reshape((slots, nz, 2) + one))
    me = r * n_col + c
    is_me = jnp.arange(devices)[:, None] == me
    labels = jnp.where(is_me, packed[None, :], meta_all.reshape(devices, -1)[:, :size])
    labels = labels.reshape(devices * slots, 1 + n_col)
    rows, cols = labels[:, 0], labels[:, 1:]
    slot_ids = jnp.arange(devices * slots, dtype=i32)
    every_row = jnp.arange(nb, dtype=i32)
    filled = rows < gcols * 2
    row_id = jnp.where(filled, gcols * (slot_ids // per_band % n_row + n_row * (rows // gcols)) + rows % gcols, nb)
    holder = jnp.sum(jnp.where(row_id[None, :] == every_row[:, None], slot_ids[None, :], 0), axis=1)
    row_cols = cols[holder]
    chip = holder // pool
    line, plane = chip // nz, chip % nz

    base = gcols * jnp.arange(n_col, dtype=i32)
    window = gcols * jnp.arange(n_row, dtype=i32)[:, None] + jnp.arange(windows, dtype=i32)[None, :]
    inner = base + row_cols[window]
    targets = base + row_cols[inner]
    is_window = jnp.any(window[:, :, None] == every_row, axis=1)
    is_inner = jnp.any(inner.reshape(n_row, -1, 1) == every_row, axis=1) & ~is_window
    is_target = jnp.any(targets.reshape(n_row, -1, 1) == every_row, axis=1) & ~is_inner & ~is_window
    urgent = jnp.any(is_window | is_inner, axis=0)
    wanted_row = urgent.astype(i32) + jnp.any(is_window | is_inner | is_target, axis=0).astype(i32)
    wanted = jnp.sum(jnp.where(row_id[:, None] == every_row[None, :], wanted_row[None, :], 0), axis=1).reshape(chips, pool)
    urgent_count = (wanted == 2).sum(axis=1)
    place = jnp.where(wanted == 2, running(wanted == 2), urgent_count[:, None] + running(wanted == 1))
    place = jnp.where(wanted > 0, place, pool)
    spot = place.reshape(-1)[holder]
    on_line = line[None, :] == jnp.arange(n_row, dtype=i32)[:, None]

    def ranks(need):
        both = need[:, None, :] & on_line[None, :, :]
        rank = jnp.sum(jnp.where(both, running(both), 0), axis=1)
        return rank, both.sum(axis=2).max()

    rank_window, _ = ranks(is_window)
    rank_inner, most_inner = ranks(is_inner)

    def shares(early, limit):
        now = is_target & (spot < early)[None, :]
        rank_now, _ = ranks(now)
        now = now & (rank_now < limit)
        later = is_target & ~now
        rank_later, most_later = ranks(later)
        return now, rank_now, later, rank_later, most_later

    inner_mine = inner[r].reshape(-1)
    targets_mine = targets[r].reshape(-1)
    cols_mine = lax.dynamic_index_in_dim(row_cols, c, 1, keepdims=False)
    square_target = cols_mine[inner_mine].reshape(windows, n_col)
    same = square_target[:, :, None] == square_target[:, None, :]
    first = jnp.argmax(same, axis=2).astype(i32)
    square_slot = (first + n_col * jnp.arange(windows, dtype=i32)[:, None]).reshape(-1)
    kept = jnp.take_along_axis(keep, square_target, axis=1).reshape(-1)
    cubed_target = cols_mine[targets_mine]
    entries = windows * n_col

    step = (z - plane + nz) % nz
    zs = jnp.arange(nz, dtype=i32)[:, None]
    place_mine = lax.dynamic_index_in_dim(place, r * nz + z, 0, keepdims=False)

    def pooled(start, count):
        position = start + jnp.arange(count, dtype=i32)
        pick_slot = jnp.sum(
            jnp.where(place_mine[None, :] == position[:, None], jnp.arange(pool, dtype=i32)[None, :], 0), axis=1)
        at = pick_slot[None, :] % slots
        index = jnp.where(
            pick_slot[None, :] // slots == k, at * n_col + 2 * zs + k, slots * n_col + at * nz + zs)
        return gather(index.reshape(-1), owned_blocks, sibling).reshape((nz, count) + one)

    def demand(need, rank, count, source_at):
        sending = need & (line == r)[None, :]
        chosen = sending[:, None, :] & (rank[:, None, :] == jnp.arange(count, dtype=i32)[None, :, None])
        return jnp.sum(jnp.where(chosen, source_at[None, None, :], 0), axis=2)

    def opening(early, most, limit, share, parts):
        now, rank_now = share[:2]
        cap1 = windows + most + limit
        now_all = is_window | is_inner | now
        now_rank = jnp.where(is_window, rank_window, jnp.where(is_inner, windows + rank_inner, windows + most + rank_now))
        send1 = gather(demand(now_all, now_rank, cap1, step * early + spot).reshape(-1), *parts)
        found1 = line * cap1 + now_rank[r] + jnp.where(line == r, n_row * cap1, 0)
        return now_all, found1, send1.reshape((n_row, cap1) + one)

    def run(early, late, rest, share, parts, opened, outgoing, number):
        later, rank_later = share[2:4]
        now_all, found1, send1 = opened
        cap1 = send1.shape[1]
        late_at = jnp.where(plane == z, nz * late + plane * outgoing.shape[1], plane * late)
        held_at = jnp.where(spot < early, step * early + spot, nz * early + late_at + spot - early)
        got_late, got1 = pl.pallas_call(
            functools.partial(second_kernel, n_row, nz),
            out_shape=(jax.ShapeDtypeStruct((nz, late) + one, dtype),
                       jax.ShapeDtypeStruct((n_row, cap1) + one, dtype)),
            in_specs=[ANY, ANY], out_specs=(ANY, ANY),
            scratch_shapes=[DMA((nz,)), DMA((nz,)), DMA((n_row,)), DMA((n_row,))],
            compiler_params=remote_params(number + 1),
        )(outgoing, send1)
        window_mine = gcols * r + jnp.arange(windows, dtype=i32)
        left_mine = gather(found1[window_mine], got1, send1)
        lefts = pl.pallas_call(
            functools.partial(left_kernel, nz),
            out_shape=jax.ShapeDtypeStruct((n_col, windows) + one, dtype),
            in_specs=[ANY], out_specs=ANY,
            scratch_shapes=[DMA((nz,))] * 4,
            compiler_params=remote_params(number + 2),
        )(left_mine)
        ws = jnp.arange(windows, dtype=i32)[:, None]
        gs = jnp.arange(n_col, dtype=i32)[None, :]
        left_at = jnp.where(gs == c, n_col * windows + ws, gs * windows + ws).reshape(-1)
        filtered = pl.pallas_call(
            square_kernel,
            out_shape=jax.ShapeDtypeStruct((entries,) + one, dtype),
            in_specs=[SMEM] * 4 + [ANY] * 4, out_specs=VMEM,
            scratch_shapes=[pltpu.VMEM((entries,) + one, dtype), pltpu.VMEM((entries,) + one, dtype),
                            pltpu.VMEM((entries,) + one, jnp.float32), DMA((2,))],
            compiler_params=pltpu.CompilerParams(vmem_limit_bytes=BIG),
        )(left_at, found1[inner_mine], square_slot, kept, flat(lefts), left_mine, flat(got1), flat(send1))
        later_at = demand(later, rank_later, rest, held_at)
        send2 = gather(later_at.reshape(-1), *parts, got_late, outgoing).reshape((n_row, rest) + one)
        got2, every = pl.pallas_call(
            functools.partial(last_kernel, n_row, nz),
            out_shape=(jax.ShapeDtypeStruct((n_row, rest) + one, dtype),
                       jax.ShapeDtypeStruct((n_col, entries) + one, dtype)),
            in_specs=[ANY, ANY], out_specs=(ANY, ANY),
            scratch_shapes=[DMA((n_row,)), DMA((n_row,))] + [DMA((nz,))] * 6,
            compiler_params=remote_params(number + 3),
        )(send2, filtered)
        found2 = jnp.where(
            now_all[r], found1,
            2 * n_row * cap1 + line * rest + rank_later[r] + jnp.where(line == r, n_row * rest, 0))
        place3 = ws[:, :, None] * n_col + gs[:, :, None]
        groups = jnp.arange(n_col, dtype=i32)[None, None, :]
        left_at = jnp.where(groups == c, n_col * entries + place3, groups * entries + place3).reshape(-1)
        count = windows * n_col * n_col
        return pl.pallas_call(
            cubed_kernel,
            out_shape=jax.ShapeDtypeStruct((windows * block, gcols * block), dtype),
            in_specs=[SMEM] * 4 + [ANY] * 6, out_specs=VMEM,
            scratch_shapes=[pltpu.VMEM((count,) + one, dtype), pltpu.VMEM((count,) + one, dtype),
                            pltpu.VMEM((entries,) + one, dtype),
                            pltpu.VMEM((windows, gcols) + one, jnp.float32), DMA((3,))],
            compiler_params=pltpu.CompilerParams(vmem_limit_bytes=BIG),
        )(left_at, found2[targets_mine], cubed_target, square_target.reshape(-1), flat(every), filtered,
          flat(got1), flat(send1), flat(got2), flat(send2))

    most_demand = windows * n_col * n_col
    early, most, limit = 7 * pool // 32, 10 * entries // 16, most_demand // 8
    small = (early, 22 * most_demand // 128)
    middle = (26 * pool // 64, most_demand // 4)
    share = shares(early, limit)
    most_pool, most_urgent = (wanted > 0).sum(axis=1).max(), urgent_count.max()
    first_out = pooled(0, early)
    parts = [lax.dynamic_index_in_dim(first_out, z, 0, keepdims=False)]
    for by in range(1, nz):
        moved = lax.dynamic_index_in_dim(first_out, (z + by) % nz, 0, keepdims=False)
        parts.append(lax.ppermute(moved, "col", [(i, (i + 2 * by) % n_col) for i in range(n_col)]))
    late_out = pooled(early, middle[0])
    opened = opening(early, most, limit, share, parts)

    def usual(caps, number):
        return run(early, caps[0], caps[1], share, parts, opened, late_out, number)

    def widest(number):
        every_share = shares(pool, limit)
        outgoing = pooled(0, pool)
        got = pl.pallas_call(
            functools.partial(first_kernel, nz, pool),
            out_shape=jax.ShapeDtypeStruct((nz, pool) + one, dtype),
            in_specs=[ANY], out_specs=ANY,
            scratch_shapes=[DMA((nz,)), DMA((nz,))],
            compiler_params=remote_params(number),
        )(outgoing)
        held = [lax.dynamic_index_in_dim(outgoing, z, 0, keepdims=False)]
        held += [lax.dynamic_index_in_dim(got, (z - by + nz) % nz, 0, keepdims=False) for by in range(1, nz)]
        return run(pool, 1, min(most_demand, nb, n_col * slots), every_share, held,
                   opening(pool, entries, limit, every_share, held), outgoing, number)

    def fits(caps):
        return ((most_pool <= early + caps[0]) & (most_urgent <= early)
                & (most_inner <= most) & (share[-1] <= caps[1]))

    choice = jnp.where(fits(small), 0, jnp.where(fits(middle), 1, 2))
    return lax.switch(choice, [lambda: usual(small, 1), lambda: usual(middle, 5), lambda: widest(9)])


F32, BF16, I32 = jnp.float32, jnp.bfloat16, jnp.int32
LANES = 128
SHIFTED = 5
META = 16
ROWS = 40
STAGE = (0, 32, 64, 128)


def log2(n):
    return n.bit_length() - 1


def iota(shape, dim):
    return lax.broadcasted_iota(I32, shape, dim)


def ones(mask):
    return jnp.where(mask, 1.0, 0.0).astype(F32)


def times(a, b):
    return lax.dot_general(a.astype(BF16), b.astype(BF16), (((1,), (0,)), ((), ())), preferred_element_type=F32)


def against(a, b):
    return lax.dot_general(a.astype(BF16), b.astype(BF16), (((1,), (1,)), ((), ())), preferred_element_type=F32)


def most(column):
    return jnp.max(column, axis=0, keepdims=True)


def plan(spread, keep, r, c, sizes, tiers):
    n_row, n_col, slots, windows, gcols, nb = sizes
    nz = n_col // 2
    z, k = c // 2, lax.rem(c, 2)
    devices = n_row * n_col
    total = devices * slots
    per_band = slots // n_row
    out = {}
    lane = iota((1, total), 1)
    label = spread[n_col:n_col + 1, :].astype(I32)
    band = (lane >> log2(per_band)) & (n_row - 1)
    row_id = gcols * (band + n_row * (label >> log2(gcols))) + (label & (gcols - 1))
    row_id = jnp.where(label < 2 * gcols, row_id, nb)
    holds = ones(iota((nb, total), 0) == row_id)
    sub = iota((META, total), 0)
    device = ((lane >> log2(slots)) & (n_row - 1)) * n_col + (lane >> log2(slots * n_row))
    fields = jnp.where(sub == n_col, device >> log2(n_col), 0)
    fields = jnp.where(sub == n_col + 1, (device & (n_col - 1)) >> 1, fields)
    fields = jnp.where(sub == n_col + 2, device & 1, fields)
    fields = jnp.where(sub == n_col + 3, lane & (slots - 1), fields)
    info = against(jnp.where(sub < n_col, spread, fields.astype(F32)), holds)
    line, plane, core, slot = [info[n_col + i:n_col + i + 1, :] for i in range(4)]
    column = jnp.zeros((1, nb), F32)
    for g in range(n_col):
        column = jnp.where(c == g, info[g:g + 1, :], column)
    within = iota((gcols, nb), 0).astype(F32)
    graph = jnp.concatenate([ones(info[g:g + 1, :] == within) for g in range(n_col)], axis=0).astype(BF16)
    upper = ones(iota((nb, nb), 0) < iota((nb, nb), 1)).astype(BF16)

    sub, row = iota((META, nb), 0), iota((META, nb), 1)
    wsel = ones((sub < n_row * windows) & (row == gcols * (sub >> log2(windows)) + (sub & (windows - 1))))
    once = against(wsel, graph)
    twice = against(once, graph)
    each = iota((1, nb), 1)
    soon, late = [], []
    for q in range(n_row):
        inner = sum(once[windows * q + i:windows * q + i + 1, :] for i in range(windows))
        target = sum(twice[windows * q + i:windows * q + i + 1, :] for i in range(windows))
        is_window = ((each >> log2(gcols)) == q) & ((each & (gcols - 1)) < windows)
        s = jnp.where(is_window, 1.0, ones(inner > 0.5))
        soon.append(s)
        late.append(ones(target > 0.5) * (1.0 - s))
    urgent = ones(sum(soon) > 0.5)
    need = ones(sum(soon) + sum(late) > 0.5)

    chip = (line * nz + plane).astype(I32)
    on_chip = ones(sub == chip)
    soon_mask, late_mask = on_chip * urgent, on_chip * (need - urgent)
    soon_count = jnp.sum(soon_mask, axis=1, keepdims=True)
    late_count = jnp.sum(late_mask, axis=1, keepdims=True)
    most_soon = most(soon_count)
    first = jnp.full((1, 1), float(tiers[-1]["n"][0]), F32)
    for tier in reversed(tiers):
        first = jnp.where(most_soon <= float(tier["n"][0]), float(tier["n"][0]), first)

    chips = (META, META)
    left, right = iota(chips, 0), iota(chips, 1)
    load = jnp.broadcast_to(soon_count + late_count, (META, LANES))
    level = times(ones((left & (nz - 1)) == (right & (nz - 1))), load)
    level = most(jnp.floor((level + (n_row - 1.0)) * (1.0 / n_row)))
    taken = jnp.zeros_like(load)
    moves = []
    for d in range(1, n_row):
        spare = jnp.maximum(jnp.minimum(level - load, level - first - taken), 0.0)
        reach = ones(right == ((((left >> log2(nz)) + d) & (n_row - 1)) << log2(nz)) + (left & (nz - 1)))
        back = ones(right == ((((left >> log2(nz)) + n_row - d) & (n_row - 1)) << log2(nz)) + (left & (nz - 1)))
        move = jnp.minimum(jnp.minimum(jnp.maximum(load - level, 0.0), float(SHIFTED)), times(reach, spare))
        arrived = times(back, move)
        load, taken = load - move + arrived, taken + arrived
        moves.append(move[:, 0:1])
    taken = taken[:, 0:1]
    stay = late_count - sum(moves)
    kept = soon_count + stay
    most_pool = most(jnp.where(taken > 0.5, jnp.maximum(kept, first) + taken, kept))
    late_rank = jnp.sum(on_chip * times(late_mask, upper), axis=0, keepdims=True)
    below = jnp.sum(on_chip * stay, axis=0, keepdims=True)
    is_late = need - urgent
    moved, entry, carrier = jnp.zeros((1, nb), F32), jnp.zeros((1, nb), F32), line
    for d in range(1, n_row):
        above = below + jnp.sum(on_chip * moves[d - 1], axis=0, keepdims=True)
        hit = is_late * ones((late_rank >= below) & (late_rank < above))
        moved = moved + hit
        entry = entry + hit * ((d - 1) * SHIFTED + late_rank - below)
        carrier = carrier + hit * d
        below = above
    carrier = jnp.where(carrier >= n_row, carrier - n_row, carrier)
    home = chip
    chip = (carrier * nz + plane).astype(I32)
    on_chip_now = ones(sub == chip)
    rank = jnp.where(urgent > 0.5, times(soon_mask, upper), soon_count + times(late_mask, upper))
    came = jnp.maximum(kept, first) + times(on_chip_now * moved, upper)
    spot = jnp.where(moved > 0.5, jnp.sum(on_chip_now * came, axis=0, keepdims=True),
                     jnp.sum(on_chip * rank, axis=0, keepdims=True))
    spot = jnp.where(need > 0.5, spot, 999.0)
    line = carrier
    m1 = tiers[0]["m"][1]

    sender, getter = sub >> log2(n_row), sub & (n_row - 1)
    soon_pair, late_pair = jnp.zeros((META, nb), F32), jnp.zeros((META, nb), F32)
    for q in range(n_row):
        soon_pair = jnp.where(getter == q, soon[q], soon_pair)
        late_pair = jnp.where(getter == q, late[q], late_pair)
    from_line = ones((sender == line.astype(I32)) & (sender != getter))
    soon_pair, late_pair = soon_pair * from_line, late_pair * from_line
    soon_sum = jnp.sum(soon_pair, axis=1, keepdims=True)
    at0 = times(soon_pair, upper)
    can = late_pair * ones(spot < first)
    at1 = times(can, upper)
    in1 = can * ones(at1 < float(m1))
    rest = late_pair * (1.0 - in1)
    at2 = times(rest, upper)
    most_line, most_rest = most(soon_sum), most(jnp.sum(rest, axis=1, keepdims=True))
    key = jnp.where(rest > 0.5, STAGE[2] + at2, -1.0)
    key = jnp.where(in1 > 0.5, STAGE[1] + at1, key)
    key = jnp.where(soon_pair > 0.5, at0, key)

    choice = jnp.full((1, 1), len(tiers), I32)
    for t in reversed(range(len(tiers))):
        n, m = tiers[t]["n"], tiers[t]["m"]
        fits = ((first == float(n[0])) & (most_soon <= float(n[0])) & (most_pool <= float(sum(n)))
                & (most_line <= float(m[0])) & (most_rest <= float(m[2])))
        choice = jnp.where(fits, t, choice)
    out[33] = jnp.broadcast_to(choice, (1, LANES))

    wide = iota((LANES, nb), 0)
    col = iota((LANES, nb), 1)
    step = z.astype(F32) - plane
    step = jnp.where(step < 0, step + nz, step)
    mine = ones(chip == (r * nz + z))
    pack = ones(wide.astype(F32) == jnp.where(mine > 0.5, spot, 999.0))
    from_slot = slot + slots * ones(core != k.astype(F32))
    given = jnp.where((moved > 0.5) & (home == (r * nz + z)), entry, -1.0)
    slot_rows = jnp.where(sub == 0, from_slot, 0.0)
    out[34] = against(slot_rows, ones(wide.astype(F32) == given))[0:1, :].astype(I32)
    from_slot = jnp.where(moved > 0.5, 2.0 * slots + entry, from_slot)
    rows = jnp.where(sub == 0, from_slot, jnp.where(sub == 1, step, jnp.where(sub == 2, spot, 0.0)))
    rows = jnp.minimum(rows, 127.0)
    out[0] = against(rows, pack)[0:1, :].astype(I32)
    for d in range(1, n_row):
        pair = r * n_row + lax.rem(r + d, n_row)
        key_of = jnp.sum(jnp.where(sub == pair, key, 0.0), axis=0, keepdims=True)
        got = against(rows, ones(wide.astype(F32) == key_of))
        out[d] = (64.0 * got[1:2, :] + got[2:3, :]).astype(I32)

    key_in = jnp.sum(jnp.where((sender == line.astype(I32)) & (getter == r), key, 0.0), axis=0, keepdims=True)
    away = r.astype(F32) - line
    away = jnp.where(away < 0, away + n_row, away)
    where_a = jnp.where(away == 0, step, nz - 1 + away)
    where_b = jnp.clip(jnp.where(away == 0, spot, key_in), 0.0, 127.0)
    fields = jnp.where(sub == 0, where_a, jnp.where(sub == 1, where_b, jnp.where(sub == 2, column, 0.0)))

    def location(found):
        return (128.0 * found[0:1, :] + found[1:2, :]).astype(I32)

    start = gcols * r
    group = col >> log2(gcols)
    out[32] = location(against(fields, ones((wide < windows) & (col == start + wide))))
    entries, count = windows * n_col, windows * n_col * n_col
    inner = against(ones(col == start + (wide >> log2(n_col))), graph)
    inner = inner * ones((group == (wide & (n_col - 1))) & (wide < entries))
    found = against(fields, inner)
    out[15] = location(found)
    lane_at = found[2:3, :]
    sub_at = jnp.sum(inner * column, axis=1, keepdims=True)
    here, there = iota((LANES, LANES), 0), iota((LANES, LANES), 1)
    same = ones((sub_at == lane_at) & ((here >> log2(n_col)) == (there >> log2(n_col)))
                & (here < entries) & (there < entries))
    leads = ones(jnp.sum(same * ones(there < here), axis=1, keepdims=True) < 0.5) * ones(here[:, 0:1] < entries)
    keeps = jnp.zeros((LANES, gcols), F32)
    tag = iota((LANES, gcols), 0) >> log2(n_col)
    for i in range(windows):
        keeps = jnp.where(tag == i, keep[i:i + 1, :].astype(F32), keeps)
    kept = jnp.sum(keeps * ones(iota((LANES, gcols), 1).astype(F32) == sub_at), axis=1, keepdims=True)
    out[16] = (same * leads * kept)[0:entries, :].astype(I32)
    place = gcols * (here[:, 0:1] >> log2(n_col)).astype(F32) + sub_at
    at = ones(place == there.astype(F32)) * leads
    out[13] = jnp.sum(at * here.astype(F32), axis=0, keepdims=True).astype(I32)
    out[14] = jnp.sum(at, axis=0, keepdims=True).astype(I32)

    inner = against(ones(col == start + (wide >> log2(n_col * n_col))), graph)
    inner = inner * ones(group == ((wide >> log2(n_col)) & (n_col - 1)))
    target = against(inner, graph) * ones(group == (wide & (n_col - 1)))
    found = against(fields, target)
    sub_at = gcols * (here[:, 0:1] >> log2(n_col * n_col)).astype(F32) + jnp.sum(target * column, axis=1, keepdims=True)
    lane_at = gcols * (there[0:1, :] >> log2(n_col * n_col)).astype(F32) + found[2:3, :]
    ahead = ones(sub_at == lane_at) * ones(there < here)
    order = jnp.sum(ones(lane_at < sub_at) + ahead, axis=1, keepdims=True)
    put = ones(order == there.astype(F32))
    narrow = iota((META, LANES), 0)
    got = times(jnp.where(narrow == 3, iota((META, LANES), 1).astype(F32), found), put)
    out[8] = location(got)
    out[9] = got[3:4, :].astype(I32)
    follows = ones(jnp.sum(ahead, axis=1, keepdims=True) > 0.5)
    out[10] = jnp.sum(put * follows, axis=0, keepdims=True).astype(I32)
    out[11] = (jnp.sum(ones(sub_at <= there.astype(F32)), axis=0, keepdims=True) - 1.0).astype(I32)
    out[12] = jnp.minimum(jnp.sum(ones(sub_at == there.astype(F32)), axis=0, keepdims=True), 1.0).astype(I32)
    return out


def plan_kernel(sizes, tiers, labels, cols, keep, owned, index, sibling, tile, line_tiles, group, tiles, send, recv,
                col_send, col_recv, pair_send, pair_recv):
    n_row, n_col, slots = sizes[:3]
    r, c = lax.axis_index("row"), lax.axis_index("col")
    z, k = c // 2, lax.rem(c, 2)
    mate = (r, 2 * z + 1 - k)
    lines = [(lax.rem(r + step, n_row), c) for step in range(1, n_row)]
    others = [(r, lax.rem(c + step, n_col)) for step in range(1, n_col)]
    barrier = pltpu.get_barrier_semaphore()
    for to in lines + others:
        pl.semaphore_signal(barrier, inc=1, device_id=to, device_id_type=MESH)
    rows = jnp.concatenate([cols[...].astype(F32), jnp.zeros((META - n_col, slots), F32)], axis=0)
    rows = jnp.where(iota((META, slots), 0) == n_col, labels[...].astype(F32), rows)
    tile[...] = times(rows, ones(iota((slots, LANES), 0) + slots * r == iota((slots, LANES), 1))).astype(BF16)
    pl.semaphore_wait(barrier, n_row + n_col - 2)
    pair = pltpu.make_async_remote_copy(
        src_ref=owned.at[:, :, 1 - k], dst_ref=sibling, send_sem=pair_send, recv_sem=pair_recv, device_id=mate,
        device_id_type=MESH)
    pair.start()
    copies = [send_to(tile, line_tiles.at[r], (send, recv), step, to) for step, to in enumerate(lines)]
    for copy in copies:
        copy.start()
    line_tiles[r] = tile[...]
    for copy in copies:
        copy.wait()
    group[...] = sum(line_tiles[q].astype(F32) for q in range(n_row)).astype(BF16)
    copies = [send_to(group, tiles.at[c], (col_send, col_recv), step, to) for step, to in enumerate(others)]
    for copy in copies:
        copy.start()
    tiles[c] = group[...]
    for copy in copies:
        copy.wait()
    spread = jnp.concatenate([tiles[q].astype(F32) for q in range(n_col)], axis=1)
    index[...] = jnp.zeros_like(index)
    for row, value in plan(spread, keep[...], r, c, sizes, tiers).items():
        index[row:row + value.shape[0], :] = value
    pair.wait()


def main_kernel(sizes, tier, index, owned, sibling, out, pool, bsend, brecv, zsend0, zsend1, zall0, zall1,
                xsend0, xsend1, xsend2, xrecv0, xrecv1, xrecv2, lefts, parts, every, rights, sums, sems, zs, zr, xs, xr,
                ls, lr, us, ur, ds, dr, ps, pr, bs, br):
    n_row, n_col, slots, windows, gcols, nb = sizes
    nz = n_col // 2
    entries, count = windows * n_col, windows * n_col * n_col
    block = out.shape[0] // windows
    r, c = lax.axis_index("row"), lax.axis_index("col")
    z, k = c // 2, lax.rem(c, 2)
    zsend, zall = (zsend0, zsend1), (zall0, zall1)
    xsend, xrecv = (xsend0, xsend1, xsend2), (xrecv0, xrecv1, xrecv2)
    n, m = tier["n"], tier["m"]
    bounds = [0, n[0], n[0] + n[1]]
    others = [(r, 2 * lax.rem(z + step, nz) + k) for step in range(1, nz)]
    lines = [(lax.rem(r + step, n_row), c) for step in range(1, n_row)]
    mate = (r, 2 * z + 1 - k)
    above, below = others[0], others[-1]
    loads = [pltpu.make_async_copy(owned.at[:, :, k], pool.at[pl.ds(0, slots)], sems.at[0]),
             pltpu.make_async_copy(sibling, pool.at[pl.ds(slots, slots)], sems.at[1])]
    for load in loads:
        load.start()
    greet(others + lines + [mate])
    for load in loads:
        load.wait()

    def bpack():
        for i in range((n_row - 1) * SHIFTED):
            slot = index[34, i]
            for other in range(nz):
                bsend[i * nz + other] = pool[slot, other]

    def bcopies():
        size = SHIFTED * nz
        return [pltpu.make_async_remote_copy(
            src_ref=bsend.at[pl.ds((d - 1) * size, size)], dst_ref=brecv.at[pl.ds((d - 1) * size, size)],
            send_sem=bs.at[d], recv_sem=br.at[d], device_id=lines[d - 1], device_id_type=MESH)
            for d in range(1, n_row)]

    def zpack(s):
        def body(p, carry):
            slot = index[0, bounds[s] + p]
            own = slot < 2 * slots
            for step in range(nz):
                to = lax.rem(z + step, nz)
                if s == 0:
                    value = pool[slot, to]
                else:
                    value = lax.select(own, pool[jnp.where(own, slot, 0), to],
                                       brecv[jnp.where(own, 0, slot - 2 * slots) * nz + to])
                if step == 0:
                    zall[s][p] = value
                else:
                    zsend[s][(step - 1) * n[s] + p] = value
            return carry

        lax.fori_loop(0, n[s], body, 0)

    def zcopies(s):
        return [pltpu.make_async_remote_copy(
            src_ref=zsend[s].at[pl.ds((step - 1) * n[s], n[s])], dst_ref=zall[s].at[pl.ds(step * n[s], n[s])],
            send_sem=zs.at[s * nz + step], recv_sem=zr.at[s * nz + step], device_id=others[step - 1],
            device_id_type=MESH) for step in range(1, nz)]

    def from_z(step, spot, upto, value):
        for s in upto:
            inside = (step >= 0) & (spot >= bounds[s]) & (spot < bounds[s + 1])
            got = zall[s][jnp.where(inside, step * n[s] + spot - bounds[s], 0)]
            value = got if value is None else lax.select(inside, got, value)
        return value

    def from_x(away, key, upto, value):
        for s in upto:
            inside = (away >= 0) & (key >= STAGE[s]) & (key < STAGE[s] + m[s])
            got = xrecv[s][jnp.where(inside, away * m[s] + key - STAGE[s], 0)]
            value = lax.select(inside, got, value)
        return value

    def fetch(code, zupto, xupto, value=None):
        a, b = code // 128, lax.rem(code, 128)
        value = from_z(jnp.where(a < nz, a, -1), b, zupto, value)
        return from_x(jnp.where(a < nz, -1, a - nz), b, xupto, value)

    def xpack(s):
        ready = [0, 1] if s == 2 else [0]

        for d in range(1, n_row):
            def body(q, carry):
                code = index[d, STAGE[s] + q]
                xsend[s][(d - 1) * m[s] + q] = from_z(code // 64, lax.rem(code, 64), ready, None)
                return carry

            lax.fori_loop(0, m[s], body, 0)

    def xcopies(s):
        return [pltpu.make_async_remote_copy(
            src_ref=xsend[s].at[pl.ds((d - 1) * m[s], m[s])], dst_ref=xrecv[s].at[pl.ds((d - 1) * m[s], m[s])],
            send_sem=xs.at[s * n_row + d], recv_sem=xr.at[s * n_row + d], device_id=lines[d - 1],
            device_id_type=MESH) for d in range(1, n_row)]

    def start(copies):
        for copy in copies:
            copy.start()

    def arrive(copies):
        for copy in copies:
            copy.wait_recv()

    def left_send(sem, source, to):
        slab = lefts.at[source]
        return pltpu.make_async_remote_copy(
            src_ref=slab, dst_ref=slab, send_sem=ls.at[sem], recv_sem=lr.at[sem], device_id=to, device_id_type=MESH)

    zpack(0)
    start(zcopies(0))
    bpack()
    start(bcopies())
    arrive(bcopies())
    zpack(1)
    arrive(zcopies(0))
    start(zcopies(1))
    xpack(0)
    start(xcopies(0))
    xpack(1)
    arrive(xcopies(0))
    for i in range(windows):
        lefts[c, i] = fetch(index[32, i], [0], [0])
    left_out = [left_send(step, c, to) for step, to in enumerate(others)]
    left_pair = [left_send(nz, c, mate)]
    start(left_out)
    start(left_pair)
    start(xcopies(1))
    for step in range(1, nz):
        left_out[step - 1].wait_recv()
        left_pair.append(left_send(nz + step, 2 * lax.rem(z - step + nz, nz) + k, mate))
        left_pair[-1].start()
    arrive(left_pair)

    def square(e, carry):
        right = fetch(index[15, e], [0], [0])
        left = lefts[lax.rem(e, n_col), e // n_col]
        parts[e] = jnp.dot(left, right, preferred_element_type=F32)
        return carry

    def merge(e, carry):
        start_at = e // n_col * n_col
        total = parts[start_at] * index[16 + e, start_at].astype(F32)
        for i in range(1, n_col):
            total += parts[start_at + i] * index[16 + e, start_at + i].astype(F32)
        every[c, e] = total.astype(BF16)
        return carry

    def pass_on(sem, half, step, place, to):
        slab = every.at[place, pl.ds(half * n_col, n_col)]
        return pltpu.make_async_remote_copy(
            src_ref=slab, dst_ref=slab, send_sem=sem[0].at[half * nz + step], recv_sem=sem[1].at[half * nz + step],
            device_id=to, device_id_type=MESH)

    def up(half, step):
        return pass_on((us, ur), half, step, 2 * lax.rem(z - step + nz, nz) + k, above)

    def down(half, step):
        return pass_on((ds, dr), half, step, 2 * lax.rem(z + step, nz) + k, below)

    def across(half, step):
        return pass_on((ps, pr), half, step, 2 * lax.rem(z + step, nz) + k, mate)

    def relay(half, step):
        @pl.when(z - step >= 0)
        def _():
            up(half, step - 1).wait_recv()

        @pl.when((z - step >= 0) & (z < nz - 1))
        def _():
            up(half, step).start()

        @pl.when(z - step >= 0)
        def _():
            across(half, nz - step).start()

        @pl.when(z + step <= nz - 1)
        def _():
            down(half, step - 1).wait_recv()

        @pl.when((z + step <= nz - 1) & (z > 0))
        def _():
            down(half, step).start()

        @pl.when(z + step <= nz - 1)
        def _():
            across(half, step).start()

    def first_pass(half):
        @pl.when(z < nz - 1)
        def _():
            up(half, 0).start()

        @pl.when(z > 0)
        def _():
            down(half, 0).start()

        across(half, 0).start()

    for w in range(windows):
        lax.fori_loop(w * n_col, (w + 1) * n_col, square, 0)
        lax.fori_loop(w * n_col, (w + 1) * n_col, merge, 0)
        first_pass(w)
    arrive(zcopies(1))
    xpack(2)
    start(xcopies(2))
    arrive(xcopies(1))

    def gather_early(t, carry):
        rights[t] = fetch(index[8, t], [0, 1], [0, 1])
        return carry

    lax.fori_loop(0, count, gather_early, 0)
    for step in range(1, nz):
        for w in range(windows):
            relay(w, step)
    for step in range(nz):
        for w in range(windows):
            across(w, step).wait_recv()
    arrive(xcopies(2))

    def multiply(q, acc):
        for i in range(4):
            t = q * 4 + i
            p = index[9, t]
            right = fetch(index[8, t], [], [2], rights[t])
            term = jnp.dot(every[lax.rem(p, n_col), p // n_col], right, preferred_element_type=F32)
            acc = acc * index[10, t].astype(F32) + term
            sums[t] = acc
        return acc

    lax.fori_loop(0, count // 4, multiply, jnp.zeros((block, block), F32))
    for w in range(windows):
        def write(j, carry):
            at = w * gcols + j
            cube = sums[jnp.maximum(index[11, at], 0)] * (-2.0 * index[12, at].astype(F32))
            own = every[c, index[13, at]].astype(F32) * (3.0 * index[14, at].astype(F32))
            out[w * block:(w + 1) * block, pl.ds(pl.multiple_of(j * block, block), block)] = (own + cube).astype(BF16)
            return carry

        lax.fori_loop(0, gcols, write, 0)

    for copies in (bcopies(), zcopies(0), zcopies(1), xcopies(0), xcopies(1), xcopies(2), left_out, left_pair):
        for copy in copies:
            copy.wait_send()
    for w in range(windows):
        for step in range(nz):
            @pl.when((z - step >= 0) & (z < nz - 1))
            def _(w=w, step=step):
                up(w, step).wait_send()

            @pl.when((z + step <= nz - 1) & (z > 0))
            def _(w=w, step=step):
                down(w, step).wait_send()

            across(w, step).wait_send()


TIERS = (dict(n=(9, 10), m=(9, 14, 18)), dict(n=(9, 18), m=(11, 14, 26)), dict(n=(11, 8), m=(11, 14, 18)),
         dict(n=(11, 16), m=(11, 14, 26)), dict(n=(14, 22), m=(14, 14, 30)))


def local(owned_blocks, owned_rows, owned_cols, keep):
    n_row, n_col = lax.axis_size("row"), lax.axis_size("col")
    nz = n_col // 2
    slots = owned_rows.shape[0]
    windows, gcols = keep.shape
    nb = gcols * n_col
    block = owned_blocks.shape[-1]
    one = (block, block)
    dtype = owned_blocks.dtype
    entries, count = windows * n_col, windows * n_col * n_col
    if (count > LANES or n_col > 8 or n_row > 4 or entries > 16 or nz > 4 or n_row * slots != LANES or 2 * slots > 64
            or windows * gcols > LANES or n_row < 2 or nz < 2):
        return general(owned_blocks, owned_rows, owned_cols, keep)
    sizes = (n_row, n_col, slots, windows, gcols, nb)
    halves = owned_blocks.reshape((slots, nz, 2) + one)
    index, sibling = pl.pallas_call(
        functools.partial(plan_kernel, sizes, TIERS),
        out_shape=(jax.ShapeDtypeStruct((ROWS, LANES), I32), jax.ShapeDtypeStruct((slots, nz) + one, dtype)),
        in_specs=[VMEM, VMEM, VMEM, ANY], out_specs=(VMEM, ANY),
        scratch_shapes=[pltpu.VMEM((META, LANES), BF16), pltpu.VMEM((n_row, META, LANES), BF16),
                        pltpu.VMEM((META, LANES), BF16), pltpu.VMEM((n_col, META, LANES), BF16),
                        DMA((n_row,)), DMA((n_row,)), DMA((n_col,)), DMA((n_col,)), DMA, DMA],
        compiler_params=pltpu.CompilerParams(collective_id=20, has_side_effects=True, vmem_limit_bytes=BIG),
    )(owned_rows[None, :], owned_cols.T, keep, halves)

    def quick(t):
        n, m = TIERS[t]["n"], TIERS[t]["m"]
        scratch = [pltpu.VMEM((2 * slots, nz) + one, dtype)]
        scratch += [pltpu.VMEM(((n_row - 1) * SHIFTED * nz,) + one, dtype)] * 2
        scratch += [pltpu.VMEM(((nz - 1) * q,) + one, dtype) for q in n]
        scratch += [pltpu.VMEM((nz * q,) + one, dtype) for q in n]
        scratch += [pltpu.VMEM(((n_row - 1) * q,) + one, dtype) for q in m] * 2
        scratch += [pltpu.VMEM((n_col, windows) + one, dtype), pltpu.VMEM((entries,) + one, F32),
                    pltpu.VMEM((n_col, entries) + one, dtype), pltpu.VMEM((count,) + one, dtype),
                    pltpu.VMEM((count,) + one, F32), DMA((2,))]
        scratch += [DMA((2 * nz,))] * 2 + [DMA((3 * n_row,))] * 2 + [DMA((2 * nz,))] * 2
        scratch += [DMA((windows * nz,))] * 6 + [DMA((n_row,))] * 2
        return pl.pallas_call(
            functools.partial(main_kernel, sizes, TIERS[t]),
            out_shape=jax.ShapeDtypeStruct((windows * block, gcols * block), dtype),
            in_specs=[SMEM, ANY, ANY], out_specs=VMEM, scratch_shapes=scratch,
            compiler_params=pltpu.CompilerParams(
                collective_id=21 + t, has_side_effects=True, vmem_limit_bytes=BIG),
        )(index, halves, sibling)

    branches = [functools.partial(quick, t) for t in range(len(TIERS))]
    branches.append(lambda: general(owned_blocks, owned_rows, owned_cols, keep))
    return lax.switch(index[33, 0], branches)


def solution(mesh):
    placed = (
        P(("row", "col"), None, None, None),
        P(("row", "col")),
        P(("row", "col"), None),
        P("row", "col"),
    )
    return jax.shard_map(
        local, mesh=mesh, in_specs=placed, out_specs=P("row", "col"), check_vma=False
    )
```

```python
import functools

import jax
import jax.numpy as jnp
from jax import lax
from jax.experimental import pallas as pl
from jax.experimental.pallas import tpu as pltpu
from jax.sharding import PartitionSpec as P

MESH = pl.DeviceIdType.MESH
ANY = pl.BlockSpec(memory_space=pl.ANY)
SMEM = pl.BlockSpec(memory_space=pltpu.SMEM)
VMEM = pl.BlockSpec(memory_space=pltpu.VMEM)
DMA = pltpu.SemaphoreType.DMA
BIG = 60 * 1024 * 1024


def remote_params(number):
    return pltpu.CompilerParams(collective_id=number, has_side_effects=True)


def spread_kernel(n_row, n_col, meta, owned, meta_all, sibling, send, recv, pair_send, pair_recv):
    r, c = lax.axis_index("row"), lax.axis_index("col")
    me = r * n_col + c
    devices = n_row * n_col
    barrier = pltpu.get_barrier_semaphore()

    def greet(i, carry):
        d = lax.rem(me + i, devices)
        pl.semaphore_signal(barrier, inc=1, device_id=(d // n_col, lax.rem(d, n_col)), device_id_type=MESH)
        return carry

    lax.fori_loop(1, devices, greet, 0)
    pl.semaphore_wait(barrier, devices - 1)
    z, k = c // 2, lax.rem(c, 2)
    other = 1 - k
    pair = pltpu.make_async_remote_copy(
        src_ref=owned.at[:, :, other], dst_ref=sibling, send_sem=pair_send, recv_sem=pair_recv,
        device_id=(r, 2 * z + other), device_id_type=MESH)
    pair.start()

    def copy_to(i):
        d = lax.rem(me + i, devices)
        return pltpu.make_async_remote_copy(
            src_ref=meta, dst_ref=meta_all.at[me], send_sem=send.at[i], recv_sem=recv.at[i],
            device_id=(d // n_col, lax.rem(d, n_col)), device_id_type=MESH)

    def begin(i, carry):
        copy_to(i).start()
        return carry

    def finish(i, carry):
        copy_to(i).wait()
        return carry

    lax.fori_loop(1, devices, begin, 0)
    lax.fori_loop(1, devices, finish, 0)
    pair.wait()


def greet(partners):
    barrier = pltpu.get_barrier_semaphore()
    for partner in partners:
        pl.semaphore_signal(barrier, inc=1, device_id=partner, device_id_type=MESH)
    pl.semaphore_wait(barrier, len(partners))


def send_to(source, dest, sems, step, partner):
    return pltpu.make_async_remote_copy(
        src_ref=source, dst_ref=dest, send_sem=sems[0].at[step], recv_sem=sems[1].at[step],
        device_id=partner, device_id_type=MESH)


def place_of(nz):
    r, c = lax.axis_index("row"), lax.axis_index("col")
    z, k = c // 2, lax.rem(c, 2)
    return r, c, z, k, [(r, 2 * lax.rem(z + step, nz) + k) for step in range(1, nz)]


def first_kernel(nz, count, source, got, send, recv):
    r, c, z, k, others = place_of(nz)
    greet(others)
    copies = [send_to(source.at[to[1] // 2, pl.ds(0, count)], got.at[z], (send, recv), step, to)
              for step, to in enumerate(others)]
    for copy in copies:
        copy.start()
    for copy in copies:
        copy.wait()


def second_kernel(n_row, nz, source, wanted, got, plane_got, send, recv, psend, precv):
    r, c, z, k, others = place_of(nz)
    lines = [(lax.rem(r + step, n_row), c) for step in range(1, n_row)]
    greet(others + lines)
    count = got.shape[1]
    copies = [send_to(wanted.at[to[0]], plane_got.at[r], (psend, precv), step, to) for step, to in enumerate(lines)]
    copies += [send_to(source.at[to[1] // 2, pl.ds(0, count)], got.at[z], (send, recv), step, to)
               for step, to in enumerate(others)]
    for copy in copies:
        copy.start()
    for copy in copies:
        copy.wait()


def left_kernel(nz, piece, got, send, recv, psend, precv):
    r, c, z, k, others = place_of(nz)
    mate = (r, 2 * z + 1 - k)
    greet(others + [mate])
    copies = [send_to(piece, got.at[c], (send, recv), step, to) for step, to in enumerate(others)]
    for copy in copies:
        copy.start()
    pairs = [send_to(piece, got.at[c], (psend, precv), 0, mate)]
    pairs[0].start()
    for step in range(1, nz):
        copies[step - 1].wait_recv()
        origin = 2 * lax.rem(z - step + nz, nz) + k
        pairs.append(send_to(got.at[origin], got.at[origin], (psend, precv), step, mate))
        pairs[-1].start()
    for copy in copies:
        copy.wait_send()
    for pair in pairs:
        pair.wait()


def last_kernel(n_row, nz, wanted, filtered, plane_got, every, send, recv, up_send, up_recv, down_send, down_recv,
                psend, precv):
    r, c, z, k, others = place_of(nz)
    mate = (r, 2 * z + 1 - k)
    lines = [(lax.rem(r + step, n_row), c) for step in range(1, n_row)]
    above, below = (r, 2 * lax.rem(z + 1, nz) + k), (r, 2 * lax.rem(z + nz - 1, nz) + k)
    greet(lines + [above, below, mate])
    plane = [send_to(wanted.at[to[0]], plane_got.at[r], (send, recv), step, to) for step, to in enumerate(lines)]

    def up(step, own):
        block = every.at[2 * lax.rem(z - step + nz, nz) + k]
        return send_to(filtered if own else block, block, (up_send, up_recv), step, above)

    def down(step, own):
        block = every.at[2 * lax.rem(z + step, nz) + k]
        return send_to(filtered if own else block, block, (down_send, down_recv), step, below)

    def across(step, own):
        block = every.at[2 * lax.rem(z + step, nz) + k]
        return send_to(filtered if own else block, block, (psend, precv), step, mate)

    @pl.when(z < nz - 1)
    def _():
        up(0, True).start()

    @pl.when(z > 0)
    def _():
        down(0, True).start()

    across(0, True).start()
    for copy in plane:
        copy.start()
    for step in range(1, nz):
        @pl.when(z - step >= 0)
        def _():
            up(step - 1, False).wait_recv()
            across(nz - step, False).start()

        @pl.when((z - step >= 0) & (z < nz - 1))
        def _():
            up(step, False).start()

        @pl.when(z + step <= nz - 1)
        def _():
            down(step - 1, False).wait_recv()
            across(step, False).start()

        @pl.when((z + step <= nz - 1) & (z > 0))
        def _():
            down(step, False).start()
    for step in range(nz):
        @pl.when((z - step >= 0) & (z < nz - 1))
        def _():
            up(step, False).wait_send()

        @pl.when((z + step <= nz - 1) & (z > 0))
        def _():
            down(step, False).wait_send()
    for step in range(nz):
        across(step, False).wait()
    for copy in plane:
        copy.wait()


def pick(sources, index, dest, sem):
    start = 0
    for source in sources:
        stop = start + source.shape[0]

        @pl.when((index >= start) & (index < stop))
        def _(source=source, start=start):
            pltpu.make_async_copy(source.at[index - start], dest, sem).start()

        start = stop


def gather_kernel(index, *refs):
    sources, (out, sem) = refs[:-2], refs[-2:]
    start = pl.program_id(0) * out.shape[0]

    def begin(i, carry):
        pick(sources, index[start + i], out.at[i], sem)
        return carry

    lax.fori_loop(0, out.shape[0], begin, 0)
    pltpu.make_async_copy(out, out, sem).wait()


def flat(array):
    return array.reshape((-1,) + array.shape[-2:])


def gather(index, *sources):
    block = sources[0].shape[-2:]
    count = index.shape[0]
    chunk = max(n for n in range(1, min(count, 512) + 1) if count % n == 0)
    return pl.pallas_call(
        gather_kernel,
        grid=(count // chunk,),
        out_shape=jax.ShapeDtypeStruct((count,) + block, sources[0].dtype),
        in_specs=[SMEM] + [ANY] * len(sources), out_specs=pl.BlockSpec((chunk,) + block, lambda i: (i, 0, 0)),
        scratch_shapes=[DMA],
        compiler_params=pltpu.CompilerParams(vmem_limit_bytes=BIG),
    )(index, *[flat(source) for source in sources])


def square_kernel(left_at, right_at, slot, keep, lefts, own_left, rights, own_rights, out, a, b, acc, sems):
    count = out.shape[0]

    def begin(i, carry):
        pick((lefts, own_left), left_at[i], a.at[i], sems.at[0])
        pick((rights, own_rights), right_at[i], b.at[i], sems.at[1])
        return carry

    lax.fori_loop(0, count, begin, 0)
    acc[...] = jnp.zeros_like(acc)
    pltpu.make_async_copy(a, a, sems.at[0]).wait()
    pltpu.make_async_copy(b, b, sems.at[1]).wait()

    def multiply(q, carry):
        ids = [q * 4 + i for i in range(4)]
        terms = [jnp.dot(a[i], b[i], preferred_element_type=jnp.float32) for i in ids]
        for i, term in zip(ids, terms):
            acc[slot[i]] += term
        return carry

    lax.fori_loop(0, count // 4, multiply, 0)

    def write(i, carry):
        out[i] = (acc[i] * keep[i].astype(jnp.float32)).astype(out.dtype)
        return carry

    lax.fori_loop(0, count, write, 0)


def cubed_kernel(left_at, right_at, target, own_target, every, own, got1, send1, got2, send2, out, a, b, f, acc, sems):
    count = a.shape[0]
    windows = acc.shape[0]
    block = a.shape[-1]
    per_window = count // windows
    own_per_window = f.shape[0] // windows
    mine = pltpu.make_async_copy(own, f, sems.at[2])
    mine.start()

    def begin(i, carry):
        pick((every, own), left_at[i], a.at[i], sems.at[0])
        pick((got1, send1, got2, send2), right_at[i], b.at[i], sems.at[1])
        return carry

    lax.fori_loop(0, count, begin, 0)
    acc[...] = jnp.zeros_like(acc)
    mine.wait()
    for w in range(windows):
        def add(i, carry):
            e = w * own_per_window + i
            acc[w, own_target[e]] -= 1.5 * f[e].astype(jnp.float32)
            return carry

        lax.fori_loop(0, own_per_window, add, 0)
    pltpu.make_async_copy(a, a, sems.at[0]).wait()
    pltpu.make_async_copy(b, b, sems.at[1]).wait()
    for w in range(windows):
        def multiply(q, carry):
            ids = [w * per_window + q * 4 + i for i in range(4)]
            terms = [jnp.dot(a[i], b[i], preferred_element_type=jnp.float32) for i in ids]
            for i, term in zip(ids, terms):
                acc[w, target[i]] += term
            return carry

        lax.fori_loop(0, per_window // 4, multiply, 0)
    for w in range(windows):
        for j in range(acc.shape[1]):
            out[w * block:(w + 1) * block, j * block:(j + 1) * block] = (-2.0 * acc[w, j]).astype(out.dtype)


def running(mask):
    n = mask.shape[-1]
    before = (jnp.arange(n)[:, None] < jnp.arange(n)[None, :]).astype(jnp.bfloat16)
    lines = mask.reshape(-1, n).astype(jnp.bfloat16)
    return jnp.dot(lines, before, preferred_element_type=jnp.float32).astype(jnp.int32).reshape(mask.shape)


def general(owned_blocks, owned_rows, owned_cols, keep):
    n_row, n_col = lax.axis_size("row"), lax.axis_size("col")
    devices = n_row * n_col
    nz = n_col // 2
    r, c = lax.axis_index("row"), lax.axis_index("col")
    z, k = c // 2, lax.rem(c, 2)
    block = owned_blocks.shape[-1]
    dtype = owned_blocks.dtype
    slots = owned_rows.shape[0]
    per_band = slots // n_row
    windows, gcols = keep.shape
    nb = gcols * n_col
    size = slots * (1 + n_col)
    tall = -(-size // 1024) * 8
    one = (block, block)
    chips = devices // 2
    pool = 2 * slots
    i32 = jnp.int32

    packed = jnp.concatenate([owned_rows[:, None], owned_cols], axis=1).reshape(-1)
    meta = jnp.pad(packed, (0, tall * 128 - size)).reshape(tall, 128)
    meta_all, sibling = pl.pallas_call(
        functools.partial(spread_kernel, n_row, n_col),
        out_shape=(jax.ShapeDtypeStruct((devices, tall, 128), i32),
                   jax.ShapeDtypeStruct((slots, nz) + one, dtype)),
        in_specs=[ANY, ANY], out_specs=(ANY, ANY),
        scratch_shapes=[DMA((devices,)), DMA((devices,)), DMA, DMA],
        compiler_params=remote_params(0),
    )(meta, owned_blocks.reshape((slots, nz, 2) + one))
    me = r * n_col + c
    is_me = jnp.arange(devices)[:, None] == me
    labels = jnp.where(is_me, packed[None, :], meta_all.reshape(devices, -1)[:, :size])
    labels = labels.reshape(devices * slots, 1 + n_col)
    rows, cols = labels[:, 0], labels[:, 1:]
    slot_ids = jnp.arange(devices * slots, dtype=i32)
    every_row = jnp.arange(nb, dtype=i32)
    filled = rows < gcols * 2
    row_id = jnp.where(filled, gcols * (slot_ids // per_band % n_row + n_row * (rows // gcols)) + rows % gcols, nb)
    holder = jnp.sum(jnp.where(row_id[None, :] == every_row[:, None], slot_ids[None, :], 0), axis=1)
    row_cols = cols[holder]
    chip = holder // pool
    line, plane = chip // nz, chip % nz

    base = gcols * jnp.arange(n_col, dtype=i32)
    window = gcols * jnp.arange(n_row, dtype=i32)[:, None] + jnp.arange(windows, dtype=i32)[None, :]
    inner = base + row_cols[window]
    targets = base + row_cols[inner]
    is_window = jnp.any(window[:, :, None] == every_row, axis=1)
    is_inner = jnp.any(inner.reshape(n_row, -1, 1) == every_row, axis=1) & ~is_window
    is_target = jnp.any(targets.reshape(n_row, -1, 1) == every_row, axis=1) & ~is_inner & ~is_window
    urgent = jnp.any(is_window | is_inner, axis=0)
    wanted_row = urgent.astype(i32) + jnp.any(is_window | is_inner | is_target, axis=0).astype(i32)
    wanted = jnp.sum(jnp.where(row_id[:, None] == every_row[None, :], wanted_row[None, :], 0), axis=1).reshape(chips, pool)
    urgent_count = (wanted == 2).sum(axis=1)
    place = jnp.where(wanted == 2, running(wanted == 2), urgent_count[:, None] + running(wanted == 1))
    place = jnp.where(wanted > 0, place, pool)
    spot = place.reshape(-1)[holder]
    on_line = line[None, :] == jnp.arange(n_row, dtype=i32)[:, None]

    def ranks(need):
        both = need[:, None, :] & on_line[None, :, :]
        rank = jnp.sum(jnp.where(both, running(both), 0), axis=1)
        return rank, both.sum(axis=2).max()

    rank_window, _ = ranks(is_window)
    rank_inner, most_inner = ranks(is_inner)

    def shares(early, limit):
        now = is_target & (spot < early)[None, :]
        rank_now, _ = ranks(now)
        now = now & (rank_now < limit)
        later = is_target & ~now
        rank_later, most_later = ranks(later)
        return now, rank_now, later, rank_later, most_later

    inner_mine = inner[r].reshape(-1)
    targets_mine = targets[r].reshape(-1)
    cols_mine = lax.dynamic_index_in_dim(row_cols, c, 1, keepdims=False)
    square_target = cols_mine[inner_mine].reshape(windows, n_col)
    same = square_target[:, :, None] == square_target[:, None, :]
    first = jnp.argmax(same, axis=2).astype(i32)
    square_slot = (first + n_col * jnp.arange(windows, dtype=i32)[:, None]).reshape(-1)
    kept = jnp.take_along_axis(keep, square_target, axis=1).reshape(-1)
    cubed_target = cols_mine[targets_mine]
    entries = windows * n_col

    step = (z - plane + nz) % nz
    zs = jnp.arange(nz, dtype=i32)[:, None]
    place_mine = lax.dynamic_index_in_dim(place, r * nz + z, 0, keepdims=False)

    def pooled(start, count):
        position = start + jnp.arange(count, dtype=i32)
        pick_slot = jnp.sum(
            jnp.where(place_mine[None, :] == position[:, None], jnp.arange(pool, dtype=i32)[None, :], 0), axis=1)
        at = pick_slot[None, :] % slots
        index = jnp.where(
            pick_slot[None, :] // slots == k, at * n_col + 2 * zs + k, slots * n_col + at * nz + zs)
        return gather(index.reshape(-1), owned_blocks, sibling).reshape((nz, count) + one)

    def demand(need, rank, count, source_at):
        sending = need & (line == r)[None, :]
        chosen = sending[:, None, :] & (rank[:, None, :] == jnp.arange(count, dtype=i32)[None, :, None])
        return jnp.sum(jnp.where(chosen, source_at[None, None, :], 0), axis=2)

    def opening(early, most, limit, share, parts):
        now, rank_now = share[:2]
        cap1 = windows + most + limit
        now_all = is_window | is_inner | now
        now_rank = jnp.where(is_window, rank_window, jnp.where(is_inner, windows + rank_inner, windows + most + rank_now))
        send1 = gather(demand(now_all, now_rank, cap1, step * early + spot).reshape(-1), *parts)
        found1 = line * cap1 + now_rank[r] + jnp.where(line == r, n_row * cap1, 0)
        return now_all, found1, send1.reshape((n_row, cap1) + one)

    def run(early, late, rest, share, parts, opened, outgoing, number):
        later, rank_later = share[2:4]
        now_all, found1, send1 = opened
        cap1 = send1.shape[1]
        late_at = jnp.where(plane == z, nz * late + plane * outgoing.shape[1], plane * late)
        held_at = jnp.where(spot < early, step * early + spot, nz * early + late_at + spot - early)
        got_late, got1 = pl.pallas_call(
            functools.partial(second_kernel, n_row, nz),
            out_shape=(jax.ShapeDtypeStruct((nz, late) + one, dtype),
                       jax.ShapeDtypeStruct((n_row, cap1) + one, dtype)),
            in_specs=[ANY, ANY], out_specs=(ANY, ANY),
            scratch_shapes=[DMA((nz,)), DMA((nz,)), DMA((n_row,)), DMA((n_row,))],
            compiler_params=remote_params(number + 1),
        )(outgoing, send1)
        window_mine = gcols * r + jnp.arange(windows, dtype=i32)
        left_mine = gather(found1[window_mine], got1, send1)
        lefts = pl.pallas_call(
            functools.partial(left_kernel, nz),
            out_shape=jax.ShapeDtypeStruct((n_col, windows) + one, dtype),
            in_specs=[ANY], out_specs=ANY,
            scratch_shapes=[DMA((nz,))] * 4,
            compiler_params=remote_params(number + 2),
        )(left_mine)
        ws = jnp.arange(windows, dtype=i32)[:, None]
        gs = jnp.arange(n_col, dtype=i32)[None, :]
        left_at = jnp.where(gs == c, n_col * windows + ws, gs * windows + ws).reshape(-1)
        filtered = pl.pallas_call(
            square_kernel,
            out_shape=jax.ShapeDtypeStruct((entries,) + one, dtype),
            in_specs=[SMEM] * 4 + [ANY] * 4, out_specs=VMEM,
            scratch_shapes=[pltpu.VMEM((entries,) + one, dtype), pltpu.VMEM((entries,) + one, dtype),
                            pltpu.VMEM((entries,) + one, jnp.float32), DMA((2,))],
            compiler_params=pltpu.CompilerParams(vmem_limit_bytes=BIG),
        )(left_at, found1[inner_mine], square_slot, kept, flat(lefts), left_mine, flat(got1), flat(send1))
        later_at = demand(later, rank_later, rest, held_at)
        send2 = gather(later_at.reshape(-1), *parts, got_late, outgoing).reshape((n_row, rest) + one)
        got2, every = pl.pallas_call(
            functools.partial(last_kernel, n_row, nz),
            out_shape=(jax.ShapeDtypeStruct((n_row, rest) + one, dtype),
                       jax.ShapeDtypeStruct((n_col, entries) + one, dtype)),
            in_specs=[ANY, ANY], out_specs=(ANY, ANY),
            scratch_shapes=[DMA((n_row,)), DMA((n_row,))] + [DMA((nz,))] * 6,
            compiler_params=remote_params(number + 3),
        )(send2, filtered)
        found2 = jnp.where(
            now_all[r], found1,
            2 * n_row * cap1 + line * rest + rank_later[r] + jnp.where(line == r, n_row * rest, 0))
        place3 = ws[:, :, None] * n_col + gs[:, :, None]
        groups = jnp.arange(n_col, dtype=i32)[None, None, :]
        left_at = jnp.where(groups == c, n_col * entries + place3, groups * entries + place3).reshape(-1)
        count = windows * n_col * n_col
        return pl.pallas_call(
            cubed_kernel,
            out_shape=jax.ShapeDtypeStruct((windows * block, gcols * block), dtype),
            in_specs=[SMEM] * 4 + [ANY] * 6, out_specs=VMEM,
            scratch_shapes=[pltpu.VMEM((count,) + one, dtype), pltpu.VMEM((count,) + one, dtype),
                            pltpu.VMEM((entries,) + one, dtype),
                            pltpu.VMEM((windows, gcols) + one, jnp.float32), DMA((3,))],
            compiler_params=pltpu.CompilerParams(vmem_limit_bytes=BIG),
        )(left_at, found2[targets_mine], cubed_target, square_target.reshape(-1), flat(every), filtered,
          flat(got1), flat(send1), flat(got2), flat(send2))

    most_demand = windows * n_col * n_col
    early, most, limit = 7 * pool // 32, 10 * entries // 16, most_demand // 8
    small = (early, 22 * most_demand // 128)
    middle = (26 * pool // 64, most_demand // 4)
    share = shares(early, limit)
    most_pool, most_urgent = (wanted > 0).sum(axis=1).max(), urgent_count.max()
    first_out = pooled(0, early)
    parts = [lax.dynamic_index_in_dim(first_out, z, 0, keepdims=False)]
    for by in range(1, nz):
        moved = lax.dynamic_index_in_dim(first_out, (z + by) % nz, 0, keepdims=False)
        parts.append(lax.ppermute(moved, "col", [(i, (i + 2 * by) % n_col) for i in range(n_col)]))
    late_out = pooled(early, middle[0])
    opened = opening(early, most, limit, share, parts)

    def usual(caps, number):
        return run(early, caps[0], caps[1], share, parts, opened, late_out, number)

    def widest(number):
        every_share = shares(pool, limit)
        outgoing = pooled(0, pool)
        got = pl.pallas_call(
            functools.partial(first_kernel, nz, pool),
            out_shape=jax.ShapeDtypeStruct((nz, pool) + one, dtype),
            in_specs=[ANY], out_specs=ANY,
            scratch_shapes=[DMA((nz,)), DMA((nz,))],
            compiler_params=remote_params(number),
        )(outgoing)
        held = [lax.dynamic_index_in_dim(outgoing, z, 0, keepdims=False)]
        held += [lax.dynamic_index_in_dim(got, (z - by + nz) % nz, 0, keepdims=False) for by in range(1, nz)]
        return run(pool, 1, min(most_demand, nb, n_col * slots), every_share, held,
                   opening(pool, entries, limit, every_share, held), outgoing, number)

    def fits(caps):
        return ((most_pool <= early + caps[0]) & (most_urgent <= early)
                & (most_inner <= most) & (share[-1] <= caps[1]))

    choice = jnp.where(fits(small), 0, jnp.where(fits(middle), 1, 2))
    return lax.switch(choice, [lambda: usual(small, 1), lambda: usual(middle, 5), lambda: widest(9)])


F32, BF16, I32 = jnp.float32, jnp.bfloat16, jnp.int32
LANES = 128
SHIFTED = 5
META = 16
ROWS = 40
STAGE = (0, 32, 64, 128)


def log2(n):
    return n.bit_length() - 1


def iota(shape, dim):
    return lax.broadcasted_iota(I32, shape, dim)


def ones(mask):
    return jnp.where(mask, 1.0, 0.0).astype(F32)


def times(a, b):
    return lax.dot_general(a.astype(BF16), b.astype(BF16), (((1,), (0,)), ((), ())), preferred_element_type=F32)


def against(a, b):
    return lax.dot_general(a.astype(BF16), b.astype(BF16), (((1,), (1,)), ((), ())), preferred_element_type=F32)


def most(column):
    return jnp.max(column, axis=0, keepdims=True)


def plan(spread, keep, r, c, sizes, tiers):
    n_row, n_col, slots, windows, gcols, nb = sizes
    nz = n_col // 2
    z, k = c // 2, lax.rem(c, 2)
    devices = n_row * n_col
    total = devices * slots
    per_band = slots // n_row
    out = {}
    lane = iota((1, total), 1)
    label = spread[n_col:n_col + 1, :].astype(I32)
    band = (lane >> log2(per_band)) & (n_row - 1)
    row_id = gcols * (band + n_row * (label >> log2(gcols))) + (label & (gcols - 1))
    row_id = jnp.where(label < 2 * gcols, row_id, nb)
    holds = ones(iota((nb, total), 0) == row_id)
    sub = iota((META, total), 0)
    device = ((lane >> log2(slots)) & (n_row - 1)) * n_col + (lane >> log2(slots * n_row))
    fields = jnp.where(sub == n_col, device >> log2(n_col), 0)
    fields = jnp.where(sub == n_col + 1, (device & (n_col - 1)) >> 1, fields)
    fields = jnp.where(sub == n_col + 2, device & 1, fields)
    fields = jnp.where(sub == n_col + 3, lane & (slots - 1), fields)
    info = against(jnp.where(sub < n_col, spread, fields.astype(F32)), holds)
    line, plane, core, slot = [info[n_col + i:n_col + i + 1, :] for i in range(4)]
    column = jnp.zeros((1, nb), F32)
    for g in range(n_col):
        column = jnp.where(c == g, info[g:g + 1, :], column)
    within = iota((gcols, nb), 0).astype(F32)
    graph = jnp.concatenate([ones(info[g:g + 1, :] == within) for g in range(n_col)], axis=0).astype(BF16)
    upper = ones(iota((nb, nb), 0) < iota((nb, nb), 1)).astype(BF16)

    sub, row = iota((META, nb), 0), iota((META, nb), 1)
    wsel = ones((sub < n_row * windows) & (row == gcols * (sub >> log2(windows)) + (sub & (windows - 1))))
    once = against(wsel, graph)
    twice = against(once, graph)
    each = iota((1, nb), 1)
    soon, late = [], []
    for q in range(n_row):
        inner = sum(once[windows * q + i:windows * q + i + 1, :] for i in range(windows))
        target = sum(twice[windows * q + i:windows * q + i + 1, :] for i in range(windows))
        is_window = ((each >> log2(gcols)) == q) & ((each & (gcols - 1)) < windows)
        s = jnp.where(is_window, 1.0, ones(inner > 0.5))
        soon.append(s)
        late.append(ones(target > 0.5) * (1.0 - s))
    urgent = ones(sum(soon) > 0.5)
    need = ones(sum(soon) + sum(late) > 0.5)

    chip = (line * nz + plane).astype(I32)
    on_chip = ones(sub == chip)
    soon_mask, late_mask = on_chip * urgent, on_chip * (need - urgent)
    soon_count = jnp.sum(soon_mask, axis=1, keepdims=True)
    late_count = jnp.sum(late_mask, axis=1, keepdims=True)
    most_soon = most(soon_count)
    first = jnp.full((1, 1), float(tiers[-1]["n"][0]), F32)
    for tier in reversed(tiers):
        first = jnp.where(most_soon <= float(tier["n"][0]), float(tier["n"][0]), first)

    chips = (META, META)
    left, right = iota(chips, 0), iota(chips, 1)
    load = jnp.broadcast_to(soon_count + late_count, (META, LANES))
    level = times(ones((left & (nz - 1)) == (right & (nz - 1))), load)
    level = most(jnp.floor((level + (n_row - 1.0)) * (1.0 / n_row)))
    taken = jnp.zeros_like(load)
    moves = []
    for d in range(1, n_row):
        spare = jnp.maximum(jnp.minimum(level - load, level - first - taken), 0.0)
        reach = ones(right == ((((left >> log2(nz)) + d) & (n_row - 1)) << log2(nz)) + (left & (nz - 1)))
        back = ones(right == ((((left >> log2(nz)) + n_row - d) & (n_row - 1)) << log2(nz)) + (left & (nz - 1)))
        move = jnp.minimum(jnp.minimum(jnp.maximum(load - level, 0.0), float(SHIFTED)), times(reach, spare))
        arrived = times(back, move)
        load, taken = load - move + arrived, taken + arrived
        moves.append(move[:, 0:1])
    taken = taken[:, 0:1]
    stay = late_count - sum(moves)
    kept = soon_count + stay
    most_pool = most(jnp.where(taken > 0.5, jnp.maximum(kept, first) + taken, kept))
    late_rank = jnp.sum(on_chip * times(late_mask, upper), axis=0, keepdims=True)
    below = jnp.sum(on_chip * stay, axis=0, keepdims=True)
    is_late = need - urgent
    moved, entry, carrier = jnp.zeros((1, nb), F32), jnp.zeros((1, nb), F32), line
    for d in range(1, n_row):
        above = below + jnp.sum(on_chip * moves[d - 1], axis=0, keepdims=True)
        hit = is_late * ones((late_rank >= below) & (late_rank < above))
        moved = moved + hit
        entry = entry + hit * ((d - 1) * SHIFTED + late_rank - below)
        carrier = carrier + hit * d
        below = above
    carrier = jnp.where(carrier >= n_row, carrier - n_row, carrier)
    home = chip
    chip = (carrier * nz + plane).astype(I32)
    on_chip_now = ones(sub == chip)
    rank = jnp.where(urgent > 0.5, times(soon_mask, upper), soon_count + times(late_mask, upper))
    came = jnp.maximum(kept, first) + times(on_chip_now * moved, upper)
    spot = jnp.where(moved > 0.5, jnp.sum(on_chip_now * came, axis=0, keepdims=True),
                     jnp.sum(on_chip * rank, axis=0, keepdims=True))
    spot = jnp.where(need > 0.5, spot, 999.0)
    line = carrier
    m1 = tiers[0]["m"][1]

    sender, getter = sub >> log2(n_row), sub & (n_row - 1)
    soon_pair, late_pair = jnp.zeros((META, nb), F32), jnp.zeros((META, nb), F32)
    for q in range(n_row):
        soon_pair = jnp.where(getter == q, soon[q], soon_pair)
        late_pair = jnp.where(getter == q, late[q], late_pair)
    from_line = ones((sender == line.astype(I32)) & (sender != getter))
    soon_pair, late_pair = soon_pair * from_line, late_pair * from_line
    soon_sum = jnp.sum(soon_pair, axis=1, keepdims=True)
    at0 = times(soon_pair, upper)
    can = late_pair * ones(spot < first)
    at1 = times(can, upper)
    in1 = can * ones(at1 < float(m1))
    rest = late_pair * (1.0 - in1)
    at2 = times(rest, upper)
    most_line, most_rest = most(soon_sum), most(jnp.sum(rest, axis=1, keepdims=True))
    key = jnp.where(rest > 0.5, STAGE[2] + at2, -1.0)
    key = jnp.where(in1 > 0.5, STAGE[1] + at1, key)
    key = jnp.where(soon_pair > 0.5, at0, key)

    choice = jnp.full((1, 1), len(tiers), I32)
    for t in reversed(range(len(tiers))):
        n, m = tiers[t]["n"], tiers[t]["m"]
        fits = ((first == float(n[0])) & (most_soon <= float(n[0])) & (most_pool <= float(sum(n)))
                & (most_line <= float(m[0])) & (most_rest <= float(m[2])))
        choice = jnp.where(fits, t, choice)
    out[33] = jnp.broadcast_to(choice, (1, LANES))

    wide = iota((LANES, nb), 0)
    col = iota((LANES, nb), 1)
    step = z.astype(F32) - plane
    step = jnp.where(step < 0, step + nz, step)
    mine = ones(chip == (r * nz + z))
    pack = ones(wide.astype(F32) == jnp.where(mine > 0.5, spot, 999.0))
    from_slot = slot + slots * ones(core != k.astype(F32))
    given = jnp.where((moved > 0.5) & (home == (r * nz + z)), entry, -1.0)
    slot_rows = jnp.where(sub == 0, from_slot, 0.0)
    out[34] = against(slot_rows, ones(wide.astype(F32) == given))[0:1, :].astype(I32)
    from_slot = jnp.where(moved > 0.5, 2.0 * slots + entry, from_slot)
    rows = jnp.where(sub == 0, from_slot, jnp.where(sub == 1, step, jnp.where(sub == 2, spot, 0.0)))
    rows = jnp.minimum(rows, 127.0)
    out[0] = against(rows, pack)[0:1, :].astype(I32)
    for d in range(1, n_row):
        pair = r * n_row + lax.rem(r + d, n_row)
        key_of = jnp.sum(jnp.where(sub == pair, key, 0.0), axis=0, keepdims=True)
        got = against(rows, ones(wide.astype(F32) == key_of))
        out[d] = (64.0 * got[1:2, :] + got[2:3, :]).astype(I32)

    key_in = jnp.sum(jnp.where((sender == line.astype(I32)) & (getter == r), key, 0.0), axis=0, keepdims=True)
    away = r.astype(F32) - line
    away = jnp.where(away < 0, away + n_row, away)
    where_a = jnp.where(away == 0, step, nz - 1 + away)
    where_b = jnp.clip(jnp.where(away == 0, spot, key_in), 0.0, 127.0)
    fields = jnp.where(sub == 0, where_a, jnp.where(sub == 1, where_b, jnp.where(sub == 2, column, 0.0)))

    def location(found):
        return (128.0 * found[0:1, :] + found[1:2, :]).astype(I32)

    start = gcols * r
    group = col >> log2(gcols)
    out[32] = location(against(fields, ones((wide < windows) & (col == start + wide))))
    entries, count = windows * n_col, windows * n_col * n_col
    inner = against(ones(col == start + (wide >> log2(n_col))), graph)
    inner = inner * ones((group == (wide & (n_col - 1))) & (wide < entries))
    found = against(fields, inner)
    out[15] = location(found)
    lane_at = found[2:3, :]
    sub_at = jnp.sum(inner * column, axis=1, keepdims=True)
    here, there = iota((LANES, LANES), 0), iota((LANES, LANES), 1)
    same = ones((sub_at == lane_at) & ((here >> log2(n_col)) == (there >> log2(n_col)))
                & (here < entries) & (there < entries))
    leads = ones(jnp.sum(same * ones(there < here), axis=1, keepdims=True) < 0.5) * ones(here[:, 0:1] < entries)
    keeps = jnp.zeros((LANES, gcols), F32)
    tag = iota((LANES, gcols), 0) >> log2(n_col)
    for i in range(windows):
        keeps = jnp.where(tag == i, keep[i:i + 1, :].astype(F32), keeps)
    kept = jnp.sum(keeps * ones(iota((LANES, gcols), 1).astype(F32) == sub_at), axis=1, keepdims=True)
    out[16] = (same * leads * kept)[0:entries, :].astype(I32)
    place = gcols * (here[:, 0:1] >> log2(n_col)).astype(F32) + sub_at
    at = ones(place == there.astype(F32)) * leads
    out[13] = jnp.sum(at * here.astype(F32), axis=0, keepdims=True).astype(I32)
    out[14] = jnp.sum(at, axis=0, keepdims=True).astype(I32)

    inner = against(ones(col == start + (wide >> log2(n_col * n_col))), graph)
    inner = inner * ones(group == ((wide >> log2(n_col)) & (n_col - 1)))
    target = against(inner, graph) * ones(group == (wide & (n_col - 1)))
    found = against(fields, target)
    sub_at = gcols * (here[:, 0:1] >> log2(n_col * n_col)).astype(F32) + jnp.sum(target * column, axis=1, keepdims=True)
    lane_at = gcols * (there[0:1, :] >> log2(n_col * n_col)).astype(F32) + found[2:3, :]
    ahead = ones(sub_at == lane_at) * ones(there < here)
    order = jnp.sum(ones(lane_at < sub_at) + ahead, axis=1, keepdims=True)
    put = ones(order == there.astype(F32))
    narrow = iota((META, LANES), 0)
    got = times(jnp.where(narrow == 3, iota((META, LANES), 1).astype(F32), found), put)
    out[8] = location(got)
    out[9] = got[3:4, :].astype(I32)
    follows = ones(jnp.sum(ahead, axis=1, keepdims=True) > 0.5)
    out[10] = jnp.sum(put * follows, axis=0, keepdims=True).astype(I32)
    out[11] = (jnp.sum(ones(sub_at <= there.astype(F32)), axis=0, keepdims=True) - 1.0).astype(I32)
    out[12] = jnp.minimum(jnp.sum(ones(sub_at == there.astype(F32)), axis=0, keepdims=True), 1.0).astype(I32)
    return out


def plan_kernel(sizes, tiers, labels, cols, keep, owned, index, sibling, tile, line_tiles, group, tiles, send, recv,
                col_send, col_recv, pair_send, pair_recv):
    n_row, n_col, slots = sizes[:3]
    r, c = lax.axis_index("row"), lax.axis_index("col")
    z, k = c // 2, lax.rem(c, 2)
    mate = (r, 2 * z + 1 - k)
    lines = [(lax.rem(r + step, n_row), c) for step in range(1, n_row)]
    others = [(r, lax.rem(c + step, n_col)) for step in range(1, n_col)]
    barrier = pltpu.get_barrier_semaphore()
    for to in lines + others:
        pl.semaphore_signal(barrier, inc=1, device_id=to, device_id_type=MESH)
    rows = jnp.concatenate([cols[...].astype(F32), jnp.zeros((META - n_col, slots), F32)], axis=0)
    rows = jnp.where(iota((META, slots), 0) == n_col, labels[...].astype(F32), rows)
    tile[...] = times(rows, ones(iota((slots, LANES), 0) + slots * r == iota((slots, LANES), 1))).astype(BF16)
    pl.semaphore_wait(barrier, n_row + n_col - 2)
    pair = pltpu.make_async_remote_copy(
        src_ref=owned.at[:, :, 1 - k], dst_ref=sibling, send_sem=pair_send, recv_sem=pair_recv, device_id=mate,
        device_id_type=MESH)
    pair.start()
    copies = [send_to(tile, line_tiles.at[r], (send, recv), step, to) for step, to in enumerate(lines)]
    for copy in copies:
        copy.start()
    line_tiles[r] = tile[...]
    for copy in copies:
        copy.wait()
    group[...] = sum(line_tiles[q].astype(F32) for q in range(n_row)).astype(BF16)
    copies = [send_to(group, tiles.at[c], (col_send, col_recv), step, to) for step, to in enumerate(others)]
    for copy in copies:
        copy.start()
    tiles[c] = group[...]
    for copy in copies:
        copy.wait()
    spread = jnp.concatenate([tiles[q].astype(F32) for q in range(n_col)], axis=1)
    index[...] = jnp.zeros_like(index)
    for row, value in plan(spread, keep[...], r, c, sizes, tiers).items():
        index[row:row + value.shape[0], :] = value
    pair.wait()


def main_kernel(sizes, tier, index, owned, sibling, out, pool, bsend, brecv, zsend0, zsend1, zall0, zall1,
                xsend0, xsend1, xsend2, xrecv0, xrecv1, xrecv2, lefts, parts, every0, every1, rights, sums, sems, zs, zr, xs, xr,
                ls, lr, us, ur, ds, dr, ps, pr, bs, br):
    n_row, n_col, slots, windows, gcols, nb = sizes
    nz = n_col // 2
    entries, count = windows * n_col, windows * n_col * n_col
    block = out.shape[0] // windows
    r, c = lax.axis_index("row"), lax.axis_index("col")
    z, k = c // 2, lax.rem(c, 2)
    zsend, zall = (zsend0, zsend1), (zall0, zall1)
    every = (every0, every1)
    xsend, xrecv = (xsend0, xsend1, xsend2), (xrecv0, xrecv1, xrecv2)
    n, m = tier["n"], tier["m"]
    bounds = [0, n[0], n[0] + n[1]]
    others = [(r, 2 * lax.rem(z + step, nz) + k) for step in range(1, nz)]
    lines = [(lax.rem(r + step, n_row), c) for step in range(1, n_row)]
    mate = (r, 2 * z + 1 - k)
    above, below = others[0], others[-1]
    loads = [pltpu.make_async_copy(owned.at[:, :, k], pool.at[pl.ds(0, slots)], sems.at[0]),
             pltpu.make_async_copy(sibling, pool.at[pl.ds(slots, slots)], sems.at[1])]
    for load in loads:
        load.start()
    greet(others + lines + [mate])
    for load in loads:
        load.wait()

    def bpack():
        for i in range((n_row - 1) * SHIFTED):
            slot = index[34, i]
            for other in range(nz):
                bsend[i * nz + other] = pool[slot, other]

    def bcopies():
        size = SHIFTED * nz
        return [pltpu.make_async_remote_copy(
            src_ref=bsend.at[pl.ds((d - 1) * size, size)], dst_ref=brecv.at[pl.ds((d - 1) * size, size)],
            send_sem=bs.at[d], recv_sem=br.at[d], device_id=lines[d - 1], device_id_type=MESH)
            for d in range(1, n_row)]

    def zpack(s):
        def body(p, carry):
            slot = index[0, bounds[s] + p]
            own = slot < 2 * slots
            for step in range(nz):
                to = lax.rem(z + step, nz)
                if s == 0:
                    value = pool[slot, to]
                else:
                    value = lax.select(own, pool[jnp.where(own, slot, 0), to],
                                       brecv[jnp.where(own, 0, slot - 2 * slots) * nz + to])
                if step == 0:
                    zall[s][p] = value
                else:
                    zsend[s][(step - 1) * n[s] + p] = value
            return carry

        lax.fori_loop(0, n[s], body, 0)

    def zcopies(s):
        return [pltpu.make_async_remote_copy(
            src_ref=zsend[s].at[pl.ds((step - 1) * n[s], n[s])], dst_ref=zall[s].at[pl.ds(step * n[s], n[s])],
            send_sem=zs.at[s * nz + step], recv_sem=zr.at[s * nz + step], device_id=others[step - 1],
            device_id_type=MESH) for step in range(1, nz)]

    def from_z(step, spot, upto, value):
        for s in upto:
            inside = (step >= 0) & (spot >= bounds[s]) & (spot < bounds[s + 1])
            got = zall[s][jnp.where(inside, step * n[s] + spot - bounds[s], 0)]
            value = got if value is None else lax.select(inside, got, value)
        return value

    def from_x(away, key, upto, value):
        for s in upto:
            inside = (away >= 0) & (key >= STAGE[s]) & (key < STAGE[s] + m[s])
            got = xrecv[s][jnp.where(inside, away * m[s] + key - STAGE[s], 0)]
            value = lax.select(inside, got, value)
        return value

    def fetch(code, zupto, xupto, value=None):
        a, b = code // 128, lax.rem(code, 128)
        value = from_z(jnp.where(a < nz, a, -1), b, zupto, value)
        return from_x(jnp.where(a < nz, -1, a - nz), b, xupto, value)

    def xpack(s):
        ready = [0, 1] if s == 2 else [0]

        for d in range(1, n_row):
            def body(q, carry):
                code = index[d, STAGE[s] + q]
                xsend[s][(d - 1) * m[s] + q] = from_z(code // 64, lax.rem(code, 64), ready, None)
                return carry

            lax.fori_loop(0, m[s], body, 0)

    def xcopies(s):
        return [pltpu.make_async_remote_copy(
            src_ref=xsend[s].at[pl.ds((d - 1) * m[s], m[s])], dst_ref=xrecv[s].at[pl.ds((d - 1) * m[s], m[s])],
            send_sem=xs.at[s * n_row + d], recv_sem=xr.at[s * n_row + d], device_id=lines[d - 1],
            device_id_type=MESH) for d in range(1, n_row)]

    def start(copies):
        for copy in copies:
            copy.start()

    def arrive(copies):
        for copy in copies:
            copy.wait_recv()

    def left_send(sem, source, to):
        slab = lefts.at[source]
        return pltpu.make_async_remote_copy(
            src_ref=slab, dst_ref=slab, send_sem=ls.at[sem], recv_sem=lr.at[sem], device_id=to, device_id_type=MESH)

    offsets = [0, nz * n[0], nz * (n[0] + n[1]), nz * (n[0] + n[1]) + (n_row - 1) * m[0]]

    def kept(at, source):
        return pltpu.make_async_copy(source, rights.at[pl.ds(offsets[at], source.shape[0])], sems.at[2 + at])

    def keep(at, source):
        kept(at, source).start()

    zpack(0)
    start(zcopies(0))
    bpack()
    start(bcopies())
    arrive(bcopies())
    zpack(1)
    arrive(zcopies(0))
    start(zcopies(1))
    keep(0, zall0)
    xpack(0)
    start(xcopies(0))
    xpack(1)
    arrive(xcopies(0))
    keep(2, xrecv0)
    for i in range(windows):
        lefts[c, i] = fetch(index[32, i], [0], [0])
    left_out = [left_send(step, c, to) for step, to in enumerate(others)]
    left_pair = [left_send(nz, c, mate)]
    start(left_out)
    start(left_pair)
    start(xcopies(1))
    for step in range(1, nz):
        left_out[step - 1].wait_recv()
        left_pair.append(left_send(nz + step, 2 * lax.rem(z - step + nz, nz) + k, mate))
        left_pair[-1].start()
    arrive(left_pair)

    def square(e, carry):
        right = fetch(index[15, e], [0], [0])
        left = lefts[lax.rem(e, n_col), e // n_col]
        parts[e] = jnp.dot(left, right, preferred_element_type=F32)
        return carry

    def merge(w):
        def body(g, carry):
            e = w * n_col + g
            total = parts[w * n_col] * index[16 + e, w * n_col].astype(F32)
            for i in range(1, n_col):
                total += parts[w * n_col + i] * index[16 + e, w * n_col + i].astype(F32)
            every[w][c, g] = total.astype(BF16)
            return carry

        lax.fori_loop(0, n_col, body, 0)

    def pass_on(sem, half, step, place, to):
        slab = every[half].at[place]
        return pltpu.make_async_remote_copy(
            src_ref=slab, dst_ref=slab, send_sem=sem[0].at[half * nz + step], recv_sem=sem[1].at[half * nz + step],
            device_id=to, device_id_type=MESH)

    def up(half, step):
        return pass_on((us, ur), half, step, 2 * lax.rem(z - step + nz, nz) + k, above)

    def down(half, step):
        return pass_on((ds, dr), half, step, 2 * lax.rem(z + step, nz) + k, below)

    def across(half, step):
        return pass_on((ps, pr), half, step, 2 * lax.rem(z + step, nz) + k, mate)

    def relay(half, step):
        @pl.when(z - step >= 0)
        def _():
            up(half, step - 1).wait_recv()

        @pl.when((z - step >= 0) & (z < nz - 1))
        def _():
            up(half, step).start()

        @pl.when(z - step >= 0)
        def _():
            across(half, nz - step).start()

        @pl.when(z + step <= nz - 1)
        def _():
            down(half, step - 1).wait_recv()

        @pl.when((z + step <= nz - 1) & (z > 0))
        def _():
            down(half, step).start()

        @pl.when(z + step <= nz - 1)
        def _():
            across(half, step).start()

    def first_pass(half):
        @pl.when(z < nz - 1)
        def _():
            up(half, 0).start()

        @pl.when(z > 0)
        def _():
            down(half, 0).start()

        across(half, 0).start()

    for w in range(windows):
        lax.fori_loop(w * n_col, (w + 1) * n_col, square, 0)
        merge(w)
        first_pass(w)
    arrive(zcopies(1))
    xpack(2)
    start(xcopies(2))
    keep(1, zall1)
    arrive(xcopies(1))
    keep(3, xrecv1)
    for step in range(1, nz):
        for w in range(windows):
            if (w, step) != (windows - 1, nz - 1):
                relay(w, step)

    def right_of(code):
        a, b = code // 128, lax.rem(code, 128)
        d = a - nz
        near = jnp.where(b < n[0], a * n[0] + b, offsets[1] + a * n[1] + b - n[0])
        far = jnp.where(b < STAGE[1], offsets[2] + d * m[0] + b, offsets[3] + d * m[1] + b - STAGE[1])
        last = (d >= 0) & (b >= STAGE[2])
        value = rights[jnp.where(last, 0, jnp.where(d < 0, near, far))]
        return lax.select(last, xrecv2[jnp.where(last, d * m[2] + b - STAGE[2], 0)], value)

    def finish(w):
        for step in range(nz):
            across(w, step).wait_recv()
        if w == 0:
            arrive(xcopies(2))
            for at, source in enumerate((zall0, zall1, xrecv0, xrecv1)):
                kept(at, source).wait()
        each = count // windows

        def multiply(q, acc):
            for i in range(8):
                t = w * each + q * 8 + i
                p = index[9, t]
                term = jnp.dot(every[w][lax.rem(p, n_col), lax.rem(p // n_col, n_col)], right_of(index[8, t]),
                               preferred_element_type=F32)
                acc = acc * index[10, t].astype(F32) + term
                sums[t] = acc
            return acc

        lax.fori_loop(0, each // 8, multiply, jnp.zeros((block, block), F32))

        def write(j, carry):
            at = w * gcols + j
            cube = sums[jnp.maximum(index[11, at], 0)] * (-2.0 * index[12, at].astype(F32))
            own = every[w][c, jnp.maximum(index[13, at] - w * n_col, 0)].astype(F32) * (3.0 * index[14, at].astype(F32))
            out[w * block:(w + 1) * block, pl.ds(pl.multiple_of(j * block, block), block)] = (own + cube).astype(BF16)
            return carry

        lax.fori_loop(0, gcols, write, 0)

    for w in range(windows):
        if w == windows - 1:
            relay(w, nz - 1)
        finish(w)
    for copies in (bcopies(), zcopies(0), zcopies(1), xcopies(0), xcopies(1), xcopies(2), left_out, left_pair):
        for copy in copies:
            copy.wait_send()
    for w in range(windows):
        for step in range(nz):
            @pl.when((z - step >= 0) & (z < nz - 1))
            def _(w=w, step=step):
                up(w, step).wait_send()

            @pl.when((z + step <= nz - 1) & (z > 0))
            def _(w=w, step=step):
                down(w, step).wait_send()

            across(w, step).wait_send()


TIERS = (dict(n=(9, 10), m=(9, 14, 18)), dict(n=(9, 18), m=(11, 14, 26)), dict(n=(11, 8), m=(11, 14, 18)),
         dict(n=(11, 16), m=(11, 14, 26)), dict(n=(14, 22), m=(14, 14, 30)))


def local(owned_blocks, owned_rows, owned_cols, keep):
    n_row, n_col = lax.axis_size("row"), lax.axis_size("col")
    nz = n_col // 2
    slots = owned_rows.shape[0]
    windows, gcols = keep.shape
    nb = gcols * n_col
    block = owned_blocks.shape[-1]
    one = (block, block)
    dtype = owned_blocks.dtype
    entries, count = windows * n_col, windows * n_col * n_col
    if (count > LANES or n_col > 8 or n_row > 4 or entries > 16 or nz > 4 or n_row * slots != LANES or 2 * slots > 64
            or windows * gcols > LANES or n_row < 2 or nz < 2 or windows != 2):
        return general(owned_blocks, owned_rows, owned_cols, keep)
    sizes = (n_row, n_col, slots, windows, gcols, nb)
    halves = owned_blocks.reshape((slots, nz, 2) + one)
    index, sibling = pl.pallas_call(
        functools.partial(plan_kernel, sizes, TIERS),
        out_shape=(jax.ShapeDtypeStruct((ROWS, LANES), I32), jax.ShapeDtypeStruct((slots, nz) + one, dtype)),
        in_specs=[VMEM, VMEM, VMEM, ANY], out_specs=(VMEM, ANY),
        scratch_shapes=[pltpu.VMEM((META, LANES), BF16), pltpu.VMEM((n_row, META, LANES), BF16),
                        pltpu.VMEM((META, LANES), BF16), pltpu.VMEM((n_col, META, LANES), BF16),
                        DMA((n_row,)), DMA((n_row,)), DMA((n_col,)), DMA((n_col,)), DMA, DMA],
        compiler_params=pltpu.CompilerParams(collective_id=20, has_side_effects=True, vmem_limit_bytes=BIG),
    )(owned_rows[None, :], owned_cols.T, keep, halves)

    def quick(t):
        n, m = TIERS[t]["n"], TIERS[t]["m"]
        scratch = [pltpu.VMEM((2 * slots, nz) + one, dtype)]
        scratch += [pltpu.VMEM(((n_row - 1) * SHIFTED * nz,) + one, dtype)] * 2
        scratch += [pltpu.VMEM(((nz - 1) * q,) + one, dtype) for q in n]
        scratch += [pltpu.VMEM((nz * q,) + one, dtype) for q in n]
        scratch += [pltpu.VMEM(((n_row - 1) * q,) + one, dtype) for q in m] * 2
        scratch += [pltpu.VMEM((n_col, windows) + one, dtype), pltpu.VMEM((entries,) + one, F32),
                    pltpu.VMEM((n_col, n_col) + one, dtype), pltpu.VMEM((n_col, n_col) + one, dtype),
                    pltpu.VMEM((nz * sum(n) + (n_row - 1) * (m[0] + m[1]),) + one, dtype),
                    pltpu.VMEM((count,) + one, F32), DMA((6,))]
        scratch += [DMA((2 * nz,))] * 2 + [DMA((3 * n_row,))] * 2 + [DMA((2 * nz,))] * 2
        scratch += [DMA((windows * nz,))] * 6 + [DMA((n_row,))] * 2
        return pl.pallas_call(
            functools.partial(main_kernel, sizes, TIERS[t]),
            out_shape=jax.ShapeDtypeStruct((windows * block, gcols * block), dtype),
            in_specs=[SMEM, ANY, ANY], out_specs=VMEM, scratch_shapes=scratch,
            compiler_params=pltpu.CompilerParams(
                collective_id=21 + t, has_side_effects=True, vmem_limit_bytes=BIG),
        )(index, halves, sibling)

    branches = [functools.partial(quick, t) for t in range(len(TIERS))]
    branches.append(lambda: general(owned_blocks, owned_rows, owned_cols, keep))
    return lax.switch(index[33, 0], branches)


def solution(mesh):
    placed = (
        P(("row", "col"), None, None, None),
        P(("row", "col")),
        P(("row", "col"), None),
        P("row", "col"),
    )
    return jax.shard_map(
        local, mesh=mesh, in_specs=placed, out_specs=P("row", "col"), check_vma=False
    )
```

```python
import functools

import jax
import jax.numpy as jnp
from jax import lax
from jax.experimental import pallas as pl
from jax.experimental.pallas import tpu as pltpu
from jax.sharding import PartitionSpec as P

MESH = pl.DeviceIdType.MESH
ANY = pl.BlockSpec(memory_space=pl.ANY)
SMEM = pl.BlockSpec(memory_space=pltpu.SMEM)
VMEM = pl.BlockSpec(memory_space=pltpu.VMEM)
DMA = pltpu.SemaphoreType.DMA
BIG = 60 * 1024 * 1024


def remote_params(number):
    return pltpu.CompilerParams(collective_id=number, has_side_effects=True)


def spread_kernel(n_row, n_col, meta, owned, meta_all, sibling, send, recv, pair_send, pair_recv):
    r, c = lax.axis_index("row"), lax.axis_index("col")
    me = r * n_col + c
    devices = n_row * n_col
    barrier = pltpu.get_barrier_semaphore()

    def greet(i, carry):
        d = lax.rem(me + i, devices)
        pl.semaphore_signal(barrier, inc=1, device_id=(d // n_col, lax.rem(d, n_col)), device_id_type=MESH)
        return carry

    lax.fori_loop(1, devices, greet, 0)
    pl.semaphore_wait(barrier, devices - 1)
    z, k = c // 2, lax.rem(c, 2)
    other = 1 - k
    pair = pltpu.make_async_remote_copy(
        src_ref=owned.at[:, :, other], dst_ref=sibling, send_sem=pair_send, recv_sem=pair_recv,
        device_id=(r, 2 * z + other), device_id_type=MESH)
    pair.start()

    def copy_to(i):
        d = lax.rem(me + i, devices)
        return pltpu.make_async_remote_copy(
            src_ref=meta, dst_ref=meta_all.at[me], send_sem=send.at[i], recv_sem=recv.at[i],
            device_id=(d // n_col, lax.rem(d, n_col)), device_id_type=MESH)

    def begin(i, carry):
        copy_to(i).start()
        return carry

    def finish(i, carry):
        copy_to(i).wait()
        return carry

    lax.fori_loop(1, devices, begin, 0)
    lax.fori_loop(1, devices, finish, 0)
    pair.wait()


def greet(partners):
    barrier = pltpu.get_barrier_semaphore()
    for partner in partners:
        pl.semaphore_signal(barrier, inc=1, device_id=partner, device_id_type=MESH)
    pl.semaphore_wait(barrier, len(partners))


def send_to(source, dest, sems, step, partner):
    return pltpu.make_async_remote_copy(
        src_ref=source, dst_ref=dest, send_sem=sems[0].at[step], recv_sem=sems[1].at[step],
        device_id=partner, device_id_type=MESH)


def place_of(nz):
    r, c = lax.axis_index("row"), lax.axis_index("col")
    z, k = c // 2, lax.rem(c, 2)
    return r, c, z, k, [(r, 2 * lax.rem(z + step, nz) + k) for step in range(1, nz)]


def first_kernel(nz, count, source, got, send, recv):
    r, c, z, k, others = place_of(nz)
    greet(others)
    copies = [send_to(source.at[to[1] // 2, pl.ds(0, count)], got.at[z], (send, recv), step, to)
              for step, to in enumerate(others)]
    for copy in copies:
        copy.start()
    for copy in copies:
        copy.wait()


def second_kernel(n_row, nz, source, wanted, got, plane_got, send, recv, psend, precv):
    r, c, z, k, others = place_of(nz)
    lines = [(lax.rem(r + step, n_row), c) for step in range(1, n_row)]
    greet(others + lines)
    count = got.shape[1]
    copies = [send_to(wanted.at[to[0]], plane_got.at[r], (psend, precv), step, to) for step, to in enumerate(lines)]
    copies += [send_to(source.at[to[1] // 2, pl.ds(0, count)], got.at[z], (send, recv), step, to)
               for step, to in enumerate(others)]
    for copy in copies:
        copy.start()
    for copy in copies:
        copy.wait()


def left_kernel(nz, piece, got, send, recv, psend, precv):
    r, c, z, k, others = place_of(nz)
    mate = (r, 2 * z + 1 - k)
    greet(others + [mate])
    copies = [send_to(piece, got.at[c], (send, recv), step, to) for step, to in enumerate(others)]
    for copy in copies:
        copy.start()
    pairs = [send_to(piece, got.at[c], (psend, precv), 0, mate)]
    pairs[0].start()
    for step in range(1, nz):
        copies[step - 1].wait_recv()
        origin = 2 * lax.rem(z - step + nz, nz) + k
        pairs.append(send_to(got.at[origin], got.at[origin], (psend, precv), step, mate))
        pairs[-1].start()
    for copy in copies:
        copy.wait_send()
    for pair in pairs:
        pair.wait()


def last_kernel(n_row, nz, wanted, filtered, plane_got, every, send, recv, up_send, up_recv, down_send, down_recv,
                psend, precv):
    r, c, z, k, others = place_of(nz)
    mate = (r, 2 * z + 1 - k)
    lines = [(lax.rem(r + step, n_row), c) for step in range(1, n_row)]
    above, below = (r, 2 * lax.rem(z + 1, nz) + k), (r, 2 * lax.rem(z + nz - 1, nz) + k)
    greet(lines + [above, below, mate])
    plane = [send_to(wanted.at[to[0]], plane_got.at[r], (send, recv), step, to) for step, to in enumerate(lines)]

    def up(step, own):
        block = every.at[2 * lax.rem(z - step + nz, nz) + k]
        return send_to(filtered if own else block, block, (up_send, up_recv), step, above)

    def down(step, own):
        block = every.at[2 * lax.rem(z + step, nz) + k]
        return send_to(filtered if own else block, block, (down_send, down_recv), step, below)

    def across(step, own):
        block = every.at[2 * lax.rem(z + step, nz) + k]
        return send_to(filtered if own else block, block, (psend, precv), step, mate)

    @pl.when(z < nz - 1)
    def _():
        up(0, True).start()

    @pl.when(z > 0)
    def _():
        down(0, True).start()

    across(0, True).start()
    for copy in plane:
        copy.start()
    for step in range(1, nz):
        @pl.when(z - step >= 0)
        def _():
            up(step - 1, False).wait_recv()
            across(nz - step, False).start()

        @pl.when((z - step >= 0) & (z < nz - 1))
        def _():
            up(step, False).start()

        @pl.when(z + step <= nz - 1)
        def _():
            down(step - 1, False).wait_recv()
            across(step, False).start()

        @pl.when((z + step <= nz - 1) & (z > 0))
        def _():
            down(step, False).start()
    for step in range(nz):
        @pl.when((z - step >= 0) & (z < nz - 1))
        def _():
            up(step, False).wait_send()

        @pl.when((z + step <= nz - 1) & (z > 0))
        def _():
            down(step, False).wait_send()
    for step in range(nz):
        across(step, False).wait()
    for copy in plane:
        copy.wait()


def pick(sources, index, dest, sem):
    start = 0
    for source in sources:
        stop = start + source.shape[0]

        @pl.when((index >= start) & (index < stop))
        def _(source=source, start=start):
            pltpu.make_async_copy(source.at[index - start], dest, sem).start()

        start = stop


def gather_kernel(index, *refs):
    sources, (out, sem) = refs[:-2], refs[-2:]
    start = pl.program_id(0) * out.shape[0]

    def begin(i, carry):
        pick(sources, index[start + i], out.at[i], sem)
        return carry

    lax.fori_loop(0, out.shape[0], begin, 0)
    pltpu.make_async_copy(out, out, sem).wait()


def flat(array):
    return array.reshape((-1,) + array.shape[-2:])


def gather(index, *sources):
    block = sources[0].shape[-2:]
    count = index.shape[0]
    chunk = max(n for n in range(1, min(count, 512) + 1) if count % n == 0)
    return pl.pallas_call(
        gather_kernel,
        grid=(count // chunk,),
        out_shape=jax.ShapeDtypeStruct((count,) + block, sources[0].dtype),
        in_specs=[SMEM] + [ANY] * len(sources), out_specs=pl.BlockSpec((chunk,) + block, lambda i: (i, 0, 0)),
        scratch_shapes=[DMA],
        compiler_params=pltpu.CompilerParams(vmem_limit_bytes=BIG),
    )(index, *[flat(source) for source in sources])


def square_kernel(left_at, right_at, slot, keep, lefts, own_left, rights, own_rights, out, a, b, acc, sems):
    count = out.shape[0]

    def begin(i, carry):
        pick((lefts, own_left), left_at[i], a.at[i], sems.at[0])
        pick((rights, own_rights), right_at[i], b.at[i], sems.at[1])
        return carry

    lax.fori_loop(0, count, begin, 0)
    acc[...] = jnp.zeros_like(acc)
    pltpu.make_async_copy(a, a, sems.at[0]).wait()
    pltpu.make_async_copy(b, b, sems.at[1]).wait()

    def multiply(q, carry):
        ids = [q * 4 + i for i in range(4)]
        terms = [jnp.dot(a[i], b[i], preferred_element_type=jnp.float32) for i in ids]
        for i, term in zip(ids, terms):
            acc[slot[i]] += term
        return carry

    lax.fori_loop(0, count // 4, multiply, 0)

    def write(i, carry):
        out[i] = (acc[i] * keep[i].astype(jnp.float32)).astype(out.dtype)
        return carry

    lax.fori_loop(0, count, write, 0)


def cubed_kernel(left_at, right_at, target, own_target, every, own, got1, send1, got2, send2, out, a, b, f, acc, sems):
    count = a.shape[0]
    windows = acc.shape[0]
    block = a.shape[-1]
    per_window = count // windows
    own_per_window = f.shape[0] // windows
    mine = pltpu.make_async_copy(own, f, sems.at[2])
    mine.start()

    def begin(i, carry):
        pick((every, own), left_at[i], a.at[i], sems.at[0])
        pick((got1, send1, got2, send2), right_at[i], b.at[i], sems.at[1])
        return carry

    lax.fori_loop(0, count, begin, 0)
    acc[...] = jnp.zeros_like(acc)
    mine.wait()
    for w in range(windows):
        def add(i, carry):
            e = w * own_per_window + i
            acc[w, own_target[e]] -= 1.5 * f[e].astype(jnp.float32)
            return carry

        lax.fori_loop(0, own_per_window, add, 0)
    pltpu.make_async_copy(a, a, sems.at[0]).wait()
    pltpu.make_async_copy(b, b, sems.at[1]).wait()
    for w in range(windows):
        def multiply(q, carry):
            ids = [w * per_window + q * 4 + i for i in range(4)]
            terms = [jnp.dot(a[i], b[i], preferred_element_type=jnp.float32) for i in ids]
            for i, term in zip(ids, terms):
                acc[w, target[i]] += term
            return carry

        lax.fori_loop(0, per_window // 4, multiply, 0)
    for w in range(windows):
        for j in range(acc.shape[1]):
            out[w * block:(w + 1) * block, j * block:(j + 1) * block] = (-2.0 * acc[w, j]).astype(out.dtype)


def running(mask):
    n = mask.shape[-1]
    before = (jnp.arange(n)[:, None] < jnp.arange(n)[None, :]).astype(jnp.bfloat16)
    lines = mask.reshape(-1, n).astype(jnp.bfloat16)
    return jnp.dot(lines, before, preferred_element_type=jnp.float32).astype(jnp.int32).reshape(mask.shape)


def general(owned_blocks, owned_rows, owned_cols, keep):
    n_row, n_col = lax.axis_size("row"), lax.axis_size("col")
    devices = n_row * n_col
    nz = n_col // 2
    r, c = lax.axis_index("row"), lax.axis_index("col")
    z, k = c // 2, lax.rem(c, 2)
    block = owned_blocks.shape[-1]
    dtype = owned_blocks.dtype
    slots = owned_rows.shape[0]
    per_band = slots // n_row
    windows, gcols = keep.shape
    nb = gcols * n_col
    size = slots * (1 + n_col)
    tall = -(-size // 1024) * 8
    one = (block, block)
    chips = devices // 2
    pool = 2 * slots
    i32 = jnp.int32

    packed = jnp.concatenate([owned_rows[:, None], owned_cols], axis=1).reshape(-1)
    meta = jnp.pad(packed, (0, tall * 128 - size)).reshape(tall, 128)
    meta_all, sibling = pl.pallas_call(
        functools.partial(spread_kernel, n_row, n_col),
        out_shape=(jax.ShapeDtypeStruct((devices, tall, 128), i32),
                   jax.ShapeDtypeStruct((slots, nz) + one, dtype)),
        in_specs=[ANY, ANY], out_specs=(ANY, ANY),
        scratch_shapes=[DMA((devices,)), DMA((devices,)), DMA, DMA],
        compiler_params=remote_params(0),
    )(meta, owned_blocks.reshape((slots, nz, 2) + one))
    me = r * n_col + c
    is_me = jnp.arange(devices)[:, None] == me
    labels = jnp.where(is_me, packed[None, :], meta_all.reshape(devices, -1)[:, :size])
    labels = labels.reshape(devices * slots, 1 + n_col)
    rows, cols = labels[:, 0], labels[:, 1:]
    slot_ids = jnp.arange(devices * slots, dtype=i32)
    every_row = jnp.arange(nb, dtype=i32)
    filled = rows < gcols * 2
    row_id = jnp.where(filled, gcols * (slot_ids // per_band % n_row + n_row * (rows // gcols)) + rows % gcols, nb)
    holder = jnp.sum(jnp.where(row_id[None, :] == every_row[:, None], slot_ids[None, :], 0), axis=1)
    row_cols = cols[holder]
    chip = holder // pool
    line, plane = chip // nz, chip % nz

    base = gcols * jnp.arange(n_col, dtype=i32)
    window = gcols * jnp.arange(n_row, dtype=i32)[:, None] + jnp.arange(windows, dtype=i32)[None, :]
    inner = base + row_cols[window]
    targets = base + row_cols[inner]
    is_window = jnp.any(window[:, :, None] == every_row, axis=1)
    is_inner = jnp.any(inner.reshape(n_row, -1, 1) == every_row, axis=1) & ~is_window
    is_target = jnp.any(targets.reshape(n_row, -1, 1) == every_row, axis=1) & ~is_inner & ~is_window
    urgent = jnp.any(is_window | is_inner, axis=0)
    wanted_row = urgent.astype(i32) + jnp.any(is_window | is_inner | is_target, axis=0).astype(i32)
    wanted = jnp.sum(jnp.where(row_id[:, None] == every_row[None, :], wanted_row[None, :], 0), axis=1).reshape(chips, pool)
    urgent_count = (wanted == 2).sum(axis=1)
    place = jnp.where(wanted == 2, running(wanted == 2), urgent_count[:, None] + running(wanted == 1))
    place = jnp.where(wanted > 0, place, pool)
    spot = place.reshape(-1)[holder]
    on_line = line[None, :] == jnp.arange(n_row, dtype=i32)[:, None]

    def ranks(need):
        both = need[:, None, :] & on_line[None, :, :]
        rank = jnp.sum(jnp.where(both, running(both), 0), axis=1)
        return rank, both.sum(axis=2).max()

    rank_window, _ = ranks(is_window)
    rank_inner, most_inner = ranks(is_inner)

    def shares(early, limit):
        now = is_target & (spot < early)[None, :]
        rank_now, _ = ranks(now)
        now = now & (rank_now < limit)
        later = is_target & ~now
        rank_later, most_later = ranks(later)
        return now, rank_now, later, rank_later, most_later

    inner_mine = inner[r].reshape(-1)
    targets_mine = targets[r].reshape(-1)
    cols_mine = lax.dynamic_index_in_dim(row_cols, c, 1, keepdims=False)
    square_target = cols_mine[inner_mine].reshape(windows, n_col)
    same = square_target[:, :, None] == square_target[:, None, :]
    first = jnp.argmax(same, axis=2).astype(i32)
    square_slot = (first + n_col * jnp.arange(windows, dtype=i32)[:, None]).reshape(-1)
    kept = jnp.take_along_axis(keep, square_target, axis=1).reshape(-1)
    cubed_target = cols_mine[targets_mine]
    entries = windows * n_col

    step = (z - plane + nz) % nz
    zs = jnp.arange(nz, dtype=i32)[:, None]
    place_mine = lax.dynamic_index_in_dim(place, r * nz + z, 0, keepdims=False)

    def pooled(start, count):
        position = start + jnp.arange(count, dtype=i32)
        pick_slot = jnp.sum(
            jnp.where(place_mine[None, :] == position[:, None], jnp.arange(pool, dtype=i32)[None, :], 0), axis=1)
        at = pick_slot[None, :] % slots
        index = jnp.where(
            pick_slot[None, :] // slots == k, at * n_col + 2 * zs + k, slots * n_col + at * nz + zs)
        return gather(index.reshape(-1), owned_blocks, sibling).reshape((nz, count) + one)

    def demand(need, rank, count, source_at):
        sending = need & (line == r)[None, :]
        chosen = sending[:, None, :] & (rank[:, None, :] == jnp.arange(count, dtype=i32)[None, :, None])
        return jnp.sum(jnp.where(chosen, source_at[None, None, :], 0), axis=2)

    def opening(early, most, limit, share, parts):
        now, rank_now = share[:2]
        cap1 = windows + most + limit
        now_all = is_window | is_inner | now
        now_rank = jnp.where(is_window, rank_window, jnp.where(is_inner, windows + rank_inner, windows + most + rank_now))
        send1 = gather(demand(now_all, now_rank, cap1, step * early + spot).reshape(-1), *parts)
        found1 = line * cap1 + now_rank[r] + jnp.where(line == r, n_row * cap1, 0)
        return now_all, found1, send1.reshape((n_row, cap1) + one)

    def run(early, late, rest, share, parts, opened, outgoing, number):
        later, rank_later = share[2:4]
        now_all, found1, send1 = opened
        cap1 = send1.shape[1]
        late_at = jnp.where(plane == z, nz * late + plane * outgoing.shape[1], plane * late)
        held_at = jnp.where(spot < early, step * early + spot, nz * early + late_at + spot - early)
        got_late, got1 = pl.pallas_call(
            functools.partial(second_kernel, n_row, nz),
            out_shape=(jax.ShapeDtypeStruct((nz, late) + one, dtype),
                       jax.ShapeDtypeStruct((n_row, cap1) + one, dtype)),
            in_specs=[ANY, ANY], out_specs=(ANY, ANY),
            scratch_shapes=[DMA((nz,)), DMA((nz,)), DMA((n_row,)), DMA((n_row,))],
            compiler_params=remote_params(number + 1),
        )(outgoing, send1)
        window_mine = gcols * r + jnp.arange(windows, dtype=i32)
        left_mine = gather(found1[window_mine], got1, send1)
        lefts = pl.pallas_call(
            functools.partial(left_kernel, nz),
            out_shape=jax.ShapeDtypeStruct((n_col, windows) + one, dtype),
            in_specs=[ANY], out_specs=ANY,
            scratch_shapes=[DMA((nz,))] * 4,
            compiler_params=remote_params(number + 2),
        )(left_mine)
        ws = jnp.arange(windows, dtype=i32)[:, None]
        gs = jnp.arange(n_col, dtype=i32)[None, :]
        left_at = jnp.where(gs == c, n_col * windows + ws, gs * windows + ws).reshape(-1)
        filtered = pl.pallas_call(
            square_kernel,
            out_shape=jax.ShapeDtypeStruct((entries,) + one, dtype),
            in_specs=[SMEM] * 4 + [ANY] * 4, out_specs=VMEM,
            scratch_shapes=[pltpu.VMEM((entries,) + one, dtype), pltpu.VMEM((entries,) + one, dtype),
                            pltpu.VMEM((entries,) + one, jnp.float32), DMA((2,))],
            compiler_params=pltpu.CompilerParams(vmem_limit_bytes=BIG),
        )(left_at, found1[inner_mine], square_slot, kept, flat(lefts), left_mine, flat(got1), flat(send1))
        later_at = demand(later, rank_later, rest, held_at)
        send2 = gather(later_at.reshape(-1), *parts, got_late, outgoing).reshape((n_row, rest) + one)
        got2, every = pl.pallas_call(
            functools.partial(last_kernel, n_row, nz),
            out_shape=(jax.ShapeDtypeStruct((n_row, rest) + one, dtype),
                       jax.ShapeDtypeStruct((n_col, entries) + one, dtype)),
            in_specs=[ANY, ANY], out_specs=(ANY, ANY),
            scratch_shapes=[DMA((n_row,)), DMA((n_row,))] + [DMA((nz,))] * 6,
            compiler_params=remote_params(number + 3),
        )(send2, filtered)
        found2 = jnp.where(
            now_all[r], found1,
            2 * n_row * cap1 + line * rest + rank_later[r] + jnp.where(line == r, n_row * rest, 0))
        place3 = ws[:, :, None] * n_col + gs[:, :, None]
        groups = jnp.arange(n_col, dtype=i32)[None, None, :]
        left_at = jnp.where(groups == c, n_col * entries + place3, groups * entries + place3).reshape(-1)
        count = windows * n_col * n_col
        return pl.pallas_call(
            cubed_kernel,
            out_shape=jax.ShapeDtypeStruct((windows * block, gcols * block), dtype),
            in_specs=[SMEM] * 4 + [ANY] * 6, out_specs=VMEM,
            scratch_shapes=[pltpu.VMEM((count,) + one, dtype), pltpu.VMEM((count,) + one, dtype),
                            pltpu.VMEM((entries,) + one, dtype),
                            pltpu.VMEM((windows, gcols) + one, jnp.float32), DMA((3,))],
            compiler_params=pltpu.CompilerParams(vmem_limit_bytes=BIG),
        )(left_at, found2[targets_mine], cubed_target, square_target.reshape(-1), flat(every), filtered,
          flat(got1), flat(send1), flat(got2), flat(send2))

    most_demand = windows * n_col * n_col
    early, most, limit = 7 * pool // 32, 10 * entries // 16, most_demand // 8
    small = (early, 22 * most_demand // 128)
    middle = (26 * pool // 64, most_demand // 4)
    share = shares(early, limit)
    most_pool, most_urgent = (wanted > 0).sum(axis=1).max(), urgent_count.max()
    first_out = pooled(0, early)
    parts = [lax.dynamic_index_in_dim(first_out, z, 0, keepdims=False)]
    for by in range(1, nz):
        moved = lax.dynamic_index_in_dim(first_out, (z + by) % nz, 0, keepdims=False)
        parts.append(lax.ppermute(moved, "col", [(i, (i + 2 * by) % n_col) for i in range(n_col)]))
    late_out = pooled(early, middle[0])
    opened = opening(early, most, limit, share, parts)

    def usual(caps, number):
        return run(early, caps[0], caps[1], share, parts, opened, late_out, number)

    def widest(number):
        every_share = shares(pool, limit)
        outgoing = pooled(0, pool)
        got = pl.pallas_call(
            functools.partial(first_kernel, nz, pool),
            out_shape=jax.ShapeDtypeStruct((nz, pool) + one, dtype),
            in_specs=[ANY], out_specs=ANY,
            scratch_shapes=[DMA((nz,)), DMA((nz,))],
            compiler_params=remote_params(number),
        )(outgoing)
        held = [lax.dynamic_index_in_dim(outgoing, z, 0, keepdims=False)]
        held += [lax.dynamic_index_in_dim(got, (z - by + nz) % nz, 0, keepdims=False) for by in range(1, nz)]
        return run(pool, 1, min(most_demand, nb, n_col * slots), every_share, held,
                   opening(pool, entries, limit, every_share, held), outgoing, number)

    def fits(caps):
        return ((most_pool <= early + caps[0]) & (most_urgent <= early)
                & (most_inner <= most) & (share[-1] <= caps[1]))

    choice = jnp.where(fits(small), 0, jnp.where(fits(middle), 1, 2))
    return lax.switch(choice, [lambda: usual(small, 1), lambda: usual(middle, 5), lambda: widest(9)])


F32, BF16, I32 = jnp.float32, jnp.bfloat16, jnp.int32
LANES = 128
SHIFTED = 5
META = 16
ROWS = 40
STAGE = (0, 32, 64, 128)


def log2(n):
    return n.bit_length() - 1


def iota(shape, dim):
    return lax.broadcasted_iota(I32, shape, dim)


def ones(mask):
    return jnp.where(mask, 1.0, 0.0).astype(F32)


def times(a, b):
    return lax.dot_general(a.astype(BF16), b.astype(BF16), (((1,), (0,)), ((), ())), preferred_element_type=F32)


def against(a, b):
    return lax.dot_general(a.astype(BF16), b.astype(BF16), (((1,), (1,)), ((), ())), preferred_element_type=F32)


def most(column):
    return jnp.max(column, axis=0, keepdims=True)


def plan(spread, keep, r, c, sizes, tiers):
    n_row, n_col, slots, windows, gcols, nb = sizes
    nz = n_col // 2
    z, k = c // 2, lax.rem(c, 2)
    devices = n_row * n_col
    total = devices * slots
    per_band = slots // n_row
    out = {}
    lane = iota((1, total), 1)
    label = spread[n_col:n_col + 1, :].astype(I32)
    band = (lane >> log2(per_band)) & (n_row - 1)
    row_id = gcols * (band + n_row * (label >> log2(gcols))) + (label & (gcols - 1))
    row_id = jnp.where(label < 2 * gcols, row_id, nb)
    holds = ones(iota((nb, total), 0) == row_id)
    sub = iota((META, total), 0)
    device = ((lane >> log2(slots)) & (n_row - 1)) * n_col + (lane >> log2(slots * n_row))
    fields = jnp.where(sub == n_col, device >> log2(n_col), 0)
    fields = jnp.where(sub == n_col + 1, (device & (n_col - 1)) >> 1, fields)
    fields = jnp.where(sub == n_col + 2, device & 1, fields)
    fields = jnp.where(sub == n_col + 3, lane & (slots - 1), fields)
    info = against(jnp.where(sub < n_col, spread, fields.astype(F32)), holds)
    line, plane, core, slot = [info[n_col + i:n_col + i + 1, :] for i in range(4)]
    column = jnp.zeros((1, nb), F32)
    for g in range(n_col):
        column = jnp.where(c == g, info[g:g + 1, :], column)
    within = iota((gcols, nb), 0).astype(F32)
    graph = jnp.concatenate([ones(info[g:g + 1, :] == within) for g in range(n_col)], axis=0).astype(BF16)
    upper = ones(iota((nb, nb), 0) < iota((nb, nb), 1)).astype(BF16)

    sub, row = iota((META, nb), 0), iota((META, nb), 1)
    wsel = ones((sub < n_row * windows) & (row == gcols * (sub >> log2(windows)) + (sub & (windows - 1))))
    once = against(wsel, graph)
    twice = against(once, graph)
    each = iota((1, nb), 1)
    soon, late = [], []
    for q in range(n_row):
        inner = sum(once[windows * q + i:windows * q + i + 1, :] for i in range(windows))
        target = sum(twice[windows * q + i:windows * q + i + 1, :] for i in range(windows))
        is_window = ((each >> log2(gcols)) == q) & ((each & (gcols - 1)) < windows)
        s = jnp.where(is_window, 1.0, ones(inner > 0.5))
        soon.append(s)
        late.append(ones(target > 0.5) * (1.0 - s))
    urgent = ones(sum(soon) > 0.5)
    need = ones(sum(soon) + sum(late) > 0.5)

    chip = (line * nz + plane).astype(I32)
    on_chip = ones(sub == chip)
    soon_mask, late_mask = on_chip * urgent, on_chip * (need - urgent)
    soon_count = jnp.sum(soon_mask, axis=1, keepdims=True)
    late_count = jnp.sum(late_mask, axis=1, keepdims=True)
    most_soon = most(soon_count)
    first = jnp.full((1, 1), float(tiers[-1]["n"][0]), F32)
    for tier in reversed(tiers):
        first = jnp.where(most_soon <= float(tier["n"][0]), float(tier["n"][0]), first)

    chips = (META, META)
    left, right = iota(chips, 0), iota(chips, 1)
    load = jnp.broadcast_to(soon_count + late_count, (META, LANES))
    level = times(ones((left & (nz - 1)) == (right & (nz - 1))), load)
    level = most(jnp.floor((level + (n_row - 1.0)) * (1.0 / n_row)))
    taken = jnp.zeros_like(load)
    moves = []
    for d in range(1, n_row):
        spare = jnp.maximum(jnp.minimum(level - load, level - first - taken), 0.0)
        reach = ones(right == ((((left >> log2(nz)) + d) & (n_row - 1)) << log2(nz)) + (left & (nz - 1)))
        back = ones(right == ((((left >> log2(nz)) + n_row - d) & (n_row - 1)) << log2(nz)) + (left & (nz - 1)))
        move = jnp.minimum(jnp.minimum(jnp.maximum(load - level, 0.0), float(SHIFTED)), times(reach, spare))
        arrived = times(back, move)
        load, taken = load - move + arrived, taken + arrived
        moves.append(move[:, 0:1])
    taken = taken[:, 0:1]
    stay = late_count - sum(moves)
    kept = soon_count + stay
    most_pool = most(jnp.where(taken > 0.5, jnp.maximum(kept, first) + taken, kept))
    late_rank = jnp.sum(on_chip * times(late_mask, upper), axis=0, keepdims=True)
    below = jnp.sum(on_chip * stay, axis=0, keepdims=True)
    is_late = need - urgent
    moved, entry, carrier = jnp.zeros((1, nb), F32), jnp.zeros((1, nb), F32), line
    for d in range(1, n_row):
        above = below + jnp.sum(on_chip * moves[d - 1], axis=0, keepdims=True)
        hit = is_late * ones((late_rank >= below) & (late_rank < above))
        moved = moved + hit
        entry = entry + hit * ((d - 1) * SHIFTED + late_rank - below)
        carrier = carrier + hit * d
        below = above
    carrier = jnp.where(carrier >= n_row, carrier - n_row, carrier)
    home = chip
    chip = (carrier * nz + plane).astype(I32)
    on_chip_now = ones(sub == chip)
    rank = jnp.where(urgent > 0.5, times(soon_mask, upper), soon_count + times(late_mask, upper))
    came = jnp.maximum(kept, first) + times(on_chip_now * moved, upper)
    spot = jnp.where(moved > 0.5, jnp.sum(on_chip_now * came, axis=0, keepdims=True),
                     jnp.sum(on_chip * rank, axis=0, keepdims=True))
    spot = jnp.where(need > 0.5, spot, 999.0)
    line = carrier
    m1 = tiers[0]["m"][1]

    sender, getter = sub >> log2(n_row), sub & (n_row - 1)
    soon_pair, late_pair = jnp.zeros((META, nb), F32), jnp.zeros((META, nb), F32)
    for q in range(n_row):
        soon_pair = jnp.where(getter == q, soon[q], soon_pair)
        late_pair = jnp.where(getter == q, late[q], late_pair)
    from_line = ones((sender == line.astype(I32)) & (sender != getter))
    soon_pair, late_pair = soon_pair * from_line, late_pair * from_line
    soon_sum = jnp.sum(soon_pair, axis=1, keepdims=True)
    at0 = times(soon_pair, upper)
    can = late_pair * ones(spot < first)
    at1 = times(can, upper)
    in1 = can * ones(at1 < float(m1))
    rest = late_pair * (1.0 - in1)
    at2 = times(rest, upper)
    most_line, most_rest = most(soon_sum), most(jnp.sum(rest, axis=1, keepdims=True))
    key = jnp.where(rest > 0.5, STAGE[2] + at2, -1.0)
    key = jnp.where(in1 > 0.5, STAGE[1] + at1, key)
    key = jnp.where(soon_pair > 0.5, at0, key)

    choice = jnp.full((1, 1), len(tiers), I32)
    for t in reversed(range(len(tiers))):
        n, m = tiers[t]["n"], tiers[t]["m"]
        fits = ((first == float(n[0])) & (most_soon <= float(n[0])) & (most_pool <= float(sum(n)))
                & (most_line <= float(m[0])) & (most_rest <= float(m[2])))
        choice = jnp.where(fits, t, choice)
    out[33] = jnp.broadcast_to(choice, (1, LANES))

    wide = iota((LANES, nb), 0)
    col = iota((LANES, nb), 1)
    step = z.astype(F32) - plane
    step = jnp.where(step < 0, step + nz, step)
    mine = ones(chip == (r * nz + z))
    pack = ones(wide.astype(F32) == jnp.where(mine > 0.5, spot, 999.0))
    from_slot = slot + slots * ones(core != k.astype(F32))
    given = jnp.where((moved > 0.5) & (home == (r * nz + z)), entry, -1.0)
    slot_rows = jnp.where(sub == 0, from_slot, 0.0)
    out[34] = against(slot_rows, ones(wide.astype(F32) == given))[0:1, :].astype(I32)
    from_slot = jnp.where(moved > 0.5, 2.0 * slots + entry, from_slot)
    rows = jnp.where(sub == 0, from_slot, jnp.where(sub == 1, step, jnp.where(sub == 2, spot, 0.0)))
    rows = jnp.minimum(rows, 127.0)
    out[0] = against(rows, pack)[0:1, :].astype(I32)
    for d in range(1, n_row):
        pair = r * n_row + lax.rem(r + d, n_row)
        key_of = jnp.sum(jnp.where(sub == pair, key, 0.0), axis=0, keepdims=True)
        got = against(rows, ones(wide.astype(F32) == key_of))
        out[d] = (64.0 * got[1:2, :] + got[2:3, :]).astype(I32)

    key_in = jnp.sum(jnp.where((sender == line.astype(I32)) & (getter == r), key, 0.0), axis=0, keepdims=True)
    away = r.astype(F32) - line
    away = jnp.where(away < 0, away + n_row, away)
    where_a = jnp.where(away == 0, step, nz - 1 + away)
    where_b = jnp.clip(jnp.where(away == 0, spot, key_in), 0.0, 127.0)
    fields = jnp.where(sub == 0, where_a, jnp.where(sub == 1, where_b, jnp.where(sub == 2, column, 0.0)))

    def location(found):
        return (128.0 * found[0:1, :] + found[1:2, :]).astype(I32)

    start = gcols * r
    group = col >> log2(gcols)
    out[32] = location(against(fields, ones((wide < windows) & (col == start + wide))))
    entries, count = windows * n_col, windows * n_col * n_col
    inner = against(ones(col == start + (wide >> log2(n_col))), graph)
    inner = inner * ones((group == (wide & (n_col - 1))) & (wide < entries))
    found = against(fields, inner)
    out[15] = location(found)
    lane_at = found[2:3, :]
    sub_at = jnp.sum(inner * column, axis=1, keepdims=True)
    here, there = iota((LANES, LANES), 0), iota((LANES, LANES), 1)
    same = ones((sub_at == lane_at) & ((here >> log2(n_col)) == (there >> log2(n_col)))
                & (here < entries) & (there < entries))
    leads = ones(jnp.sum(same * ones(there < here), axis=1, keepdims=True) < 0.5) * ones(here[:, 0:1] < entries)
    keeps = jnp.zeros((LANES, gcols), F32)
    tag = iota((LANES, gcols), 0) >> log2(n_col)
    for i in range(windows):
        keeps = jnp.where(tag == i, keep[i:i + 1, :].astype(F32), keeps)
    kept = jnp.sum(keeps * ones(iota((LANES, gcols), 1).astype(F32) == sub_at), axis=1, keepdims=True)
    out[16] = (same * leads * kept)[0:entries, :].astype(I32)
    place = gcols * (here[:, 0:1] >> log2(n_col)).astype(F32) + sub_at
    at = ones(place == there.astype(F32)) * leads
    out[13] = jnp.sum(at * here.astype(F32), axis=0, keepdims=True).astype(I32)
    out[14] = jnp.sum(at, axis=0, keepdims=True).astype(I32)

    inner = against(ones(col == start + (wide >> log2(n_col * n_col))), graph)
    inner = inner * ones(group == ((wide >> log2(n_col)) & (n_col - 1)))
    target = against(inner, graph) * ones(group == (wide & (n_col - 1)))
    found = against(fields, target)
    sub_at = gcols * (here[:, 0:1] >> log2(n_col * n_col)).astype(F32) + jnp.sum(target * column, axis=1, keepdims=True)
    lane_at = gcols * (there[0:1, :] >> log2(n_col * n_col)).astype(F32) + found[2:3, :]
    ahead = ones(sub_at == lane_at) * ones(there < here)
    order = jnp.sum(ones(lane_at < sub_at) + ahead, axis=1, keepdims=True)
    put = ones(order == there.astype(F32))
    narrow = iota((META, LANES), 0)
    got = times(jnp.where(narrow == 3, iota((META, LANES), 1).astype(F32), found), put)
    out[8] = location(got)
    out[9] = got[3:4, :].astype(I32)
    follows = ones(jnp.sum(ahead, axis=1, keepdims=True) > 0.5)
    out[10] = jnp.sum(put * follows, axis=0, keepdims=True).astype(I32)
    out[11] = (jnp.sum(ones(sub_at <= there.astype(F32)), axis=0, keepdims=True) - 1.0).astype(I32)
    out[12] = jnp.minimum(jnp.sum(ones(sub_at == there.astype(F32)), axis=0, keepdims=True), 1.0).astype(I32)
    return out


def plan_kernel(sizes, tiers, labels, cols, keep, owned, index, sibling, tile, line_tiles, group, tiles, send, recv,
                col_send, col_recv, pair_send, pair_recv):
    n_row, n_col, slots = sizes[:3]
    r, c = lax.axis_index("row"), lax.axis_index("col")
    z, k = c // 2, lax.rem(c, 2)
    mate = (r, 2 * z + 1 - k)
    lines = [(lax.rem(r + step, n_row), c) for step in range(1, n_row)]
    others = [(r, lax.rem(c + step, n_col)) for step in range(1, n_col)]
    barrier = pltpu.get_barrier_semaphore()
    for to in lines + others:
        pl.semaphore_signal(barrier, inc=1, device_id=to, device_id_type=MESH)
    rows = jnp.concatenate([cols[...].astype(F32), jnp.zeros((META - n_col, slots), F32)], axis=0)
    rows = jnp.where(iota((META, slots), 0) == n_col, labels[...].astype(F32), rows)
    tile[...] = times(rows, ones(iota((slots, LANES), 0) + slots * r == iota((slots, LANES), 1))).astype(BF16)
    pl.semaphore_wait(barrier, n_row + n_col - 2)
    pair = pltpu.make_async_remote_copy(
        src_ref=owned.at[:, :, 1 - k], dst_ref=sibling, send_sem=pair_send, recv_sem=pair_recv, device_id=mate,
        device_id_type=MESH)
    pair.start()
    copies = [send_to(tile, line_tiles.at[r], (send, recv), step, to) for step, to in enumerate(lines)]
    for copy in copies:
        copy.start()
    line_tiles[r] = tile[...]
    for copy in copies:
        copy.wait()
    group[...] = sum(line_tiles[q].astype(F32) for q in range(n_row)).astype(BF16)
    copies = [send_to(group, tiles.at[c], (col_send, col_recv), step, to) for step, to in enumerate(others)]
    for copy in copies:
        copy.start()
    tiles[c] = group[...]
    for copy in copies:
        copy.wait()
    spread = jnp.concatenate([tiles[q].astype(F32) for q in range(n_col)], axis=1)
    index[...] = jnp.zeros_like(index)
    for row, value in plan(spread, keep[...], r, c, sizes, tiers).items():
        index[row:row + value.shape[0], :] = value
    pair.wait()


def main_kernel(sizes, tier, index, owned, sibling, out, pool, bsend, brecv, zsend0, zsend1, zall0, zall1,
                xsend0, xsend1, xsend2, xrecv0, xrecv1, xrecv2, lefts, parts, every0, every1, rights, sums, sems, zs, zr, xs, xr,
                ls, lr, us, ur, ds, dr, ps, pr, bs, br):
    n_row, n_col, slots, windows, gcols, nb = sizes
    nz = n_col // 2
    entries, count = windows * n_col, windows * n_col * n_col
    block = out.shape[0] // windows
    r, c = lax.axis_index("row"), lax.axis_index("col")
    z, k = c // 2, lax.rem(c, 2)
    zsend, zall = (zsend0, zsend1), (zall0, zall1)
    every = (every0, every1)
    xsend, xrecv = (xsend0, xsend1, xsend2), (xrecv0, xrecv1, xrecv2)
    n, m = tier["n"], tier["m"]
    bounds = [0, n[0], n[0] + n[1]]
    others = [(r, 2 * lax.rem(z + step, nz) + k) for step in range(1, nz)]
    lines = [(lax.rem(r + step, n_row), c) for step in range(1, n_row)]
    mate = (r, 2 * z + 1 - k)
    above, below = others[0], others[-1]
    loads = [pltpu.make_async_copy(owned.at[:, :, k], pool.at[pl.ds(0, slots)], sems.at[0]),
             pltpu.make_async_copy(sibling, pool.at[pl.ds(slots, slots)], sems.at[1])]
    for load in loads:
        load.start()
    greet(others + lines + [mate])
    for load in loads:
        load.wait()

    def bpack():
        for i in range((n_row - 1) * SHIFTED):
            slot = index[34, i]
            for other in range(nz):
                bsend[i * nz + other] = pool[slot, other]

    def bcopies():
        size = SHIFTED * nz
        return [pltpu.make_async_remote_copy(
            src_ref=bsend.at[pl.ds((d - 1) * size, size)], dst_ref=brecv.at[pl.ds((d - 1) * size, size)],
            send_sem=bs.at[d], recv_sem=br.at[d], device_id=lines[d - 1], device_id_type=MESH)
            for d in range(1, n_row)]

    def zpack(s):
        def body(p, carry):
            slot = index[0, bounds[s] + p]
            own = slot < 2 * slots
            for step in range(nz):
                to = lax.rem(z + step, nz)
                if s == 0:
                    value = pool[slot, to]
                else:
                    value = lax.select(own, pool[jnp.where(own, slot, 0), to],
                                       brecv[jnp.where(own, 0, slot - 2 * slots) * nz + to])
                if step == 0:
                    zall[s][p] = value
                else:
                    zsend[s][(step - 1) * n[s] + p] = value
            return carry

        lax.fori_loop(0, n[s], body, 0)

    def zcopies(s):
        return [pltpu.make_async_remote_copy(
            src_ref=zsend[s].at[pl.ds((step - 1) * n[s], n[s])], dst_ref=zall[s].at[pl.ds(step * n[s], n[s])],
            send_sem=zs.at[s * nz + step], recv_sem=zr.at[s * nz + step], device_id=others[step - 1],
            device_id_type=MESH) for step in range(1, nz)]

    def from_z(step, spot, upto, value):
        for s in upto:
            inside = (step >= 0) & (spot >= bounds[s]) & (spot < bounds[s + 1])
            got = zall[s][jnp.where(inside, step * n[s] + spot - bounds[s], 0)]
            value = got if value is None else lax.select(inside, got, value)
        return value

    def from_x(away, key, upto, value):
        for s in upto:
            inside = (away >= 0) & (key >= STAGE[s]) & (key < STAGE[s] + m[s])
            got = xrecv[s][jnp.where(inside, away * m[s] + key - STAGE[s], 0)]
            value = lax.select(inside, got, value)
        return value

    def fetch(code, zupto, xupto, value=None):
        a, b = code // 128, lax.rem(code, 128)
        value = from_z(jnp.where(a < nz, a, -1), b, zupto, value)
        return from_x(jnp.where(a < nz, -1, a - nz), b, xupto, value)

    def xpack(s):
        ready = [0, 1] if s == 2 else [0]

        for d in range(1, n_row):
            def body(q, carry):
                code = index[d, STAGE[s] + q]
                xsend[s][(d - 1) * m[s] + q] = from_z(code // 64, lax.rem(code, 64), ready, None)
                return carry

            lax.fori_loop(0, m[s], body, 0)

    def xcopies(s):
        return [pltpu.make_async_remote_copy(
            src_ref=xsend[s].at[pl.ds((d - 1) * m[s], m[s])], dst_ref=xrecv[s].at[pl.ds((d - 1) * m[s], m[s])],
            send_sem=xs.at[s * n_row + d], recv_sem=xr.at[s * n_row + d], device_id=lines[d - 1],
            device_id_type=MESH) for d in range(1, n_row)]

    def start(copies):
        for copy in copies:
            copy.start()

    def arrive(copies):
        for copy in copies:
            copy.wait_recv()

    def left_send(sem, source, to):
        slab = lefts.at[source]
        return pltpu.make_async_remote_copy(
            src_ref=slab, dst_ref=slab, send_sem=ls.at[sem], recv_sem=lr.at[sem], device_id=to, device_id_type=MESH)

    offsets = [0, nz * n[0], nz * (n[0] + n[1]), nz * (n[0] + n[1]) + (n_row - 1) * m[0]]

    def kept(at, source):
        return pltpu.make_async_copy(source, rights.at[pl.ds(offsets[at], source.shape[0])], sems.at[2 + at])

    def keep(at, source):
        kept(at, source).start()

    zpack(0)
    start(zcopies(0))
    bpack()
    start(bcopies())
    arrive(bcopies())
    zpack(1)
    arrive(zcopies(0))
    start(zcopies(1))
    keep(0, zall0)
    xpack(0)
    start(xcopies(0))
    xpack(1)
    arrive(xcopies(0))
    keep(2, xrecv0)
    for i in range(windows):
        lefts[c, i] = fetch(index[32, i], [0], [0])
    left_out = [left_send(step, c, to) for step, to in enumerate(others)]
    left_pair = [left_send(nz, c, mate)]
    start(left_out)
    start(left_pair)
    start(xcopies(1))
    for step in range(1, nz):
        left_out[step - 1].wait_recv()
        left_pair.append(left_send(nz + step, 2 * lax.rem(z - step + nz, nz) + k, mate))
        left_pair[-1].start()
    arrive(left_pair)

    def square(e, carry):
        right = fetch(index[15, e], [0], [0])
        left = lefts[lax.rem(e, n_col), e // n_col]
        parts[e] = jnp.dot(left, right, preferred_element_type=F32)
        return carry

    def merge(w):
        def body(g, carry):
            e = w * n_col + g
            total = parts[w * n_col] * index[16 + e, w * n_col].astype(F32)
            for i in range(1, n_col):
                total += parts[w * n_col + i] * index[16 + e, w * n_col + i].astype(F32)
            every[w][c, g] = total.astype(BF16)
            return carry

        lax.fori_loop(0, n_col, body, 0)

    def pass_on(sem, half, step, place, to):
        slab = every[half].at[place]
        return pltpu.make_async_remote_copy(
            src_ref=slab, dst_ref=slab, send_sem=sem[0].at[half * nz + step], recv_sem=sem[1].at[half * nz + step],
            device_id=to, device_id_type=MESH)

    def up(half, step):
        return pass_on((us, ur), half, step, 2 * lax.rem(z - step + nz, nz) + k, above)

    def down(half, step):
        return pass_on((ds, dr), half, step, 2 * lax.rem(z + step, nz) + k, below)

    def across(half, step):
        return pass_on((ps, pr), half, step, 2 * lax.rem(z + step, nz) + k, mate)

    def relay(half, step):
        @pl.when(z - step >= 0)
        def _():
            up(half, step - 1).wait_recv()

        @pl.when((z - step >= 0) & (z < nz - 1))
        def _():
            up(half, step).start()

        @pl.when(z - step >= 0)
        def _():
            across(half, nz - step).start()

        @pl.when(z + step <= nz - 1)
        def _():
            down(half, step - 1).wait_recv()

        @pl.when((z + step <= nz - 1) & (z > 0))
        def _():
            down(half, step).start()

        @pl.when(z + step <= nz - 1)
        def _():
            across(half, step).start()

    def first_pass(half):
        @pl.when(z < nz - 1)
        def _():
            up(half, 0).start()

        @pl.when(z > 0)
        def _():
            down(half, 0).start()

        across(half, 0).start()

    for w in range(windows):
        lax.fori_loop(w * n_col, (w + 1) * n_col, square, 0)
        merge(w)
        first_pass(w)
    arrive(zcopies(1))
    xpack(2)
    start(xcopies(2))
    keep(1, zall1)
    arrive(xcopies(1))
    keep(3, xrecv1)
    for step in range(1, nz):
        for w in range(windows):
            if (w, step) != (windows - 1, nz - 1):
                relay(w, step)

    def right_of(code):
        a, b = code // 128, lax.rem(code, 128)
        d = a - nz
        near = jnp.where(b < n[0], a * n[0] + b, offsets[1] + a * n[1] + b - n[0])
        far = jnp.where(b < STAGE[1], offsets[2] + d * m[0] + b, offsets[3] + d * m[1] + b - STAGE[1])
        last = (d >= 0) & (b >= STAGE[2])
        value = rights[jnp.where(last, 0, jnp.where(d < 0, near, far))]
        return lax.select(last, xrecv2[jnp.where(last, d * m[2] + b - STAGE[2], 0)], value)

    def finish(w):
        for step in range(nz):
            across(w, step).wait_recv()
        if w == 0:
            arrive(xcopies(2))
            for at, source in enumerate((zall0, zall1, xrecv0, xrecv1)):
                kept(at, source).wait()
        each = count // windows

        def multiply(q, acc):
            for i in range(8):
                t = w * each + q * 8 + i
                p = index[9, t]
                term = jnp.dot(every[w][lax.rem(p, n_col), lax.rem(p // n_col, n_col)], right_of(index[8, t]),
                               preferred_element_type=F32)
                acc = acc * index[10, t].astype(F32) + term
                sums[t] = acc
            return acc

        lax.fori_loop(0, each // 8, multiply, jnp.zeros((block, block), F32))

        def write(j, carry):
            at = w * gcols + j
            cube = sums[jnp.maximum(index[11, at], 0)] * (-2.0 * index[12, at].astype(F32))
            own = every[w][c, jnp.maximum(index[13, at] - w * n_col, 0)].astype(F32) * (3.0 * index[14, at].astype(F32))
            out[w * block:(w + 1) * block, pl.ds(pl.multiple_of(j * block, block), block)] = (own + cube).astype(BF16)
            return carry

        lax.fori_loop(0, gcols, write, 0)

    for w in range(windows):
        if w == windows - 1:
            relay(w, nz - 1)
        finish(w)
    for copies in (bcopies(), zcopies(0), zcopies(1), xcopies(0), xcopies(1), xcopies(2), left_out, left_pair):
        for copy in copies:
            copy.wait_send()
    for w in range(windows):
        for step in range(nz):
            @pl.when((z - step >= 0) & (z < nz - 1))
            def _(w=w, step=step):
                up(w, step).wait_send()

            @pl.when((z + step <= nz - 1) & (z > 0))
            def _(w=w, step=step):
                down(w, step).wait_send()

            across(w, step).wait_send()


TIERS = tuple(dict(n=(a, b), m=(c, 14, d)) for a, b, c, d in (
    (9, 8, 9, 18), (9, 10, 9, 22), (9, 13, 11, 22), (9, 18, 12, 28), (11, 8, 9, 18), (11, 11, 11, 22), (11, 16, 12, 28),
    (14, 12, 12, 24), (14, 22, 14, 30)))


def local(owned_blocks, owned_rows, owned_cols, keep):
    n_row, n_col = lax.axis_size("row"), lax.axis_size("col")
    nz = n_col // 2
    slots = owned_rows.shape[0]
    windows, gcols = keep.shape
    nb = gcols * n_col
    block = owned_blocks.shape[-1]
    one = (block, block)
    dtype = owned_blocks.dtype
    entries, count = windows * n_col, windows * n_col * n_col
    if (count > LANES or n_col > 8 or n_row > 4 or entries > 16 or nz > 4 or n_row * slots != LANES or 2 * slots > 64
            or windows * gcols > LANES or n_row < 2 or nz < 2 or windows != 2):
        return general(owned_blocks, owned_rows, owned_cols, keep)
    sizes = (n_row, n_col, slots, windows, gcols, nb)
    halves = owned_blocks.reshape((slots, nz, 2) + one)
    index, sibling = pl.pallas_call(
        functools.partial(plan_kernel, sizes, TIERS),
        out_shape=(jax.ShapeDtypeStruct((ROWS, LANES), I32), jax.ShapeDtypeStruct((slots, nz) + one, dtype)),
        in_specs=[VMEM, VMEM, VMEM, ANY], out_specs=(VMEM, ANY),
        scratch_shapes=[pltpu.VMEM((META, LANES), BF16), pltpu.VMEM((n_row, META, LANES), BF16),
                        pltpu.VMEM((META, LANES), BF16), pltpu.VMEM((n_col, META, LANES), BF16),
                        DMA((n_row,)), DMA((n_row,)), DMA((n_col,)), DMA((n_col,)), DMA, DMA],
        compiler_params=pltpu.CompilerParams(collective_id=20, has_side_effects=True, vmem_limit_bytes=BIG),
    )(owned_rows[None, :], owned_cols.T, keep, halves)

    def quick(t):
        n, m = TIERS[t]["n"], TIERS[t]["m"]
        scratch = [pltpu.VMEM((2 * slots, nz) + one, dtype)]
        scratch += [pltpu.VMEM(((n_row - 1) * SHIFTED * nz,) + one, dtype)] * 2
        scratch += [pltpu.VMEM(((nz - 1) * q,) + one, dtype) for q in n]
        scratch += [pltpu.VMEM((nz * q,) + one, dtype) for q in n]
        scratch += [pltpu.VMEM(((n_row - 1) * q,) + one, dtype) for q in m] * 2
        scratch += [pltpu.VMEM((n_col, windows) + one, dtype), pltpu.VMEM((entries,) + one, F32),
                    pltpu.VMEM((n_col, n_col) + one, dtype), pltpu.VMEM((n_col, n_col) + one, dtype),
                    pltpu.VMEM((nz * sum(n) + (n_row - 1) * (m[0] + m[1]),) + one, dtype),
                    pltpu.VMEM((count,) + one, F32), DMA((6,))]
        scratch += [DMA((2 * nz,))] * 2 + [DMA((3 * n_row,))] * 2 + [DMA((2 * nz,))] * 2
        scratch += [DMA((windows * nz,))] * 6 + [DMA((n_row,))] * 2
        return pl.pallas_call(
            functools.partial(main_kernel, sizes, TIERS[t]),
            out_shape=jax.ShapeDtypeStruct((windows * block, gcols * block), dtype),
            in_specs=[SMEM, ANY, ANY], out_specs=VMEM, scratch_shapes=scratch,
            compiler_params=pltpu.CompilerParams(
                collective_id=21 + t, has_side_effects=True, vmem_limit_bytes=BIG),
        )(index, halves, sibling)

    branches = [functools.partial(quick, t) for t in range(len(TIERS))]
    branches.append(lambda: general(owned_blocks, owned_rows, owned_cols, keep))
    return lax.switch(index[33, 0], branches)


def solution(mesh):
    placed = (
        P(("row", "col"), None, None, None),
        P(("row", "col")),
        P(("row", "col"), None),
        P("row", "col"),
    )
    return jax.shard_map(
        local, mesh=mesh, in_specs=placed, out_specs=P("row", "col"), check_vma=False
    )
```

```python
import functools

import jax
import jax.numpy as jnp
from jax import lax
from jax.experimental import pallas as pl
from jax.experimental.pallas import tpu as pltpu
from jax.sharding import PartitionSpec as P

MESH = pl.DeviceIdType.MESH
ANY = pl.BlockSpec(memory_space=pl.ANY)
SMEM = pl.BlockSpec(memory_space=pltpu.SMEM)
VMEM = pl.BlockSpec(memory_space=pltpu.VMEM)
DMA = pltpu.SemaphoreType.DMA
BIG = 60 * 1024 * 1024


def remote_params(number):
    return pltpu.CompilerParams(collective_id=number, has_side_effects=True)


def spread_kernel(n_row, n_col, meta, owned, meta_all, sibling, send, recv, pair_send, pair_recv):
    r, c = lax.axis_index("row"), lax.axis_index("col")
    me = r * n_col + c
    devices = n_row * n_col
    barrier = pltpu.get_barrier_semaphore()

    def greet(i, carry):
        d = lax.rem(me + i, devices)
        pl.semaphore_signal(barrier, inc=1, device_id=(d // n_col, lax.rem(d, n_col)), device_id_type=MESH)
        return carry

    lax.fori_loop(1, devices, greet, 0)
    pl.semaphore_wait(barrier, devices - 1)
    z, k = c // 2, lax.rem(c, 2)
    other = 1 - k
    pair = pltpu.make_async_remote_copy(
        src_ref=owned.at[:, :, other], dst_ref=sibling, send_sem=pair_send, recv_sem=pair_recv,
        device_id=(r, 2 * z + other), device_id_type=MESH)
    pair.start()

    def copy_to(i):
        d = lax.rem(me + i, devices)
        return pltpu.make_async_remote_copy(
            src_ref=meta, dst_ref=meta_all.at[me], send_sem=send.at[i], recv_sem=recv.at[i],
            device_id=(d // n_col, lax.rem(d, n_col)), device_id_type=MESH)

    def begin(i, carry):
        copy_to(i).start()
        return carry

    def finish(i, carry):
        copy_to(i).wait()
        return carry

    lax.fori_loop(1, devices, begin, 0)
    lax.fori_loop(1, devices, finish, 0)
    pair.wait()


def greet(partners):
    barrier = pltpu.get_barrier_semaphore()
    for partner in partners:
        pl.semaphore_signal(barrier, inc=1, device_id=partner, device_id_type=MESH)
    pl.semaphore_wait(barrier, len(partners))


def send_to(source, dest, sems, step, partner):
    return pltpu.make_async_remote_copy(
        src_ref=source, dst_ref=dest, send_sem=sems[0].at[step], recv_sem=sems[1].at[step],
        device_id=partner, device_id_type=MESH)


def place_of(nz):
    r, c = lax.axis_index("row"), lax.axis_index("col")
    z, k = c // 2, lax.rem(c, 2)
    return r, c, z, k, [(r, 2 * lax.rem(z + step, nz) + k) for step in range(1, nz)]


def first_kernel(nz, count, source, got, send, recv):
    r, c, z, k, others = place_of(nz)
    greet(others)
    copies = [send_to(source.at[to[1] // 2, pl.ds(0, count)], got.at[z], (send, recv), step, to)
              for step, to in enumerate(others)]
    for copy in copies:
        copy.start()
    for copy in copies:
        copy.wait()


def second_kernel(n_row, nz, source, wanted, got, plane_got, send, recv, psend, precv):
    r, c, z, k, others = place_of(nz)
    lines = [(lax.rem(r + step, n_row), c) for step in range(1, n_row)]
    greet(others + lines)
    count = got.shape[1]
    copies = [send_to(wanted.at[to[0]], plane_got.at[r], (psend, precv), step, to) for step, to in enumerate(lines)]
    copies += [send_to(source.at[to[1] // 2, pl.ds(0, count)], got.at[z], (send, recv), step, to)
               for step, to in enumerate(others)]
    for copy in copies:
        copy.start()
    for copy in copies:
        copy.wait()


def left_kernel(nz, piece, got, send, recv, psend, precv):
    r, c, z, k, others = place_of(nz)
    mate = (r, 2 * z + 1 - k)
    greet(others + [mate])
    copies = [send_to(piece, got.at[c], (send, recv), step, to) for step, to in enumerate(others)]
    for copy in copies:
        copy.start()
    pairs = [send_to(piece, got.at[c], (psend, precv), 0, mate)]
    pairs[0].start()
    for step in range(1, nz):
        copies[step - 1].wait_recv()
        origin = 2 * lax.rem(z - step + nz, nz) + k
        pairs.append(send_to(got.at[origin], got.at[origin], (psend, precv), step, mate))
        pairs[-1].start()
    for copy in copies:
        copy.wait_send()
    for pair in pairs:
        pair.wait()


def last_kernel(n_row, nz, wanted, filtered, plane_got, every, send, recv, up_send, up_recv, down_send, down_recv,
                psend, precv):
    r, c, z, k, others = place_of(nz)
    mate = (r, 2 * z + 1 - k)
    lines = [(lax.rem(r + step, n_row), c) for step in range(1, n_row)]
    above, below = (r, 2 * lax.rem(z + 1, nz) + k), (r, 2 * lax.rem(z + nz - 1, nz) + k)
    greet(lines + [above, below, mate])
    plane = [send_to(wanted.at[to[0]], plane_got.at[r], (send, recv), step, to) for step, to in enumerate(lines)]

    def up(step, own):
        block = every.at[2 * lax.rem(z - step + nz, nz) + k]
        return send_to(filtered if own else block, block, (up_send, up_recv), step, above)

    def down(step, own):
        block = every.at[2 * lax.rem(z + step, nz) + k]
        return send_to(filtered if own else block, block, (down_send, down_recv), step, below)

    def across(step, own):
        block = every.at[2 * lax.rem(z + step, nz) + k]
        return send_to(filtered if own else block, block, (psend, precv), step, mate)

    @pl.when(z < nz - 1)
    def _():
        up(0, True).start()

    @pl.when(z > 0)
    def _():
        down(0, True).start()

    across(0, True).start()
    for copy in plane:
        copy.start()
    for step in range(1, nz):
        @pl.when(z - step >= 0)
        def _():
            up(step - 1, False).wait_recv()
            across(nz - step, False).start()

        @pl.when((z - step >= 0) & (z < nz - 1))
        def _():
            up(step, False).start()

        @pl.when(z + step <= nz - 1)
        def _():
            down(step - 1, False).wait_recv()
            across(step, False).start()

        @pl.when((z + step <= nz - 1) & (z > 0))
        def _():
            down(step, False).start()
    for step in range(nz):
        @pl.when((z - step >= 0) & (z < nz - 1))
        def _():
            up(step, False).wait_send()

        @pl.when((z + step <= nz - 1) & (z > 0))
        def _():
            down(step, False).wait_send()
    for step in range(nz):
        across(step, False).wait()
    for copy in plane:
        copy.wait()


def pick(sources, index, dest, sem):
    start = 0
    for source in sources:
        stop = start + source.shape[0]

        @pl.when((index >= start) & (index < stop))
        def _(source=source, start=start):
            pltpu.make_async_copy(source.at[index - start], dest, sem).start()

        start = stop


def gather_kernel(index, *refs):
    sources, (out, sem) = refs[:-2], refs[-2:]
    start = pl.program_id(0) * out.shape[0]

    def begin(i, carry):
        pick(sources, index[start + i], out.at[i], sem)
        return carry

    lax.fori_loop(0, out.shape[0], begin, 0)
    pltpu.make_async_copy(out, out, sem).wait()


def flat(array):
    return array.reshape((-1,) + array.shape[-2:])


def gather(index, *sources):
    block = sources[0].shape[-2:]
    count = index.shape[0]
    chunk = max(n for n in range(1, min(count, 512) + 1) if count % n == 0)
    return pl.pallas_call(
        gather_kernel,
        grid=(count // chunk,),
        out_shape=jax.ShapeDtypeStruct((count,) + block, sources[0].dtype),
        in_specs=[SMEM] + [ANY] * len(sources), out_specs=pl.BlockSpec((chunk,) + block, lambda i: (i, 0, 0)),
        scratch_shapes=[DMA],
        compiler_params=pltpu.CompilerParams(vmem_limit_bytes=BIG),
    )(index, *[flat(source) for source in sources])


def square_kernel(left_at, right_at, slot, keep, lefts, own_left, rights, own_rights, out, a, b, acc, sems):
    count = out.shape[0]

    def begin(i, carry):
        pick((lefts, own_left), left_at[i], a.at[i], sems.at[0])
        pick((rights, own_rights), right_at[i], b.at[i], sems.at[1])
        return carry

    lax.fori_loop(0, count, begin, 0)
    acc[...] = jnp.zeros_like(acc)
    pltpu.make_async_copy(a, a, sems.at[0]).wait()
    pltpu.make_async_copy(b, b, sems.at[1]).wait()

    def multiply(q, carry):
        ids = [q * 4 + i for i in range(4)]
        terms = [jnp.dot(a[i], b[i], preferred_element_type=jnp.float32) for i in ids]
        for i, term in zip(ids, terms):
            acc[slot[i]] += term
        return carry

    lax.fori_loop(0, count // 4, multiply, 0)

    def write(i, carry):
        out[i] = (acc[i] * keep[i].astype(jnp.float32)).astype(out.dtype)
        return carry

    lax.fori_loop(0, count, write, 0)


def cubed_kernel(left_at, right_at, target, own_target, every, own, got1, send1, got2, send2, out, a, b, f, acc, sems):
    count = a.shape[0]
    windows = acc.shape[0]
    block = a.shape[-1]
    per_window = count // windows
    own_per_window = f.shape[0] // windows
    mine = pltpu.make_async_copy(own, f, sems.at[2])
    mine.start()

    def begin(i, carry):
        pick((every, own), left_at[i], a.at[i], sems.at[0])
        pick((got1, send1, got2, send2), right_at[i], b.at[i], sems.at[1])
        return carry

    lax.fori_loop(0, count, begin, 0)
    acc[...] = jnp.zeros_like(acc)
    mine.wait()
    for w in range(windows):
        def add(i, carry):
            e = w * own_per_window + i
            acc[w, own_target[e]] -= 1.5 * f[e].astype(jnp.float32)
            return carry

        lax.fori_loop(0, own_per_window, add, 0)
    pltpu.make_async_copy(a, a, sems.at[0]).wait()
    pltpu.make_async_copy(b, b, sems.at[1]).wait()
    for w in range(windows):
        def multiply(q, carry):
            ids = [w * per_window + q * 4 + i for i in range(4)]
            terms = [jnp.dot(a[i], b[i], preferred_element_type=jnp.float32) for i in ids]
            for i, term in zip(ids, terms):
                acc[w, target[i]] += term
            return carry

        lax.fori_loop(0, per_window // 4, multiply, 0)
    for w in range(windows):
        for j in range(acc.shape[1]):
            out[w * block:(w + 1) * block, j * block:(j + 1) * block] = (-2.0 * acc[w, j]).astype(out.dtype)


def running(mask):
    n = mask.shape[-1]
    before = (jnp.arange(n)[:, None] < jnp.arange(n)[None, :]).astype(jnp.bfloat16)
    lines = mask.reshape(-1, n).astype(jnp.bfloat16)
    return jnp.dot(lines, before, preferred_element_type=jnp.float32).astype(jnp.int32).reshape(mask.shape)


def general(owned_blocks, owned_rows, owned_cols, keep):
    n_row, n_col = lax.axis_size("row"), lax.axis_size("col")
    devices = n_row * n_col
    nz = n_col // 2
    r, c = lax.axis_index("row"), lax.axis_index("col")
    z, k = c // 2, lax.rem(c, 2)
    block = owned_blocks.shape[-1]
    dtype = owned_blocks.dtype
    slots = owned_rows.shape[0]
    per_band = slots // n_row
    windows, gcols = keep.shape
    nb = gcols * n_col
    size = slots * (1 + n_col)
    tall = -(-size // 1024) * 8
    one = (block, block)
    chips = devices // 2
    pool = 2 * slots
    i32 = jnp.int32

    packed = jnp.concatenate([owned_rows[:, None], owned_cols], axis=1).reshape(-1)
    meta = jnp.pad(packed, (0, tall * 128 - size)).reshape(tall, 128)
    meta_all, sibling = pl.pallas_call(
        functools.partial(spread_kernel, n_row, n_col),
        out_shape=(jax.ShapeDtypeStruct((devices, tall, 128), i32),
                   jax.ShapeDtypeStruct((slots, nz) + one, dtype)),
        in_specs=[ANY, ANY], out_specs=(ANY, ANY),
        scratch_shapes=[DMA((devices,)), DMA((devices,)), DMA, DMA],
        compiler_params=remote_params(0),
    )(meta, owned_blocks.reshape((slots, nz, 2) + one))
    me = r * n_col + c
    is_me = jnp.arange(devices)[:, None] == me
    labels = jnp.where(is_me, packed[None, :], meta_all.reshape(devices, -1)[:, :size])
    labels = labels.reshape(devices * slots, 1 + n_col)
    rows, cols = labels[:, 0], labels[:, 1:]
    slot_ids = jnp.arange(devices * slots, dtype=i32)
    every_row = jnp.arange(nb, dtype=i32)
    filled = rows < gcols * 2
    row_id = jnp.where(filled, gcols * (slot_ids // per_band % n_row + n_row * (rows // gcols)) + rows % gcols, nb)
    holder = jnp.sum(jnp.where(row_id[None, :] == every_row[:, None], slot_ids[None, :], 0), axis=1)
    row_cols = cols[holder]
    chip = holder // pool
    line, plane = chip // nz, chip % nz

    base = gcols * jnp.arange(n_col, dtype=i32)
    window = gcols * jnp.arange(n_row, dtype=i32)[:, None] + jnp.arange(windows, dtype=i32)[None, :]
    inner = base + row_cols[window]
    targets = base + row_cols[inner]
    is_window = jnp.any(window[:, :, None] == every_row, axis=1)
    is_inner = jnp.any(inner.reshape(n_row, -1, 1) == every_row, axis=1) & ~is_window
    is_target = jnp.any(targets.reshape(n_row, -1, 1) == every_row, axis=1) & ~is_inner & ~is_window
    urgent = jnp.any(is_window | is_inner, axis=0)
    wanted_row = urgent.astype(i32) + jnp.any(is_window | is_inner | is_target, axis=0).astype(i32)
    wanted = jnp.sum(jnp.where(row_id[:, None] == every_row[None, :], wanted_row[None, :], 0), axis=1).reshape(chips, pool)
    urgent_count = (wanted == 2).sum(axis=1)
    place = jnp.where(wanted == 2, running(wanted == 2), urgent_count[:, None] + running(wanted == 1))
    place = jnp.where(wanted > 0, place, pool)
    spot = place.reshape(-1)[holder]
    on_line = line[None, :] == jnp.arange(n_row, dtype=i32)[:, None]

    def ranks(need):
        both = need[:, None, :] & on_line[None, :, :]
        rank = jnp.sum(jnp.where(both, running(both), 0), axis=1)
        return rank, both.sum(axis=2).max()

    rank_window, _ = ranks(is_window)
    rank_inner, most_inner = ranks(is_inner)

    def shares(early, limit):
        now = is_target & (spot < early)[None, :]
        rank_now, _ = ranks(now)
        now = now & (rank_now < limit)
        later = is_target & ~now
        rank_later, most_later = ranks(later)
        return now, rank_now, later, rank_later, most_later

    inner_mine = inner[r].reshape(-1)
    targets_mine = targets[r].reshape(-1)
    cols_mine = lax.dynamic_index_in_dim(row_cols, c, 1, keepdims=False)
    square_target = cols_mine[inner_mine].reshape(windows, n_col)
    same = square_target[:, :, None] == square_target[:, None, :]
    first = jnp.argmax(same, axis=2).astype(i32)
    square_slot = (first + n_col * jnp.arange(windows, dtype=i32)[:, None]).reshape(-1)
    kept = jnp.take_along_axis(keep, square_target, axis=1).reshape(-1)
    cubed_target = cols_mine[targets_mine]
    entries = windows * n_col

    step = (z - plane + nz) % nz
    zs = jnp.arange(nz, dtype=i32)[:, None]
    place_mine = lax.dynamic_index_in_dim(place, r * nz + z, 0, keepdims=False)

    def pooled(start, count):
        position = start + jnp.arange(count, dtype=i32)
        pick_slot = jnp.sum(
            jnp.where(place_mine[None, :] == position[:, None], jnp.arange(pool, dtype=i32)[None, :], 0), axis=1)
        at = pick_slot[None, :] % slots
        index = jnp.where(
            pick_slot[None, :] // slots == k, at * n_col + 2 * zs + k, slots * n_col + at * nz + zs)
        return gather(index.reshape(-1), owned_blocks, sibling).reshape((nz, count) + one)

    def demand(need, rank, count, source_at):
        sending = need & (line == r)[None, :]
        chosen = sending[:, None, :] & (rank[:, None, :] == jnp.arange(count, dtype=i32)[None, :, None])
        return jnp.sum(jnp.where(chosen, source_at[None, None, :], 0), axis=2)

    def opening(early, most, limit, share, parts):
        now, rank_now = share[:2]
        cap1 = windows + most + limit
        now_all = is_window | is_inner | now
        now_rank = jnp.where(is_window, rank_window, jnp.where(is_inner, windows + rank_inner, windows + most + rank_now))
        send1 = gather(demand(now_all, now_rank, cap1, step * early + spot).reshape(-1), *parts)
        found1 = line * cap1 + now_rank[r] + jnp.where(line == r, n_row * cap1, 0)
        return now_all, found1, send1.reshape((n_row, cap1) + one)

    def run(early, late, rest, share, parts, opened, outgoing, number):
        later, rank_later = share[2:4]
        now_all, found1, send1 = opened
        cap1 = send1.shape[1]
        late_at = jnp.where(plane == z, nz * late + plane * outgoing.shape[1], plane * late)
        held_at = jnp.where(spot < early, step * early + spot, nz * early + late_at + spot - early)
        got_late, got1 = pl.pallas_call(
            functools.partial(second_kernel, n_row, nz),
            out_shape=(jax.ShapeDtypeStruct((nz, late) + one, dtype),
                       jax.ShapeDtypeStruct((n_row, cap1) + one, dtype)),
            in_specs=[ANY, ANY], out_specs=(ANY, ANY),
            scratch_shapes=[DMA((nz,)), DMA((nz,)), DMA((n_row,)), DMA((n_row,))],
            compiler_params=remote_params(number + 1),
        )(outgoing, send1)
        window_mine = gcols * r + jnp.arange(windows, dtype=i32)
        left_mine = gather(found1[window_mine], got1, send1)
        lefts = pl.pallas_call(
            functools.partial(left_kernel, nz),
            out_shape=jax.ShapeDtypeStruct((n_col, windows) + one, dtype),
            in_specs=[ANY], out_specs=ANY,
            scratch_shapes=[DMA((nz,))] * 4,
            compiler_params=remote_params(number + 2),
        )(left_mine)
        ws = jnp.arange(windows, dtype=i32)[:, None]
        gs = jnp.arange(n_col, dtype=i32)[None, :]
        left_at = jnp.where(gs == c, n_col * windows + ws, gs * windows + ws).reshape(-1)
        filtered = pl.pallas_call(
            square_kernel,
            out_shape=jax.ShapeDtypeStruct((entries,) + one, dtype),
            in_specs=[SMEM] * 4 + [ANY] * 4, out_specs=VMEM,
            scratch_shapes=[pltpu.VMEM((entries,) + one, dtype), pltpu.VMEM((entries,) + one, dtype),
                            pltpu.VMEM((entries,) + one, jnp.float32), DMA((2,))],
            compiler_params=pltpu.CompilerParams(vmem_limit_bytes=BIG),
        )(left_at, found1[inner_mine], square_slot, kept, flat(lefts), left_mine, flat(got1), flat(send1))
        later_at = demand(later, rank_later, rest, held_at)
        send2 = gather(later_at.reshape(-1), *parts, got_late, outgoing).reshape((n_row, rest) + one)
        got2, every = pl.pallas_call(
            functools.partial(last_kernel, n_row, nz),
            out_shape=(jax.ShapeDtypeStruct((n_row, rest) + one, dtype),
                       jax.ShapeDtypeStruct((n_col, entries) + one, dtype)),
            in_specs=[ANY, ANY], out_specs=(ANY, ANY),
            scratch_shapes=[DMA((n_row,)), DMA((n_row,))] + [DMA((nz,))] * 6,
            compiler_params=remote_params(number + 3),
        )(send2, filtered)
        found2 = jnp.where(
            now_all[r], found1,
            2 * n_row * cap1 + line * rest + rank_later[r] + jnp.where(line == r, n_row * rest, 0))
        place3 = ws[:, :, None] * n_col + gs[:, :, None]
        groups = jnp.arange(n_col, dtype=i32)[None, None, :]
        left_at = jnp.where(groups == c, n_col * entries + place3, groups * entries + place3).reshape(-1)
        count = windows * n_col * n_col
        return pl.pallas_call(
            cubed_kernel,
            out_shape=jax.ShapeDtypeStruct((windows * block, gcols * block), dtype),
            in_specs=[SMEM] * 4 + [ANY] * 6, out_specs=VMEM,
            scratch_shapes=[pltpu.VMEM((count,) + one, dtype), pltpu.VMEM((count,) + one, dtype),
                            pltpu.VMEM((entries,) + one, dtype),
                            pltpu.VMEM((windows, gcols) + one, jnp.float32), DMA((3,))],
            compiler_params=pltpu.CompilerParams(vmem_limit_bytes=BIG),
        )(left_at, found2[targets_mine], cubed_target, square_target.reshape(-1), flat(every), filtered,
          flat(got1), flat(send1), flat(got2), flat(send2))

    most_demand = windows * n_col * n_col
    early, most, limit = 7 * pool // 32, 10 * entries // 16, most_demand // 8
    small = (early, 22 * most_demand // 128)
    middle = (26 * pool // 64, most_demand // 4)
    share = shares(early, limit)
    most_pool, most_urgent = (wanted > 0).sum(axis=1).max(), urgent_count.max()
    first_out = pooled(0, early)
    parts = [lax.dynamic_index_in_dim(first_out, z, 0, keepdims=False)]
    for by in range(1, nz):
        moved = lax.dynamic_index_in_dim(first_out, (z + by) % nz, 0, keepdims=False)
        parts.append(lax.ppermute(moved, "col", [(i, (i + 2 * by) % n_col) for i in range(n_col)]))
    late_out = pooled(early, middle[0])
    opened = opening(early, most, limit, share, parts)

    def usual(caps, number):
        return run(early, caps[0], caps[1], share, parts, opened, late_out, number)

    def widest(number):
        every_share = shares(pool, limit)
        outgoing = pooled(0, pool)
        got = pl.pallas_call(
            functools.partial(first_kernel, nz, pool),
            out_shape=jax.ShapeDtypeStruct((nz, pool) + one, dtype),
            in_specs=[ANY], out_specs=ANY,
            scratch_shapes=[DMA((nz,)), DMA((nz,))],
            compiler_params=remote_params(number),
        )(outgoing)
        held = [lax.dynamic_index_in_dim(outgoing, z, 0, keepdims=False)]
        held += [lax.dynamic_index_in_dim(got, (z - by + nz) % nz, 0, keepdims=False) for by in range(1, nz)]
        return run(pool, 1, min(most_demand, nb, n_col * slots), every_share, held,
                   opening(pool, entries, limit, every_share, held), outgoing, number)

    def fits(caps):
        return ((most_pool <= early + caps[0]) & (most_urgent <= early)
                & (most_inner <= most) & (share[-1] <= caps[1]))

    choice = jnp.where(fits(small), 0, jnp.where(fits(middle), 1, 2))
    return lax.switch(choice, [lambda: usual(small, 1), lambda: usual(middle, 5), lambda: widest(9)])


F32, BF16, I32 = jnp.float32, jnp.bfloat16, jnp.int32
LANES = 128
SHIFTED = 5
META = 16
ROWS = 40
STAGE = (0, 32, 64, 128)


def log2(n):
    return n.bit_length() - 1


def iota(shape, dim):
    return lax.broadcasted_iota(I32, shape, dim)


def ones(mask):
    return jnp.where(mask, 1.0, 0.0).astype(F32)


def times(a, b):
    return lax.dot_general(a.astype(BF16), b.astype(BF16), (((1,), (0,)), ((), ())), preferred_element_type=F32)


def against(a, b):
    return lax.dot_general(a.astype(BF16), b.astype(BF16), (((1,), (1,)), ((), ())), preferred_element_type=F32)


def most(column):
    return jnp.max(column, axis=0, keepdims=True)


def plan(spread, keep, r, c, sizes, tiers):
    n_row, n_col, slots, windows, gcols, nb = sizes
    nz = n_col // 2
    z, k = c // 2, lax.rem(c, 2)
    devices = n_row * n_col
    total = devices * slots
    per_band = slots // n_row
    out = {}
    lane = iota((1, total), 1)
    label = spread[n_col:n_col + 1, :].astype(I32)
    band = (lane >> log2(per_band)) & (n_row - 1)
    row_id = gcols * (band + n_row * (label >> log2(gcols))) + (label & (gcols - 1))
    row_id = jnp.where(label < 2 * gcols, row_id, nb)
    holds = ones(iota((nb, total), 0) == row_id)
    sub = iota((META, total), 0)
    device = ((lane >> log2(slots)) & (n_row - 1)) * n_col + (lane >> log2(slots * n_row))
    fields = jnp.where(sub == n_col, device >> log2(n_col), 0)
    fields = jnp.where(sub == n_col + 1, (device & (n_col - 1)) >> 1, fields)
    fields = jnp.where(sub == n_col + 2, device & 1, fields)
    fields = jnp.where(sub == n_col + 3, lane & (slots - 1), fields)
    info = against(jnp.where(sub < n_col, spread, fields.astype(F32)), holds)
    line, plane, core, slot = [info[n_col + i:n_col + i + 1, :] for i in range(4)]
    column = jnp.zeros((1, nb), F32)
    for g in range(n_col):
        column = jnp.where(c == g, info[g:g + 1, :], column)
    within = iota((gcols, nb), 0).astype(F32)
    graph = jnp.concatenate([ones(info[g:g + 1, :] == within) for g in range(n_col)], axis=0).astype(BF16)
    upper = ones(iota((nb, nb), 0) < iota((nb, nb), 1)).astype(BF16)

    sub, row = iota((META, nb), 0), iota((META, nb), 1)
    wsel = ones((sub < n_row * windows) & (row == gcols * (sub >> log2(windows)) + (sub & (windows - 1))))
    once = against(wsel, graph)
    twice = against(once, graph)
    each = iota((1, nb), 1)
    soon, late = [], []
    for q in range(n_row):
        inner = sum(once[windows * q + i:windows * q + i + 1, :] for i in range(windows))
        target = sum(twice[windows * q + i:windows * q + i + 1, :] for i in range(windows))
        is_window = ((each >> log2(gcols)) == q) & ((each & (gcols - 1)) < windows)
        s = jnp.where(is_window, 1.0, ones(inner > 0.5))
        soon.append(s)
        late.append(ones(target > 0.5) * (1.0 - s))
    urgent = ones(sum(soon) > 0.5)
    need = ones(sum(soon) + sum(late) > 0.5)

    chip = (line * nz + plane).astype(I32)
    on_chip = ones(sub == chip)
    soon_mask, late_mask = on_chip * urgent, on_chip * (need - urgent)
    soon_count = jnp.sum(soon_mask, axis=1, keepdims=True)
    late_count = jnp.sum(late_mask, axis=1, keepdims=True)
    most_soon = most(soon_count)
    first = jnp.full((1, 1), float(tiers[-1]["n"][0]), F32)
    for tier in reversed(tiers):
        first = jnp.where(most_soon <= float(tier["n"][0]), float(tier["n"][0]), first)

    chips = (META, META)
    left, right = iota(chips, 0), iota(chips, 1)
    load = jnp.broadcast_to(soon_count + late_count, (META, LANES))
    level = times(ones((left & (nz - 1)) == (right & (nz - 1))), load)
    level = most(jnp.floor((level + (n_row - 1.0)) * (1.0 / n_row)))
    taken = jnp.zeros_like(load)
    moves = []
    for d in range(1, n_row):
        spare = jnp.maximum(jnp.minimum(level - load, level - first - taken), 0.0)
        reach = ones(right == ((((left >> log2(nz)) + d) & (n_row - 1)) << log2(nz)) + (left & (nz - 1)))
        back = ones(right == ((((left >> log2(nz)) + n_row - d) & (n_row - 1)) << log2(nz)) + (left & (nz - 1)))
        move = jnp.minimum(jnp.minimum(jnp.maximum(load - level, 0.0), float(SHIFTED)), times(reach, spare))
        arrived = times(back, move)
        load, taken = load - move + arrived, taken + arrived
        moves.append(move[:, 0:1])
    taken = taken[:, 0:1]
    stay = late_count - sum(moves)
    kept = soon_count + stay
    most_pool = most(jnp.where(taken > 0.5, jnp.maximum(kept, first) + taken, kept))
    late_rank = jnp.sum(on_chip * times(late_mask, upper), axis=0, keepdims=True)
    below = jnp.sum(on_chip * stay, axis=0, keepdims=True)
    is_late = need - urgent
    moved, entry, carrier = jnp.zeros((1, nb), F32), jnp.zeros((1, nb), F32), line
    for d in range(1, n_row):
        above = below + jnp.sum(on_chip * moves[d - 1], axis=0, keepdims=True)
        hit = is_late * ones((late_rank >= below) & (late_rank < above))
        moved = moved + hit
        entry = entry + hit * ((d - 1) * SHIFTED + late_rank - below)
        carrier = carrier + hit * d
        below = above
    carrier = jnp.where(carrier >= n_row, carrier - n_row, carrier)
    home = chip
    chip = (carrier * nz + plane).astype(I32)
    on_chip_now = ones(sub == chip)
    rank = jnp.where(urgent > 0.5, times(soon_mask, upper), soon_count + times(late_mask, upper))
    came = jnp.maximum(kept, first) + times(on_chip_now * moved, upper)
    spot = jnp.where(moved > 0.5, jnp.sum(on_chip_now * came, axis=0, keepdims=True),
                     jnp.sum(on_chip * rank, axis=0, keepdims=True))
    spot = jnp.where(need > 0.5, spot, 999.0)
    line = carrier
    m1 = tiers[0]["m"][1]

    sender, getter = sub >> log2(n_row), sub & (n_row - 1)
    soon_pair, late_pair = jnp.zeros((META, nb), F32), jnp.zeros((META, nb), F32)
    for q in range(n_row):
        soon_pair = jnp.where(getter == q, soon[q], soon_pair)
        late_pair = jnp.where(getter == q, late[q], late_pair)
    from_line = ones((sender == line.astype(I32)) & (sender != getter))
    soon_pair, late_pair = soon_pair * from_line, late_pair * from_line
    soon_sum = jnp.sum(soon_pair, axis=1, keepdims=True)
    at0 = times(soon_pair, upper)
    can = late_pair * ones(spot < first)
    at1 = times(can, upper)
    in1 = can * ones(at1 < float(m1))
    rest = late_pair * (1.0 - in1)
    at2 = times(rest, upper)
    most_line, most_rest = most(soon_sum), most(jnp.sum(rest, axis=1, keepdims=True))
    key = jnp.where(rest > 0.5, STAGE[2] + at2, -1.0)
    key = jnp.where(in1 > 0.5, STAGE[1] + at1, key)
    key = jnp.where(soon_pair > 0.5, at0, key)

    choice = jnp.full((1, 1), len(tiers), I32)
    for t in reversed(range(len(tiers))):
        n, m = tiers[t]["n"], tiers[t]["m"]
        fits = ((first == float(n[0])) & (most_soon <= float(n[0])) & (most_pool <= float(sum(n)))
                & (most_line <= float(m[0])) & (most_rest <= float(m[2])))
        choice = jnp.where(fits, t, choice)
    out[33] = jnp.broadcast_to(choice, (1, LANES))

    wide = iota((LANES, nb), 0)
    col = iota((LANES, nb), 1)
    step = z.astype(F32) - plane
    step = jnp.where(step < 0, step + nz, step)
    mine = ones(chip == (r * nz + z))
    pack = ones(wide.astype(F32) == jnp.where(mine > 0.5, spot, 999.0))
    from_slot = slot + slots * ones(core != k.astype(F32))
    given = jnp.where((moved > 0.5) & (home == (r * nz + z)), entry, -1.0)
    slot_rows = jnp.where(sub == 0, from_slot, 0.0)
    out[34] = against(slot_rows, ones(wide.astype(F32) == given))[0:1, :].astype(I32)
    from_slot = jnp.where(moved > 0.5, 2.0 * slots + entry, from_slot)
    rows = jnp.where(sub == 0, from_slot, jnp.where(sub == 1, step, jnp.where(sub == 2, spot, 0.0)))
    rows = jnp.minimum(rows, 127.0)
    out[0] = against(rows, pack)[0:1, :].astype(I32)
    for d in range(1, n_row):
        pair = r * n_row + lax.rem(r + d, n_row)
        key_of = jnp.sum(jnp.where(sub == pair, key, 0.0), axis=0, keepdims=True)
        got = against(rows, ones(wide.astype(F32) == key_of))
        out[d] = (64.0 * got[1:2, :] + got[2:3, :]).astype(I32)

    key_in = jnp.sum(jnp.where((sender == line.astype(I32)) & (getter == r), key, 0.0), axis=0, keepdims=True)
    away = r.astype(F32) - line
    away = jnp.where(away < 0, away + n_row, away)
    where_a = jnp.where(away == 0, step, nz - 1 + away)
    where_b = jnp.clip(jnp.where(away == 0, spot, key_in), 0.0, 127.0)
    fields = jnp.where(sub == 0, where_a, jnp.where(sub == 1, where_b, jnp.where(sub == 2, column, 0.0)))

    def location(found):
        return (128.0 * found[0:1, :] + found[1:2, :]).astype(I32)

    start = gcols * r
    group = col >> log2(gcols)
    out[32] = location(against(fields, ones((wide < windows) & (col == start + wide))))
    entries, count = windows * n_col, windows * n_col * n_col
    inner = against(ones(col == start + (wide >> log2(n_col))), graph)
    inner = inner * ones((group == (wide & (n_col - 1))) & (wide < entries))
    found = against(fields, inner)
    out[15] = location(found)
    lane_at = found[2:3, :]
    sub_at = jnp.sum(inner * column, axis=1, keepdims=True)
    here, there = iota((LANES, LANES), 0), iota((LANES, LANES), 1)
    same = ones((sub_at == lane_at) & ((here >> log2(n_col)) == (there >> log2(n_col)))
                & (here < entries) & (there < entries))
    leads = ones(jnp.sum(same * ones(there < here), axis=1, keepdims=True) < 0.5) * ones(here[:, 0:1] < entries)
    keeps = jnp.zeros((LANES, gcols), F32)
    tag = iota((LANES, gcols), 0) >> log2(n_col)
    for i in range(windows):
        keeps = jnp.where(tag == i, keep[i:i + 1, :].astype(F32), keeps)
    kept = jnp.sum(keeps * ones(iota((LANES, gcols), 1).astype(F32) == sub_at), axis=1, keepdims=True)
    out[16] = (same * leads * kept)[0:entries, :].astype(I32)
    place = gcols * (here[:, 0:1] >> log2(n_col)).astype(F32) + sub_at
    at = ones(place == there.astype(F32)) * leads
    out[13] = jnp.sum(at * here.astype(F32), axis=0, keepdims=True).astype(I32)
    out[14] = jnp.sum(at, axis=0, keepdims=True).astype(I32)

    inner = against(ones(col == start + (wide >> log2(n_col * n_col))), graph)
    inner = inner * ones(group == ((wide >> log2(n_col)) & (n_col - 1)))
    target = against(inner, graph) * ones(group == (wide & (n_col - 1)))
    found = against(fields, target)
    sub_at = gcols * (here[:, 0:1] >> log2(n_col * n_col)).astype(F32) + jnp.sum(target * column, axis=1, keepdims=True)
    lane_at = gcols * (there[0:1, :] >> log2(n_col * n_col)).astype(F32) + found[2:3, :]
    ahead = ones(sub_at == lane_at) * ones(there < here)
    order = jnp.sum(ones(lane_at < sub_at) + ahead, axis=1, keepdims=True)
    put = ones(order == there.astype(F32))
    narrow = iota((META, LANES), 0)
    got = times(jnp.where(narrow == 3, iota((META, LANES), 1).astype(F32), found), put)
    out[8] = location(got)
    out[9] = got[3:4, :].astype(I32)
    follows = ones(jnp.sum(ahead, axis=1, keepdims=True) > 0.5)
    out[10] = jnp.sum(put * follows, axis=0, keepdims=True).astype(I32)
    out[11] = (jnp.sum(ones(sub_at <= there.astype(F32)), axis=0, keepdims=True) - 1.0).astype(I32)
    out[12] = jnp.minimum(jnp.sum(ones(sub_at == there.astype(F32)), axis=0, keepdims=True), 1.0).astype(I32)
    return out


def plan_kernel(sizes, tiers, labels, cols, keep, owned, index, sibling, tile, line_tiles, group, tiles, send, recv,
                col_send, col_recv, pair_send, pair_recv):
    n_row, n_col, slots = sizes[:3]
    r, c = lax.axis_index("row"), lax.axis_index("col")
    z, k = c // 2, lax.rem(c, 2)
    mate = (r, 2 * z + 1 - k)
    lines = [(lax.rem(r + step, n_row), c) for step in range(1, n_row)]
    others = [(r, lax.rem(c + step, n_col)) for step in range(1, n_col)]
    barrier = pltpu.get_barrier_semaphore()
    for to in lines + others:
        pl.semaphore_signal(barrier, inc=1, device_id=to, device_id_type=MESH)
    rows = jnp.concatenate([cols[...].astype(F32), jnp.zeros((META - n_col, slots), F32)], axis=0)
    rows = jnp.where(iota((META, slots), 0) == n_col, labels[...].astype(F32), rows)
    tile[...] = times(rows, ones(iota((slots, LANES), 0) + slots * r == iota((slots, LANES), 1))).astype(BF16)
    pl.semaphore_wait(barrier, n_row + n_col - 2)
    pair = pltpu.make_async_remote_copy(
        src_ref=owned.at[:, :, 1 - k], dst_ref=sibling, send_sem=pair_send, recv_sem=pair_recv, device_id=mate,
        device_id_type=MESH)
    pair.start()
    copies = [send_to(tile, line_tiles.at[r], (send, recv), step, to) for step, to in enumerate(lines)]
    for copy in copies:
        copy.start()
    line_tiles[r] = tile[...]
    for copy in copies:
        copy.wait()
    group[...] = sum(line_tiles[q].astype(F32) for q in range(n_row)).astype(BF16)
    copies = [send_to(group, tiles.at[c], (col_send, col_recv), step, to) for step, to in enumerate(others)]
    for copy in copies:
        copy.start()
    tiles[c] = group[...]
    for copy in copies:
        copy.wait()
    spread = jnp.concatenate([tiles[q].astype(F32) for q in range(n_col)], axis=1)
    index[...] = jnp.zeros_like(index)
    for row, value in plan(spread, keep[...], r, c, sizes, tiers).items():
        index[row:row + value.shape[0], :] = value
    pair.wait()


def main_kernel(sizes, tier, index, owned, sibling, out, pool, bsend, brecv, zsend0, zsend1, zall0, zall1,
                xsend0, xsend1, xsend2, xrecv0, xrecv1, xrecv2, lefts, parts, every0, every1, rights, sums, sems, zs, zr, xs, xr,
                ls, lr, us, ur, ds, dr, ps, pr, bs, br):
    n_row, n_col, slots, windows, gcols, nb = sizes
    nz = n_col // 2
    entries, count = windows * n_col, windows * n_col * n_col
    block = out.shape[0] // windows
    r, c = lax.axis_index("row"), lax.axis_index("col")
    z, k = c // 2, lax.rem(c, 2)
    zsend, zall = (zsend0, zsend1), (zall0, zall1)
    every = (every0, every1)
    xsend, xrecv = (xsend0, xsend1, xsend2), (xrecv0, xrecv1, xrecv2)
    n, m = tier["n"], tier["m"]
    bounds = [0, n[0], n[0] + n[1]]
    others = [(r, 2 * lax.rem(z + step, nz) + k) for step in range(1, nz)]
    lines = [(lax.rem(r + step, n_row), c) for step in range(1, n_row)]
    mate = (r, 2 * z + 1 - k)
    above, below = others[0], others[-1]
    loads = [pltpu.make_async_copy(owned.at[:, :, k], pool.at[pl.ds(0, slots)], sems.at[0]),
             pltpu.make_async_copy(sibling, pool.at[pl.ds(slots, slots)], sems.at[1])]
    for load in loads:
        load.start()
    greet(others + lines + [mate])
    for load in loads:
        load.wait()

    def bpack():
        for i in range((n_row - 1) * SHIFTED):
            slot = index[34, i]
            for other in range(nz):
                bsend[i * nz + other] = pool[slot, other]

    def bcopies():
        size = SHIFTED * nz
        return [pltpu.make_async_remote_copy(
            src_ref=bsend.at[pl.ds((d - 1) * size, size)], dst_ref=brecv.at[pl.ds((d - 1) * size, size)],
            send_sem=bs.at[d], recv_sem=br.at[d], device_id=lines[d - 1], device_id_type=MESH)
            for d in range(1, n_row)]

    def zpack(s):
        def body(p, carry):
            slot = index[0, bounds[s] + p]
            own = slot < 2 * slots
            for step in range(nz):
                to = lax.rem(z + step, nz)
                if s == 0:
                    value = pool[slot, to]
                else:
                    value = lax.select(own, pool[jnp.where(own, slot, 0), to],
                                       brecv[jnp.where(own, 0, slot - 2 * slots) * nz + to])
                if step == 0:
                    zall[s][p] = value
                else:
                    zsend[s][(step - 1) * n[s] + p] = value
            return carry

        lax.fori_loop(0, n[s], body, 0)

    def zcopies(s):
        return [pltpu.make_async_remote_copy(
            src_ref=zsend[s].at[pl.ds((step - 1) * n[s], n[s])], dst_ref=zall[s].at[pl.ds(step * n[s], n[s])],
            send_sem=zs.at[s * nz + step], recv_sem=zr.at[s * nz + step], device_id=others[step - 1],
            device_id_type=MESH) for step in range(1, nz)]

    def from_z(step, spot, upto, value):
        for s in upto:
            inside = (step >= 0) & (spot >= bounds[s]) & (spot < bounds[s + 1])
            got = zall[s][jnp.where(inside, step * n[s] + spot - bounds[s], 0)]
            value = got if value is None else lax.select(inside, got, value)
        return value

    def from_x(away, key, upto, value):
        for s in upto:
            inside = (away >= 0) & (key >= STAGE[s]) & (key < STAGE[s] + m[s])
            got = xrecv[s][jnp.where(inside, away * m[s] + key - STAGE[s], 0)]
            value = lax.select(inside, got, value)
        return value

    def fetch(code, zupto, xupto, value=None):
        a, b = code // 128, lax.rem(code, 128)
        value = from_z(jnp.where(a < nz, a, -1), b, zupto, value)
        return from_x(jnp.where(a < nz, -1, a - nz), b, xupto, value)

    def xpack(s):
        ready = [0, 1] if s == 2 else [0]

        for d in range(1, n_row):
            def body(q, carry):
                code = index[d, STAGE[s] + q]
                xsend[s][(d - 1) * m[s] + q] = from_z(code // 64, lax.rem(code, 64), ready, None)
                return carry

            lax.fori_loop(0, m[s], body, 0)

    def xcopies(s):
        return [pltpu.make_async_remote_copy(
            src_ref=xsend[s].at[pl.ds((d - 1) * m[s], m[s])], dst_ref=xrecv[s].at[pl.ds((d - 1) * m[s], m[s])],
            send_sem=xs.at[s * n_row + d], recv_sem=xr.at[s * n_row + d], device_id=lines[d - 1],
            device_id_type=MESH) for d in range(1, n_row)]

    def start(copies):
        for copy in copies:
            copy.start()

    def arrive(copies):
        for copy in copies:
            copy.wait_recv()

    def left_send(sem, source, to):
        slab = lefts.at[source]
        return pltpu.make_async_remote_copy(
            src_ref=slab, dst_ref=slab, send_sem=ls.at[sem], recv_sem=lr.at[sem], device_id=to, device_id_type=MESH)

    offsets = [0, nz * n[0], nz * (n[0] + n[1]), nz * (n[0] + n[1]) + (n_row - 1) * m[0]]

    def kept(at, source):
        return pltpu.make_async_copy(source, rights.at[pl.ds(offsets[at], source.shape[0])], sems.at[2 + at])

    def keep(at, source):
        kept(at, source).start()

    zpack(0)
    start(zcopies(0))
    bpack()
    start(bcopies())
    arrive(bcopies())
    zpack(1)
    arrive(zcopies(0))
    start(zcopies(1))
    keep(0, zall0)
    xpack(0)
    start(xcopies(0))
    xpack(1)
    arrive(xcopies(0))
    keep(2, xrecv0)
    for i in range(windows):
        lefts[c, i] = fetch(index[32, i], [0], [0])
    left_out = [left_send(step, c, to) for step, to in enumerate(others)]
    left_pair = [left_send(nz, c, mate)]
    start(left_out)
    start(left_pair)
    start(xcopies(1))
    for step in range(1, nz):
        left_out[step - 1].wait_recv()
        left_pair.append(left_send(nz + step, 2 * lax.rem(z - step + nz, nz) + k, mate))
        left_pair[-1].start()
    arrive(left_pair)

    def square(e, carry):
        right = fetch(index[15, e], [0], [0])
        left = lefts[lax.rem(e, n_col), e // n_col]
        parts[e] = jnp.dot(left, right, preferred_element_type=F32)
        return carry

    def merge(w):
        def body(g, carry):
            e = w * n_col + g
            total = parts[w * n_col] * index[16 + e, w * n_col].astype(F32)
            for i in range(1, n_col):
                total += parts[w * n_col + i] * index[16 + e, w * n_col + i].astype(F32)
            every[w][c, g] = total.astype(BF16)
            return carry

        lax.fori_loop(0, n_col, body, 0)

    def pass_on(sem, half, step, place, to):
        slab = every[half].at[place]
        return pltpu.make_async_remote_copy(
            src_ref=slab, dst_ref=slab, send_sem=sem[0].at[half * nz + step], recv_sem=sem[1].at[half * nz + step],
            device_id=to, device_id_type=MESH)

    def up(half, step):
        return pass_on((us, ur), half, step, 2 * lax.rem(z - step + nz, nz) + k, above)

    def down(half, step):
        return pass_on((ds, dr), half, step, 2 * lax.rem(z + step, nz) + k, below)

    def across(half, step):
        return pass_on((ps, pr), half, step, 2 * lax.rem(z + step, nz) + k, mate)

    def relay(half, step):
        @pl.when(z - step >= 0)
        def _():
            up(half, step - 1).wait_recv()

        @pl.when((z - step >= 0) & (z < nz - 1))
        def _():
            up(half, step).start()

        @pl.when(z - step >= 0)
        def _():
            across(half, nz - step).start()

        @pl.when(z + step <= nz - 1)
        def _():
            down(half, step - 1).wait_recv()

        @pl.when((z + step <= nz - 1) & (z > 0))
        def _():
            down(half, step).start()

        @pl.when(z + step <= nz - 1)
        def _():
            across(half, step).start()

    def first_pass(half):
        @pl.when(z < nz - 1)
        def _():
            up(half, 0).start()

        @pl.when(z > 0)
        def _():
            down(half, 0).start()

        across(half, 0).start()

    for w in range(windows):
        lax.fori_loop(w * n_col, (w + 1) * n_col, square, 0)
        merge(w)
        first_pass(w)
    arrive(zcopies(1))
    xpack(2)
    start(xcopies(2))
    keep(1, zall1)
    arrive(xcopies(1))
    keep(3, xrecv1)
    for step in range(1, nz):
        for w in range(windows):
            if (w, step) != (windows - 1, nz - 1):
                relay(w, step)

    def right_of(code):
        a, b = code // 128, lax.rem(code, 128)
        d = a - nz
        near = jnp.where(b < n[0], a * n[0] + b, offsets[1] + a * n[1] + b - n[0])
        far = jnp.where(b < STAGE[1], offsets[2] + d * m[0] + b, offsets[3] + d * m[1] + b - STAGE[1])
        last = (d >= 0) & (b >= STAGE[2])
        value = rights[jnp.where(last, 0, jnp.where(d < 0, near, far))]
        return lax.select(last, xrecv2[jnp.where(last, d * m[2] + b - STAGE[2], 0)], value)

    def finish(w):
        for step in range(nz):
            across(w, step).wait_recv()
        if w == 0:
            arrive(xcopies(2))
            for at, source in enumerate((zall0, zall1, xrecv0, xrecv1)):
                kept(at, source).wait()
        each = count // windows

        def multiply(q, acc):
            for i in range(8):
                t = w * each + q * 8 + i
                p = index[9, t]
                term = jnp.dot(every[w][lax.rem(p, n_col), lax.rem(p // n_col, n_col)], right_of(index[8, t]),
                               preferred_element_type=F32)
                acc = acc * index[10, t].astype(F32) + term
                sums[t] = acc
            return acc

        lax.fori_loop(0, each // 8, multiply, jnp.zeros((block, block), F32))

        def write(j, carry):
            at = w * gcols + j
            cube = sums[jnp.maximum(index[11, at], 0)] * (-2.0 * index[12, at].astype(F32))
            own = every[w][c, jnp.maximum(index[13, at] - w * n_col, 0)].astype(F32) * (3.0 * index[14, at].astype(F32))
            out[w * block:(w + 1) * block, pl.ds(pl.multiple_of(j * block, block), block)] = (own + cube).astype(BF16)
            return carry

        lax.fori_loop(0, gcols, write, 0)

    for w in range(windows):
        if w == windows - 1:
            relay(w, nz - 1)
        finish(w)
    for copies in (bcopies(), zcopies(0), zcopies(1), xcopies(0), xcopies(1), xcopies(2), left_out, left_pair):
        for copy in copies:
            copy.wait_send()
    for w in range(windows):
        for step in range(nz):
            @pl.when((z - step >= 0) & (z < nz - 1))
            def _(w=w, step=step):
                up(w, step).wait_send()

            @pl.when((z + step <= nz - 1) & (z > 0))
            def _(w=w, step=step):
                down(w, step).wait_send()

            across(w, step).wait_send()


TIERS = tuple(dict(n=(a, b), m=(c, 14, d)) for a, b, c, d in (
    (8, 9, 9, 18), (8, 11, 9, 20), (8, 19, 12, 28), (9, 8, 9, 18), (9, 10, 9, 20), (9, 18, 12, 28), (11, 8, 9, 18),
    (11, 10, 11, 20), (11, 16, 12, 28), (14, 12, 12, 24), (14, 22, 14, 30)))


def local(owned_blocks, owned_rows, owned_cols, keep):
    n_row, n_col = lax.axis_size("row"), lax.axis_size("col")
    nz = n_col // 2
    slots = owned_rows.shape[0]
    windows, gcols = keep.shape
    nb = gcols * n_col
    block = owned_blocks.shape[-1]
    one = (block, block)
    dtype = owned_blocks.dtype
    entries, count = windows * n_col, windows * n_col * n_col
    if (count > LANES or n_col > 8 or n_row > 4 or entries > 16 or nz > 4 or n_row * slots != LANES or 2 * slots > 64
            or windows * gcols > LANES or n_row < 2 or nz < 2 or windows != 2):
        return general(owned_blocks, owned_rows, owned_cols, keep)
    sizes = (n_row, n_col, slots, windows, gcols, nb)
    halves = owned_blocks.reshape((slots, nz, 2) + one)
    index, sibling = pl.pallas_call(
        functools.partial(plan_kernel, sizes, TIERS),
        out_shape=(jax.ShapeDtypeStruct((ROWS, LANES), I32), jax.ShapeDtypeStruct((slots, nz) + one, dtype)),
        in_specs=[VMEM, VMEM, VMEM, ANY], out_specs=(VMEM, ANY),
        scratch_shapes=[pltpu.VMEM((META, LANES), BF16), pltpu.VMEM((n_row, META, LANES), BF16),
                        pltpu.VMEM((META, LANES), BF16), pltpu.VMEM((n_col, META, LANES), BF16),
                        DMA((n_row,)), DMA((n_row,)), DMA((n_col,)), DMA((n_col,)), DMA, DMA],
        compiler_params=pltpu.CompilerParams(collective_id=20, has_side_effects=True, vmem_limit_bytes=BIG),
    )(owned_rows[None, :], owned_cols.T, keep, halves)

    def quick(t):
        n, m = TIERS[t]["n"], TIERS[t]["m"]
        scratch = [pltpu.VMEM((2 * slots, nz) + one, dtype)]
        scratch += [pltpu.VMEM(((n_row - 1) * SHIFTED * nz,) + one, dtype)] * 2
        scratch += [pltpu.VMEM(((nz - 1) * q,) + one, dtype) for q in n]
        scratch += [pltpu.VMEM((nz * q,) + one, dtype) for q in n]
        scratch += [pltpu.VMEM(((n_row - 1) * q,) + one, dtype) for q in m] * 2
        scratch += [pltpu.VMEM((n_col, windows) + one, dtype), pltpu.VMEM((entries,) + one, F32),
                    pltpu.VMEM((n_col, n_col) + one, dtype), pltpu.VMEM((n_col, n_col) + one, dtype),
                    pltpu.VMEM((nz * sum(n) + (n_row - 1) * (m[0] + m[1]),) + one, dtype),
                    pltpu.VMEM((count,) + one, F32), DMA((6,))]
        scratch += [DMA((2 * nz,))] * 2 + [DMA((3 * n_row,))] * 2 + [DMA((2 * nz,))] * 2
        scratch += [DMA((windows * nz,))] * 6 + [DMA((n_row,))] * 2
        return pl.pallas_call(
            functools.partial(main_kernel, sizes, TIERS[t]),
            out_shape=jax.ShapeDtypeStruct((windows * block, gcols * block), dtype),
            in_specs=[SMEM, ANY, ANY], out_specs=VMEM, scratch_shapes=scratch,
            compiler_params=pltpu.CompilerParams(
                collective_id=21 + t, has_side_effects=True, vmem_limit_bytes=BIG),
        )(index, halves, sibling)

    branches = [functools.partial(quick, t) for t in range(len(TIERS))]
    branches.append(lambda: general(owned_blocks, owned_rows, owned_cols, keep))
    return lax.switch(index[33, 0], branches)


def solution(mesh):
    placed = (
        P(("row", "col"), None, None, None),
        P(("row", "col")),
        P(("row", "col"), None),
        P("row", "col"),
    )
    return jax.shard_map(
        local, mesh=mesh, in_specs=placed, out_specs=P("row", "col"), check_vma=False
    )
```
